128 devices in a mesh: dp: 4 (over y_lo, core), cent: 32 (over x, y_hi, z).
Axes of the slice: x: 4, y: 4 (y_hi: 2, y_lo: 2; y = y_hi * 2 + y_lo), z: 4, core: 2. Of those that a mesh axis runs over, the one named last changes fastest.
Arguments:
- queries: bfloat16 [2048, 768], P('dp')
- centroids: bfloat16 [16384, 768], P('cent'), as said below
- beta: float32 [2048], P('dp'), may hold values from 16 to 400
- teacher_ids: int32 [2048, 16], P('dp'), may hold values from 0 to 16383
Outputs:
- query_grad: float32 [2048, 768], P(('dp', 'cent'))
- centroid_grad: float32 [16384, 768], P('cent', 'dp')
The draws below stay inside these ranges and needn't reach their ends.
Inputs may be any that keep to these rules, and one draw needn't show every extreme that they name: `centroids`: each centroid row has length one before rounding to bfloat16.
All inputs are finite; a program needn't handle non-finite values.
Results may differ from the reference program's by a relative error of at most 0.0098.
Values may be sent and summed in bfloat16 or wider, within the bound.
A program may use at most 64 MiB of HBM per device.

```python
import math
import jax
import jax.numpy as jnp
from jax import lax

D = 768
TOPK = 16
QUERIES = 2048
CELLS = 16384


def unit_table(key):
    base = jax.random.normal(jax.random.fold_in(key, 7), (CELLS, D), jnp.float32)
    return base / jnp.sqrt(jnp.sum(base * base, axis=1, keepdims=True))


def draw_centroids(key, part):
    return unit_table(key).astype(jnp.bfloat16)


def draw_beta(key, part):
    inner = jax.random.fold_in(key, 31)
    rates = jnp.exp(jax.random.uniform(inner, (QUERIES,), jnp.float32, math.log(16.0), math.log(96.0)))
    return rates


def draw_queries(key, part):
    inner = jax.random.fold_in(key, 21)
    scales = jnp.exp(jax.random.uniform(jax.random.fold_in(inner, 1), (QUERIES, 1), jnp.float32, math.log(0.5), math.log(5.0)))
    values = jax.random.normal(jax.random.fold_in(inner, 2), (QUERIES, D), jnp.float32) * scales
    return values.astype(jnp.bfloat16)


def touch_ends(values, stream_key, smallest, largest):
    extent = values.shape
    index_at = [jax.random.randint(jax.random.fold_in(stream_key, axis), (), 0, extent[axis]) for axis in range(len(extent))]
    values = values.at[tuple(index_at)].set(smallest)
    longest = extent.index(max(extent))
    index_at[longest] = (index_at[longest] + 1) % extent[longest]
    return values.at[tuple(index_at)].set(largest)


def setup_inputs(seed: int = 0) -> dict:
    splits = jax.random.split(jax.random.key(seed), 5)
    return {
        "queries": draw_queries(jax.random.fold_in(splits[4], 71), 0),
        "centroids": draw_centroids(jax.random.fold_in(splits[4], 71), 0),
        "beta": draw_beta(jax.random.fold_in(splits[4], 71), 0),
        "teacher_ids": touch_ends(jax.random.randint(splits[3], (QUERIES, TOPK), 0, CELLS), jax.random.fold_in(splits[3], 1), 0, CELLS - 1).astype(jnp.int32),
    }


grad_scale = 1024.0
eps = 1e-06

def reference(queries, centroids, beta, teacher_ids):
    query_float = queries.astype(jnp.float32)
    qnorm = jnp.sqrt(lax.optimization_barrier(jnp.sum(query_float * query_float, axis=1)) + eps)
    qhat = (query_float / qnorm[:, None]).astype(jnp.bfloat16)
    block = math.gcd(QUERIES, 256)
    blocks = QUERIES // block

    def one_block(carry, inputs):
        qpart, bpart, ipart = inputs
        cosine = jnp.dot(qpart, centroids.T, preferred_element_type=jnp.float32)
        score = bpart[:, None] * cosine
        prob = jax.nn.softmax(score, axis=1)
        rownum = jnp.arange(block, dtype=jnp.int32)[:, None]
        shifted = prob.at[rownum, ipart].add(-1.0 / TOPK)
        dscore = (grad_scale * shifted).astype(jnp.bfloat16)
        qgrad = jnp.dot(dscore, centroids, preferred_element_type=jnp.float32)
        carry = carry + jnp.dot(dscore.T, qpart, preferred_element_type=jnp.float32)
        return (carry, qgrad)
    start_grad = jnp.zeros((CELLS, D), jnp.float32)
    cgrad, qgrads = lax.scan(one_block, start_grad, (qhat.reshape(blocks, block, D), beta.reshape(blocks, block), teacher_ids.reshape(blocks, block, TOPK)))
    qgrad_unit = qgrads.reshape(QUERIES, D)
    qhat_float = qhat.astype(jnp.float32)
    along = lax.optimization_barrier(jnp.sum(qgrad_unit * qhat_float, axis=1))
    query_grad = (qgrad_unit - along[:, None] * qhat_float) / qnorm[:, None]
    cent_float = centroids.astype(jnp.float32)
    rowdot = lax.optimization_barrier(jnp.sum(cent_float * cgrad, axis=1))
    centroid_grad = cgrad - rowdot[:, None] * cent_float
    return (query_grad, centroid_grad)
```

```python
import functools

import jax
import jax.numpy as jnp
from jax import lax
from jax.experimental import pallas as pl
from jax.experimental.pallas import tpu as pltpu
from jax.sharding import PartitionSpec as P

EPS = 1e-06
SCALE = 1024.0
MESH = pl.DeviceIdType.MESH
F32 = jnp.float32
BF16 = jnp.bfloat16
NT = (((1,), (1,)), ((), ()))
TN = (((0,), (0,)), ((), ()))


def dot(a, b, dims):
    return lax.dot_general(a, b, dims, preferred_element_type=F32)


def kernel(
    q_hbm, c_hbm, beta_hbm, ids_hbm,
    qg_ref, cg_ref,
    q_v, c_v, beta_v, ids_v,
    qh_v, qht_v, ct_v, cos_v, e_v, d_v,
    es_v, ts_v,
    lse_s, lse_r,
    gx_s, gx_r, gz_s, gz_r,
    bx_s, bx_r, bz_s, bz_r,
    core_s, core_r, y_s, y_r,
    row_s, row_r,
    in_sem, lse_sem, a_send, a_recv, b_sem, core_send, core_recv, y_sem, row_sem,
):
    rows, width = q_hbm.shape
    cells = c_hbm.shape[0]
    slots = ids_hbm.shape[0]
    half = width // 2
    part = width // 4
    dp = lax.axis_index("dp")
    cent = lax.axis_index("cent")
    x = cent // 8
    yhi = (cent // 4) % 2
    z = cent % 4
    core = dp % 2
    ylo = dp // 2

    loads = [
        pltpu.make_async_copy(src, dst, in_sem.at[i])
        for i, (src, dst) in enumerate(((q_hbm, q_v), (c_hbm, c_v), (beta_hbm, beta_v), (ids_hbm, ids_v)))
    ]
    for load in loads:
        load.start()

    barrier = pltpu.get_barrier_semaphore()

    @pl.loop(1, 32)
    def _(r):
        pl.semaphore_signal(barrier, inc=1, device_id=(dp, (cent + r) % 32), device_id_type=MESH)

    @pl.loop(1, 4)
    def _(r):
        pl.semaphore_signal(barrier, inc=1, device_id=((dp + r) % 4, cent), device_id_type=MESH)

    loads[0].wait()
    for i in range(4):
        block = pl.ds(i * (rows // 4), rows // 4)
        qf = q_v[block, :].astype(F32)
        inv = 1.0 / jnp.sqrt(jnp.sum(qf * qf, axis=1, keepdims=True) + EPS)
        qh_v[block, :] = (qf * inv).astype(BF16)

    loads[1].wait()
    loads[2].wait()
    loads[3].wait()
    tops = []
    for i in range(2):
        lanes = pl.ds(i * (rows // 2), rows // 2)
        cosine = dot(c_v[...], qh_v[lanes, :], NT)
        cos_v[:, lanes] = cosine
        score = cosine * beta_v[:, lanes]
        top = jnp.max(score, axis=0, keepdims=True)
        expo = jnp.exp(score - top)
        e_v[:, lanes] = expo
        lse_s[0, :, lanes] = top + jnp.log(jnp.sum(expo, axis=0, keepdims=True))
        tops.append(top)

    pl.semaphore_wait(barrier, 34)

    def lse_copy(r):
        return pltpu.make_async_remote_copy(
            src_ref=lse_s.at[0],
            dst_ref=lse_r.at[r - 1],
            send_sem=lse_sem.at[0],
            recv_sem=lse_sem.at[1],
            device_id=(dp, (cent + r) % 32),
            device_id_type=MESH,
        )

    @pl.loop(1, 32)
    def _(r):
        lse_copy(r).start()

    qht_v[...] = qh_v[...].T
    ct_v[...] = c_v[...].T
    first = cent * cells
    for i in range(2):
        lanes = pl.ds(i * (rows // 2), rows // 2)
        cell_pos = lax.broadcasted_iota(jnp.int32, (cells, rows // 2), 0) + first
        count = jnp.zeros((cells, rows // 2), F32)
        for slot in range(slots):
            count = count + jnp.where(ids_v[slot : slot + 1, lanes] == cell_pos, SCALE / slots, 0.0)
        d_v[:, lanes] = count
        e = e_v[:, lanes]
        high = e.astype(BF16)
        low = (e - high.astype(F32)).astype(BF16)
        es_v[lanes, :] = dot(high, c_v[...], TN) + dot(low, c_v[...], TN)
        ts_v[lanes, :] = dot(count.astype(BF16), c_v[...], TN)

    pltpu.make_async_copy(lse_r, lse_r, lse_sem.at[1]).wait()
    own = lse_s[0]
    others = lse_r[...]
    top_all = jnp.maximum(jnp.max(others, axis=0), own)
    lse = top_all + jnp.log(jnp.sum(jnp.exp(others - top_all[None]), axis=0) + jnp.exp(own - top_all))
    weight = jnp.exp(jnp.concatenate(tops, axis=1) - lse) * SCALE
    weight_col = jnp.broadcast_to(weight, (128, rows)).T

    for i in range(rows // 128):
        block = pl.ds(i * 128, 128)
        for j in range(3):
            cols = pl.ds(j * 128, 128)
            gx_s[i, :, cols] = (es_v[block, cols] * weight_col[i * 128 : (i + 1) * 128] - ts_v[block, cols]).astype(BF16)
        for j in range(3):
            cols = pl.ds(half + j * 128, 128)
            g = (es_v[block, cols] * weight_col[i * 128 : (i + 1) * 128] - ts_v[block, cols]).astype(BF16)
            for k in range(8):
                gz_s[k % 4, 2 * i + k // 4, :, pl.ds(j * 128, 128)] = g[k * 16 : (k + 1) * 16]

    def x_copy(r):
        to = (x + r) % 4
        return pltpu.make_async_remote_copy(
            src_ref=gx_s.at[to], dst_ref=gx_r.at[r - 1], send_sem=a_send.at[0, r - 1], recv_sem=a_recv.at[0, r - 1],
            device_id=(dp, (to * 2 + yhi) * 4 + z), device_id_type=MESH,
        )

    def z_copy(r):
        to = (z + r) % 4
        return pltpu.make_async_remote_copy(
            src_ref=gz_s.at[to], dst_ref=gz_r.at[r - 1], send_sem=a_send.at[1, r - 1], recv_sem=a_recv.at[1, r - 1],
            device_id=(dp, (x * 2 + yhi) * 4 + to), device_id_type=MESH,
        )

    for r in (2, 1, 3):
        x_copy(r).start()
        z_copy(r).start()

    d = (e_v[...] * weight - d_v[...]).astype(BF16)
    df = d.astype(F32)

    def grad_part(to):
        return dot(qht_v[pl.ds(pl.multiple_of(to * part, 64), part), :], d, NT)

    def core_copy(i):
        return pltpu.make_async_remote_copy(
            src_ref=core_s.at[i], dst_ref=core_r.at[i], send_sem=core_send.at[i], recv_sem=core_recv.at[i],
            device_id=(ylo * 2 + 1 - core, cent), device_id_type=MESH,
        )

    y_copy = pltpu.make_async_remote_copy(
        src_ref=y_s, dst_ref=y_r, send_sem=y_sem.at[0], recv_sem=y_sem.at[1],
        device_id=((1 - ylo) * 2 + core, cent), device_id_type=MESH,
    )

    core_s[0] = grad_part((1 - ylo) * 2 + 1 - core).astype(BF16)
    core_copy(0).start()
    core_s[1] = grad_part(ylo * 2 + 1 - core).astype(BF16)
    core_copy(1).start()
    far = grad_part((1 - ylo) * 2 + core)
    core_copy(0).wait()
    y_s[...] = (far + core_r[0].astype(F32)).astype(BF16)
    y_copy.start()
    near = grad_part(dp)

    prod = df * cos_v[...]
    prod = prod[:, 0:128] + prod[:, 128:256] + prod[:, 256:384] + prod[:, 384:512]
    rowdot = jnp.sum(prod.T, axis=0, keepdims=True)
    row_s[...] = rowdot

    def row_copy(r):
        return pltpu.make_async_remote_copy(
            src_ref=row_s, dst_ref=row_r.at[r - 1], send_sem=row_sem.at[0, r - 1], recv_sem=row_sem.at[1, r - 1],
            device_id=((dp + r) % 4, cent), device_id_type=MESH,
        )

    for r in range(1, 4):
        row_copy(r).start()
    core_copy(1).wait()
    near = near + core_r[1].astype(F32)

    def bx_copy(r):
        tz = (z + r) % 4
        ty = (yhi + r // 4) % 2
        return pltpu.make_async_remote_copy(
            src_ref=bx_s.at[ty * 4 + tz], dst_ref=bx_r.at[r - 1], send_sem=b_sem.at[0], recv_sem=b_sem.at[1],
            device_id=(dp, (x * 2 + ty) * 4 + tz), device_id_type=MESH,
        )

    def bz_copy(r):
        tx = (x + r) % 4
        ty = (yhi + r // 4) % 2
        return pltpu.make_async_remote_copy(
            src_ref=bz_s.at[tx * 2 + ty], dst_ref=bz_r.at[r - 1], send_sem=b_sem.at[2], recv_sem=b_sem.at[3],
            device_id=(dp, (tx * 2 + ty) * 4 + z), device_id_type=MESH,
        )

    for r in range(1, 4):
        x_copy(r).wait()
    total = gx_s[x].astype(F32)
    for r in range(3):
        total = total + gx_r[r].astype(F32)
    bx_s[...] = total.astype(BF16).reshape(8, 16, half)

    @pl.loop(1, 8)
    def _(r):
        bx_copy(r).start()

    for r in range(1, 4):
        z_copy(r).wait()
    total = gz_s[z].astype(F32)
    for r in range(3):
        total = total + gz_r[r].astype(F32)
    bz_s[...] = total.astype(BF16)

    @pl.loop(1, 8)
    def _(r):
        bz_copy(r).start()

    y_copy.wait()
    for r in range(1, 4):
        row_copy(r).wait()
        rowdot = rowdot + row_r[r - 1]
    near = near + y_r[...].astype(F32)
    own_cent = ct_v[pl.ds(pl.multiple_of(dp * part, 64), part), :].astype(F32)
    cg_ref[...] = (near - rowdot * own_cent).T

    mine = pl.ds(pl.multiple_of(cent * 16, 16), 16)
    qf = q_v[mine, :].astype(F32)
    norm = jnp.sqrt(jnp.sum(qf * qf, axis=1, keepdims=True) + EPS)
    hat = qh_v[mine, :].astype(F32)
    pltpu.make_async_copy(bx_r, bx_r, b_sem.at[1]).wait()
    left = bx_s[yhi * 4 + z].astype(F32) + jnp.sum(bx_r[...].astype(F32), axis=0)
    pltpu.make_async_copy(bz_r, bz_r, b_sem.at[3]).wait()
    right = bz_s[x * 2 + yhi].astype(F32) + jnp.sum(bz_r[...].astype(F32), axis=0)
    grad = jnp.concatenate([left, right], axis=1)
    along = jnp.sum(grad * hat, axis=1, keepdims=True)
    qg_ref[...] = (grad - along * hat) / norm

    pltpu.make_async_copy(lse_r, lse_r, lse_sem.at[0]).wait()
    pltpu.make_async_copy(bx_r, bx_r, b_sem.at[0]).wait()
    pltpu.make_async_copy(bz_r, bz_r, b_sem.at[2]).wait()


def local(queries, centroids, beta, teacher_ids):
    rows, width = queries.shape
    cells = centroids.shape[0]
    slots = teacher_ids.shape[1]
    half, part = width // 2, width // 4
    dma = pltpu.SemaphoreType.DMA
    return pl.pallas_call(
        kernel,
        out_shape=(
            jax.ShapeDtypeStruct((rows // 32, width), F32),
            jax.ShapeDtypeStruct((cells, part), F32),
        ),
        in_specs=[pl.BlockSpec(memory_space=pl.ANY)] * 4,
        out_specs=[pl.BlockSpec(memory_space=pltpu.VMEM)] * 2,
        scratch_shapes=[
            pltpu.VMEM((rows, width), BF16),
            pltpu.VMEM((cells, width), BF16),
            pltpu.VMEM((1, rows), F32),
            pltpu.VMEM((slots, rows), jnp.int32),
            pltpu.VMEM((rows, width), BF16),
            pltpu.VMEM((width, rows), BF16),
            pltpu.VMEM((width, cells), BF16),
            pltpu.VMEM((cells, rows), F32),
            pltpu.VMEM((cells, rows), F32),
            pltpu.VMEM((cells, rows), F32),
            pltpu.VMEM((rows, width), F32),
            pltpu.VMEM((rows, width), F32),
            pltpu.VMEM((1, 1, rows), F32),
            pltpu.VMEM((31, 1, rows), F32),
            pltpu.VMEM((4, rows // 4, half), BF16),
            pltpu.VMEM((3, rows // 4, half), BF16),
            pltpu.VMEM((4, 8, 16, half), BF16),
            pltpu.VMEM((3, 8, 16, half), BF16),
            pltpu.VMEM((8, 16, half), BF16),
            pltpu.VMEM((7, 16, half), BF16),
            pltpu.VMEM((8, 16, half), BF16),
            pltpu.VMEM((7, 16, half), BF16),
            pltpu.VMEM((2, part, cells), BF16),
            pltpu.VMEM((2, part, cells), BF16),
            pltpu.VMEM((part, cells), BF16),
            pltpu.VMEM((part, cells), BF16),
            pltpu.VMEM((1, cells), F32),
            pltpu.VMEM((3, 1, cells), F32),
            dma((4,)),
            dma((2,)),
            dma((2, 3)),
            dma((2, 3)),
            dma((4,)),
            dma((2,)),
            dma((2,)),
            dma((2,)),
            dma((2, 3)),
        ],
        compiler_params=pltpu.CompilerParams(
            collective_id=0, has_side_effects=True, vmem_limit_bytes=60 * 1024 * 1024
        ),
    )(queries, centroids, beta.reshape(1, rows), teacher_ids.T)


def solution(mesh):
    in_specs = (P("dp", None), P("cent", None), P("dp"), P("dp", None))
    out_specs = (P(("dp", "cent"), None), P("cent", "dp"))
    return jax.shard_map(local, mesh=mesh, in_specs=in_specs, out_specs=out_specs, check_vma=False)
```

```python
import functools

import jax
import jax.numpy as jnp
from jax import lax
from jax.experimental import pallas as pl
from jax.experimental.pallas import tpu as pltpu
from jax.sharding import PartitionSpec as P

EPS = 1e-06
SCALE = 1024.0
MESH = pl.DeviceIdType.MESH
F32 = jnp.float32
BF16 = jnp.bfloat16
NT = (((1,), (1,)), ((), ()))
TN = (((0,), (0,)), ((), ()))


def dot(a, b, dims):
    return lax.dot_general(a, b, dims, preferred_element_type=F32)


def join(own, others):
    top = jnp.maximum(jnp.max(others, axis=0), own)
    return top + jnp.log(jnp.sum(jnp.exp(others - top[None]), axis=0) + jnp.exp(own - top))


def kernel(
    q_hbm, c_hbm, beta_hbm, ids_hbm,
    qg_ref, cg_ref,
    q_v, c_v, beta_v, ids_v,
    qh_v, qht_v, ct_v, cos_v, e_v, d_v,
    es_v, ts_v,
    lse_s, lse_r,
    gx_s, gx_r, gz_s, gz_r,
    bx_s, bx_r, bz_s, bz_r,
    core_s, core_r, y_s, y_r,
    near_v, row_s, row_r,
    in_sem, lse_sem, a_send, a_recv, b_sem, core_send, core_recv, y_send, y_recv, row_sem, ready_sem,
):
    rows, width = q_hbm.shape
    cells = c_hbm.shape[0]
    slots = ids_hbm.shape[0]
    half = width // 2
    part = width // 4
    dp = lax.axis_index("dp")
    cent = lax.axis_index("cent")
    x = cent // 8
    yhi = (cent // 4) % 2
    z = cent % 4
    core = dp % 2
    ylo = dp // 2

    loads = [
        pltpu.make_async_copy(src, dst, in_sem.at[i])
        for i, (src, dst) in enumerate(((q_hbm, q_v), (c_hbm, c_v), (beta_hbm, beta_v), (ids_hbm, ids_v)))
    ]
    for load in loads:
        load.start()

    barrier = pltpu.get_barrier_semaphore()

    for r in range(1, 4):
        pl.semaphore_signal(barrier, inc=1, device_id=(dp, (((x + r) % 4) * 2 + yhi) * 4 + z), device_id_type=MESH)
        pl.semaphore_signal(barrier, inc=1, device_id=(dp, (x * 2 + yhi) * 4 + (z + r) % 4), device_id_type=MESH)
        pl.semaphore_signal(barrier, inc=1, device_id=((dp + r) % 4, cent), device_id_type=MESH)
    pl.semaphore_signal(barrier, inc=1, device_id=(dp, (x * 2 + 1 - yhi) * 4 + z), device_id_type=MESH)

    loads[0].wait()
    for i in range(4):
        block = pl.ds(i * (rows // 4), rows // 4)
        qf = q_v[block, :].astype(F32)
        inv = 1.0 / jnp.sqrt(jnp.sum(qf * qf, axis=1, keepdims=True) + EPS)
        qh_v[block, :] = (qf * inv).astype(BF16)

    loads[1].wait()
    loads[2].wait()
    loads[3].wait()
    tops = []
    for i in range(2):
        lanes = pl.ds(i * (rows // 2), rows // 2)
        cosine = dot(c_v[...], qh_v[lanes, :], NT)
        cos_v[:, lanes] = cosine
        score = cosine * beta_v[:, lanes]
        top = jnp.max(score, axis=0, keepdims=True)
        expo = jnp.exp(score - top)
        e_v[:, lanes] = expo
        lse_s[0, :, lanes] = top + jnp.log(jnp.sum(expo, axis=0, keepdims=True))
        tops.append(top)

    pl.semaphore_wait(barrier, 10)
    pl.semaphore_signal(ready_sem, inc=1, device_id=(dp, (x * 2 + 1 - yhi) * 4 + z), device_id_type=MESH)

    def line_copy(r):
        return pltpu.make_async_remote_copy(
            src_ref=lse_s.at[0], dst_ref=lse_r.at[r - 1], send_sem=lse_sem.at[0], recv_sem=lse_sem.at[1],
            device_id=(dp, (((x + r) % 4) * 2 + yhi) * 4 + z), device_id_type=MESH,
        )

    def plane_copy(r):
        return pltpu.make_async_remote_copy(
            src_ref=lse_s.at[1], dst_ref=lse_r.at[r + 2], send_sem=lse_sem.at[2], recv_sem=lse_sem.at[3],
            device_id=(dp, (x * 2 + (yhi + r // 4) % 2) * 4 + (z + r) % 4), device_id_type=MESH,
        )

    for r in (2, 1, 3):
        line_copy(r).start()

    qht_v[...] = qh_v[...].T
    ct_v[...] = c_v[...].T
    for i in range(2):
        lanes = pl.ds(i * (rows // 2), rows // 2)
        e = e_v[:, lanes]
        high = e.astype(BF16)
        low = (e - high.astype(F32)).astype(BF16)
        es_v[lanes, :] = dot(high, c_v[...], TN) + dot(low, c_v[...], TN)

    line = pl.ds(0, 3)
    pltpu.make_async_copy(lse_r.at[line], lse_r.at[line], lse_sem.at[1]).wait()
    lse_s[1] = join(lse_s[0], lse_r[0:3])
    for r in (1, 2, 3, 4):
        plane_copy(r).start()
    pl.semaphore_wait(ready_sem, 1)
    for r in (5, 6, 7):
        plane_copy(r).start()

    first = cent * cells
    for i in range(2):
        lanes = pl.ds(i * (rows // 2), rows // 2)
        cell_pos = lax.broadcasted_iota(jnp.int32, (cells, rows // 2), 0) + first
        count = jnp.zeros((cells, rows // 2), F32)
        for slot in range(slots):
            count = count + jnp.where(ids_v[slot : slot + 1, lanes] == cell_pos, SCALE / slots, 0.0)
        d_v[:, lanes] = count
        ts_v[lanes, :] = dot(count.astype(BF16), c_v[...], TN)

    plane = pl.ds(3, 7)
    pltpu.make_async_copy(lse_r.at[plane], lse_r.at[plane], lse_sem.at[3]).wait()
    lse = join(lse_s[1], lse_r[3:10])
    weight = jnp.exp(jnp.concatenate(tops, axis=1) - lse) * SCALE
    weight_col = jnp.broadcast_to(weight, (128, rows)).T

    for i in range(rows // 128):
        block = pl.ds(i * 128, 128)
        for j in range(3):
            cols = pl.ds(j * 128, 128)
            gx_s[i, :, cols] = (es_v[block, cols] * weight_col[i * 128 : (i + 1) * 128] - ts_v[block, cols]).astype(BF16)
        for j in range(3):
            cols = pl.ds(half + j * 128, 128)
            g = (es_v[block, cols] * weight_col[i * 128 : (i + 1) * 128] - ts_v[block, cols]).astype(BF16)
            for k in range(8):
                gz_s[k % 4, 2 * i + k // 4, :, pl.ds(j * 128, 128)] = g[k * 16 : (k + 1) * 16]

    def x_copy(to, r):
        return pltpu.make_async_remote_copy(
            src_ref=gx_s.at[to], dst_ref=gx_r.at[r - 1], send_sem=a_send.at[0, r - 1], recv_sem=a_recv.at[0, r - 1],
            device_id=(dp, (to * 2 + yhi) * 4 + z), device_id_type=MESH,
        )

    def z_copy(to, r):
        return pltpu.make_async_remote_copy(
            src_ref=gz_s.at[to], dst_ref=gz_r.at[r - 1], send_sem=a_send.at[1, r - 1], recv_sem=a_recv.at[1, r - 1],
            device_id=(dp, (x * 2 + yhi) * 4 + to), device_id_type=MESH,
        )

    for to in range(4):

        @pl.when(to != x)
        def _():
            x_copy(to, (to + 4 - x) % 4).start()

        @pl.when(to != z)
        def _():
            z_copy(to, (to + 4 - z) % 4).start()

    def grad_part(to, d):
        return dot(qht_v[pl.ds(pl.multiple_of(to * part, 64), part), :], d, NT)

    def core_copy(i):
        return pltpu.make_async_remote_copy(
            src_ref=core_s.at[i], dst_ref=core_r.at[i], send_sem=core_send.at[i], recv_sem=core_recv.at[i],
            device_id=(ylo * 2 + 1 - core, cent), device_id_type=MESH,
        )

    def y_copy(i):
        return pltpu.make_async_remote_copy(
            src_ref=y_s.at[i], dst_ref=y_r.at[i], send_sem=y_send.at[i], recv_sem=y_recv.at[i],
            device_id=((1 - ylo) * 2 + core, cent), device_id_type=MESH,
        )

    ds = []
    for i in range(2):
        block = pl.ds(i * (cells // 2), cells // 2)
        d = (e_v[block, :] * weight - d_v[block, :]).astype(BF16)
        ds.append(d)
        core_s[i] = grad_part((1 - ylo) * 2 + 1 - core, d).astype(BF16)
        core_copy(i).start()
    far = [grad_part((1 - ylo) * 2 + core, d) for d in ds]
    for i in range(2):
        core_copy(i).wait()
        y_s[i] = (far[i] + core_r[i].astype(F32)).astype(BF16)
        y_copy(i).start()
    for i in range(2):
        core_s[2 + i] = grad_part(ylo * 2 + 1 - core, ds[i]).astype(BF16)
        core_copy(2 + i).start()
    for i in range(2):
        near_v[i] = grad_part(dp, ds[i])

    for i in range(2):
        block = pl.ds(i * (cells // 2), cells // 2)
        prod = ds[i].astype(F32) * cos_v[block, :]
        prod = prod[:, 0:128] + prod[:, 128:256] + prod[:, 256:384] + prod[:, 384:512]
        row_s[:, block] = jnp.sum(prod.T, axis=0, keepdims=True)

    def row_copy(r):
        return pltpu.make_async_remote_copy(
            src_ref=row_s, dst_ref=row_r.at[r - 1], send_sem=row_sem.at[0, r - 1], recv_sem=row_sem.at[1, r - 1],
            device_id=((dp + r) % 4, cent), device_id_type=MESH,
        )

    for r in range(1, 4):
        row_copy(r).start()

    def bx_copy(to, r):
        return pltpu.make_async_remote_copy(
            src_ref=bx_s.at[to], dst_ref=bx_r.at[r - 1], send_sem=b_sem.at[0], recv_sem=b_sem.at[1],
            device_id=(dp, x * 8 + to), device_id_type=MESH,
        )

    def bz_copy(to, r):
        return pltpu.make_async_remote_copy(
            src_ref=bz_s.at[to], dst_ref=bz_r.at[r - 1], send_sem=b_sem.at[2], recv_sem=b_sem.at[3],
            device_id=(dp, to * 4 + z), device_id_type=MESH,
        )

    for r in range(1, 4):
        x_copy(0, r).wait()
    total = gx_s[x].astype(F32)
    for r in range(3):
        total = total + gx_r[r].astype(F32)
    bx_s[...] = total.astype(BF16).reshape(8, 16, half)

    @pl.loop(0, 8)
    def _(to):
        @pl.when(to != yhi * 4 + z)
        def _():
            bx_copy(to, ((to // 4 + 2 - yhi) % 2) * 4 + (to + 4 - z) % 4).start()

    for r in range(1, 4):
        z_copy(0, r).wait()
    total = gz_s[z].astype(F32)
    for r in range(3):
        total = total + gz_r[r].astype(F32)
    bz_s[...] = total.astype(BF16)

    @pl.loop(0, 8)
    def _(to):
        @pl.when(to != x * 2 + yhi)
        def _():
            bz_copy(to, ((to + 2 - yhi) % 2) * 4 + (to // 2 + 4 - x) % 4).start()

    for r in range(1, 4):
        row_copy(r).wait()
    rowdot = row_s[...] + row_r[0] + row_r[1] + row_r[2]
    own_rows = pl.ds(pl.multiple_of(dp * part, 64), part)
    for i in range(2):
        block = pl.ds(i * (cells // 2), cells // 2)
        core_copy(2 + i).wait()
        y_copy(i).wait()
        grad = near_v[i] + core_r[2 + i].astype(F32) + y_r[i].astype(F32)
        here = slice(i * (cells // 2), (i + 1) * (cells // 2))
        cg_ref[:, block] = grad - rowdot[:, here] * ct_v[own_rows, block].astype(F32)

    mine = pl.ds(pl.multiple_of(cent * 16, 16), 16)
    qf = q_v[mine, :].astype(F32)
    norm = jnp.sqrt(jnp.sum(qf * qf, axis=1, keepdims=True) + EPS)
    hat = qh_v[mine, :].astype(F32)
    pltpu.make_async_copy(bx_r, bx_r, b_sem.at[1]).wait()
    left = bx_s[yhi * 4 + z].astype(F32) + jnp.sum(bx_r[...].astype(F32), axis=0)
    pltpu.make_async_copy(bz_r, bz_r, b_sem.at[3]).wait()
    right = bz_s[x * 2 + yhi].astype(F32) + jnp.sum(bz_r[...].astype(F32), axis=0)
    grad = jnp.concatenate([left, right], axis=1)
    along = jnp.sum(grad * hat, axis=1, keepdims=True)
    qg_ref[...] = (grad - along * hat) / norm

    pltpu.make_async_copy(lse_r.at[line], lse_r.at[line], lse_sem.at[0]).wait()
    pltpu.make_async_copy(lse_r.at[plane], lse_r.at[plane], lse_sem.at[2]).wait()
    pltpu.make_async_copy(bx_r, bx_r, b_sem.at[0]).wait()
    pltpu.make_async_copy(bz_r, bz_r, b_sem.at[2]).wait()


def local(queries, centroids, beta, teacher_ids):
    rows, width = queries.shape
    cells = centroids.shape[0]
    slots = teacher_ids.shape[1]
    half, part = width // 2, width // 4
    dma = pltpu.SemaphoreType.DMA
    query_grad, centroid_grad = pl.pallas_call(
        kernel,
        out_shape=(
            jax.ShapeDtypeStruct((rows // 32, width), F32),
            jax.ShapeDtypeStruct((part, cells), F32),
        ),
        in_specs=[pl.BlockSpec(memory_space=pltpu.MemorySpace.HBM)] * 4,
        out_specs=[pl.BlockSpec(memory_space=pltpu.VMEM)] * 2,
        scratch_shapes=[
            pltpu.VMEM((rows, width), BF16),
            pltpu.VMEM((cells, width), BF16),
            pltpu.VMEM((1, rows), F32),
            pltpu.VMEM((slots, rows), jnp.int32),
            pltpu.VMEM((rows, width), BF16),
            pltpu.VMEM((width, rows), BF16),
            pltpu.VMEM((width, cells), BF16),
            pltpu.VMEM((cells, rows), F32),
            pltpu.VMEM((cells, rows), F32),
            pltpu.VMEM((cells, rows), F32),
            pltpu.VMEM((rows, width), F32),
            pltpu.VMEM((rows, width), F32),
            pltpu.VMEM((2, 1, rows), F32),
            pltpu.VMEM((10, 1, rows), F32),
            pltpu.VMEM((4, rows // 4, half), BF16),
            pltpu.VMEM((3, rows // 4, half), BF16),
            pltpu.VMEM((4, 8, 16, half), BF16),
            pltpu.VMEM((3, 8, 16, half), BF16),
            pltpu.VMEM((8, 16, half), BF16),
            pltpu.VMEM((7, 16, half), BF16),
            pltpu.VMEM((8, 16, half), BF16),
            pltpu.VMEM((7, 16, half), BF16),
            pltpu.VMEM((4, part, cells // 2), BF16),
            pltpu.VMEM((4, part, cells // 2), BF16),
            pltpu.VMEM((2, part, cells // 2), BF16),
            pltpu.VMEM((2, part, cells // 2), BF16),
            pltpu.VMEM((2, part, cells // 2), F32),
            pltpu.VMEM((1, cells), F32),
            pltpu.VMEM((3, 1, cells), F32),
            dma((4,)),
            dma((4,)),
            dma((2, 3)),
            dma((2, 3)),
            dma((4,)),
            dma((4,)),
            dma((4,)),
            dma((2,)),
            dma((2,)),
            dma((2, 3)),
            pltpu.SemaphoreType.REGULAR,
        ],
        compiler_params=pltpu.CompilerParams(
            collective_id=0, has_side_effects=True, vmem_limit_bytes=24 * 1024 * 1024
        ),
    )(queries, centroids, beta.reshape(1, rows), teacher_ids.T)
    return query_grad, centroid_grad.T


def solution(mesh):
    in_specs = (P("dp", None), P("cent", None), P("dp"), P("dp", None))
    out_specs = (P(("dp", "cent"), None), P("cent", "dp"))
    return jax.shard_map(local, mesh=mesh, in_specs=in_specs, out_specs=out_specs, check_vma=False)
```

```python
import functools

import jax
import jax.numpy as jnp
from jax import lax
from jax.experimental import pallas as pl
from jax.experimental.pallas import tpu as pltpu
from jax.sharding import PartitionSpec as P

EPS = 1e-06
SCALE = 1024.0
MESH = pl.DeviceIdType.MESH
F32 = jnp.float32
BF16 = jnp.bfloat16
NT = (((1,), (1,)), ((), ()))
TN = (((0,), (0,)), ((), ()))


def dot(a, b, dims):
    return lax.dot_general(a, b, dims, preferred_element_type=F32)


def join(own, others):
    top = jnp.maximum(jnp.max(others, axis=0), own)
    return top + jnp.log(jnp.sum(jnp.exp(others - top[None]), axis=0) + jnp.exp(own - top))


def kernel(
    q_hbm, c_hbm, beta_hbm, ids_hbm,
    qg_ref, cg_ref,
    q_v, c_v, beta_v, ids_v,
    qh_v, qht_v, ct_v, cos_v, e_v, d_v,
    es_v, ts_v,
    lse_s, lse_r,
    gx_s, gx_r, gz_s, gz_r,
    bx_s, bx_r, bz_s, bz_r,
    core_s, core_r, y_s, y_r,
    near_v, row_s, row_r,
    in_sem, lse_sem, a_send, a_recv, b_sem, core_send, core_recv, y_send, y_recv, row_sem, ready_sem,
):
    rows, width = q_hbm.shape
    cells = c_hbm.shape[0]
    slots = ids_hbm.shape[0]
    half = width // 2
    part = width // 4
    dp = lax.axis_index("dp")
    cent = lax.axis_index("cent")
    x = cent // 8
    yhi = (cent // 4) % 2
    z = cent % 4
    core = dp % 2
    ylo = dp // 2

    loads = [
        pltpu.make_async_copy(src, dst, in_sem.at[i])
        for i, (src, dst) in enumerate(((q_hbm, q_v), (c_hbm, c_v), (beta_hbm, beta_v), (ids_hbm, ids_v)))
    ]
    for load in loads:
        load.start()

    barrier = pltpu.get_barrier_semaphore()

    for r in range(1, 4):
        pl.semaphore_signal(barrier, inc=1, device_id=(dp, (((x + r) % 4) * 2 + yhi) * 4 + z), device_id_type=MESH)
        pl.semaphore_signal(barrier, inc=1, device_id=(dp, (x * 2 + yhi) * 4 + (z + r) % 4), device_id_type=MESH)
        pl.semaphore_signal(barrier, inc=1, device_id=((dp + r) % 4, cent), device_id_type=MESH)
    pl.semaphore_signal(barrier, inc=1, device_id=(dp, (x * 2 + 1 - yhi) * 4 + z), device_id_type=MESH)

    loads[0].wait()
    for i in range(4):
        block = pl.ds(i * (rows // 4), rows // 4)
        qf = q_v[block, :].astype(F32)
        inv = 1.0 / jnp.sqrt(jnp.sum(qf * qf, axis=1, keepdims=True) + EPS)
        qh_v[block, :] = (qf * inv).astype(BF16)

    loads[1].wait()
    loads[2].wait()
    loads[3].wait()
    tops = []
    for i in range(2):
        lanes = pl.ds(i * (rows // 2), rows // 2)
        cosine = dot(c_v[...], qh_v[lanes, :], NT)
        cos_v[:, lanes] = cosine
        score = cosine * beta_v[:, lanes]
        top = jnp.max(score, axis=0, keepdims=True)
        expo = jnp.exp(score - top)
        e_v[:, lanes] = expo
        lse_s[0, :, lanes] = top + jnp.log(jnp.sum(expo, axis=0, keepdims=True))
        tops.append(top)

    pl.semaphore_wait(barrier, 10)
    pl.semaphore_signal(ready_sem, inc=1, device_id=(dp, (x * 2 + 1 - yhi) * 4 + z), device_id_type=MESH)

    def line_copy(r):
        return pltpu.make_async_remote_copy(
            src_ref=lse_s.at[0], dst_ref=lse_r.at[r - 1], send_sem=lse_sem.at[0], recv_sem=lse_sem.at[1],
            device_id=(dp, (((x + r) % 4) * 2 + yhi) * 4 + z), device_id_type=MESH,
        )

    def plane_copy(r):
        return pltpu.make_async_remote_copy(
            src_ref=lse_s.at[1], dst_ref=lse_r.at[r + 2], send_sem=lse_sem.at[2], recv_sem=lse_sem.at[3],
            device_id=(dp, (x * 2 + (yhi + r // 4) % 2) * 4 + (z + r) % 4), device_id_type=MESH,
        )

    for r in (2, 1, 3):
        line_copy(r).start()

    qht_v[...] = qh_v[...].T
    ct_v[...] = c_v[...].T
    for i in range(2):
        lanes = pl.ds(i * (rows // 2), rows // 2)
        e = e_v[:, lanes]
        high = e.astype(BF16)
        low = (e - high.astype(F32)).astype(BF16)
        es_v[lanes, :] = dot(high, c_v[...], TN) + dot(low, c_v[...], TN)

    line = pl.ds(0, 3)
    pltpu.make_async_copy(lse_r.at[line], lse_r.at[line], lse_sem.at[1]).wait()
    lse_s[1] = join(lse_s[0], lse_r[0:3])
    for r in (1, 2, 3, 4):
        plane_copy(r).start()
    pl.semaphore_wait(ready_sem, 1)
    for r in (5, 6, 7):
        plane_copy(r).start()

    first = cent * cells
    for i in range(2):
        lanes = pl.ds(i * (rows // 2), rows // 2)
        cell_pos = lax.broadcasted_iota(jnp.int32, (cells, rows // 2), 0) + first
        count = jnp.zeros((cells, rows // 2), F32)
        for slot in range(slots):
            count = count + jnp.where(ids_v[slot : slot + 1, lanes] == cell_pos, SCALE / slots, 0.0)
        d_v[:, lanes] = count
        ts_v[lanes, :] = dot(count.astype(BF16), c_v[...], TN)

    plane = pl.ds(3, 7)
    pltpu.make_async_copy(lse_r.at[plane], lse_r.at[plane], lse_sem.at[3]).wait()
    lse = join(lse_s[1], lse_r[3:10])
    weight = jnp.exp(jnp.concatenate(tops, axis=1) - lse) * SCALE
    weight_col = jnp.broadcast_to(weight, (128, rows)).T

    for i in range(rows // 128):
        block = pl.ds(i * 128, 128)
        for j in range(3):
            cols = pl.ds(j * 128, 128)
            gx_s[i, :, cols] = (es_v[block, cols] * weight_col[i * 128 : (i + 1) * 128] - ts_v[block, cols]).astype(BF16)
        for j in range(3):
            cols = pl.ds(half + j * 128, 128)
            g = (es_v[block, cols] * weight_col[i * 128 : (i + 1) * 128] - ts_v[block, cols]).astype(BF16)
            for k in range(8):
                gz_s[k % 4, 2 * i + k // 4, :, pl.ds(j * 128, 128)] = g[k * 16 : (k + 1) * 16]

    def x_copy(to, r):
        return pltpu.make_async_remote_copy(
            src_ref=gx_s.at[to], dst_ref=gx_r.at[r - 1], send_sem=a_send.at[0, r - 1], recv_sem=a_recv.at[0, r - 1],
            device_id=(dp, (to * 2 + yhi) * 4 + z), device_id_type=MESH,
        )

    def z_copy(to, r):
        return pltpu.make_async_remote_copy(
            src_ref=gz_s.at[to], dst_ref=gz_r.at[r - 1], send_sem=a_send.at[1, r - 1], recv_sem=a_recv.at[1, r - 1],
            device_id=(dp, (x * 2 + yhi) * 4 + to), device_id_type=MESH,
        )

    for to in range(4):

        @pl.when(to != x)
        def _():
            x_copy(to, (to + 4 - x) % 4).start()

        @pl.when(to != z)
        def _():
            z_copy(to, (to + 4 - z) % 4).start()

    def grad_part(to, d):
        return dot(qht_v[pl.ds(pl.multiple_of(to * part, 64), part), :], d, NT)

    def core_copy(i):
        return pltpu.make_async_remote_copy(
            src_ref=core_s.at[i], dst_ref=core_r.at[i], send_sem=core_send.at[i], recv_sem=core_recv.at[i],
            device_id=(ylo * 2 + 1 - core, cent), device_id_type=MESH,
        )

    def y_copy(i):
        return pltpu.make_async_remote_copy(
            src_ref=y_s.at[i], dst_ref=y_r.at[i], send_sem=y_send.at[i], recv_sem=y_recv.at[i],
            device_id=((1 - ylo) * 2 + core, cent), device_id_type=MESH,
        )

    ds = []
    for i in range(2):
        block = pl.ds(i * (cells // 2), cells // 2)
        d = (e_v[block, :] * weight - d_v[block, :]).astype(BF16)
        ds.append(d)
        core_s[i] = grad_part((1 - ylo) * 2 + 1 - core, d).astype(BF16)
        core_copy(i).start()
    far = [grad_part((1 - ylo) * 2 + core, d) for d in ds]
    for i in range(2):
        core_copy(i).wait()
        y_s[i] = (far[i] + core_r[i].astype(F32)).astype(BF16)
        y_copy(i).start()
    for i in range(2):
        core_s[2 + i] = grad_part(ylo * 2 + 1 - core, ds[i]).astype(BF16)
        core_copy(2 + i).start()
    for i in range(2):
        near_v[i] = grad_part(dp, ds[i])

    for i in range(2):
        block = pl.ds(i * (cells // 2), cells // 2)
        prod = ds[i].astype(F32) * cos_v[block, :]
        prod = prod[:, 0:128] + prod[:, 128:256] + prod[:, 256:384] + prod[:, 384:512]
        row_s[:, block] = jnp.sum(prod.T, axis=0, keepdims=True)

    def row_copy(r):
        return pltpu.make_async_remote_copy(
            src_ref=row_s, dst_ref=row_r.at[r - 1], send_sem=row_sem.at[0, r - 1], recv_sem=row_sem.at[1, r - 1],
            device_id=((dp + r) % 4, cent), device_id_type=MESH,
        )

    for r in range(1, 4):
        row_copy(r).start()

    def bx_copy(to, r):
        return pltpu.make_async_remote_copy(
            src_ref=bx_s.at[to], dst_ref=bx_r.at[r - 1], send_sem=b_sem.at[0], recv_sem=b_sem.at[1],
            device_id=(dp, x * 8 + to), device_id_type=MESH,
        )

    def bz_copy(to, r):
        return pltpu.make_async_remote_copy(
            src_ref=bz_s.at[to], dst_ref=bz_r.at[r - 1], send_sem=b_sem.at[2], recv_sem=b_sem.at[3],
            device_id=(dp, to * 4 + z), device_id_type=MESH,
        )

    for r in range(1, 4):
        x_copy(0, r).wait()
    total = gx_s[x].astype(F32)
    for r in range(3):
        total = total + gx_r[r].astype(F32)
    bx_s[...] = total.astype(BF16).reshape(8, 16, half)

    @pl.loop(0, 8)
    def _(to):
        @pl.when(to != yhi * 4 + z)
        def _():
            bx_copy(to, ((to // 4 + 2 - yhi) % 2) * 4 + (to + 4 - z) % 4).start()

    for r in range(1, 4):
        z_copy(0, r).wait()
    total = gz_s[z].astype(F32)
    for r in range(3):
        total = total + gz_r[r].astype(F32)
    bz_s[...] = total.astype(BF16)

    @pl.loop(0, 8)
    def _(to):
        @pl.when(to != x * 2 + yhi)
        def _():
            bz_copy(to, ((to + 2 - yhi) % 2) * 4 + (to // 2 + 4 - x) % 4).start()

    for r in range(1, 4):
        row_copy(r).wait()
    rowdot = row_s[...] + row_r[0] + row_r[1] + row_r[2]
    own_rows = pl.ds(pl.multiple_of(dp * part, 64), part)
    for i in range(2):
        block = pl.ds(i * (cells // 2), cells // 2)
        core_copy(2 + i).wait()
        y_copy(i).wait()
        grad = near_v[i] + core_r[2 + i].astype(F32) + y_r[i].astype(F32)
        here = slice(i * (cells // 2), (i + 1) * (cells // 2))
        cg_ref[:, block] = grad - rowdot[:, here] * ct_v[own_rows, block].astype(F32)

    mine = pl.ds(pl.multiple_of(cent * 16, 16), 16)
    qf = q_v[mine, :].astype(F32)
    norm = jnp.sqrt(jnp.sum(qf * qf, axis=1, keepdims=True) + EPS)
    hat = qh_v[mine, :].astype(F32)
    pltpu.make_async_copy(bx_r, bx_r, b_sem.at[1]).wait()
    left = bx_s[yhi * 4 + z].astype(F32) + jnp.sum(bx_r[...].astype(F32), axis=0)
    pltpu.make_async_copy(bz_r, bz_r, b_sem.at[3]).wait()
    right = bz_s[x * 2 + yhi].astype(F32) + jnp.sum(bz_r[...].astype(F32), axis=0)
    grad = jnp.concatenate([left, right], axis=1)
    along = jnp.sum(grad * hat, axis=1, keepdims=True)
    qg_ref[...] = (grad - along * hat) / norm

    pltpu.make_async_copy(lse_r.at[line], lse_r.at[line], lse_sem.at[0]).wait()
    pltpu.make_async_copy(lse_r.at[plane], lse_r.at[plane], lse_sem.at[2]).wait()
    pltpu.make_async_copy(bx_r, bx_r, b_sem.at[0]).wait()
    pltpu.make_async_copy(bz_r, bz_r, b_sem.at[2]).wait()


def store_results(qg_v, cg_v, qg_hbm, cg_hbm, sem):
    copies = [pltpu.make_async_copy(cg_v, cg_hbm, sem.at[0]), pltpu.make_async_copy(qg_v, qg_hbm, sem.at[1])]
    for copy in copies:
        copy.start()
    for copy in copies:
        copy.wait()


def local(queries, centroids, beta, teacher_ids):
    rows, width = queries.shape
    cells = centroids.shape[0]
    slots = teacher_ids.shape[1]
    half, part = width // 2, width // 4
    dma = pltpu.SemaphoreType.DMA
    results = pl.pallas_call(
        kernel,
        out_shape=(
            jax.ShapeDtypeStruct((rows // 32, width), F32),
            jax.ShapeDtypeStruct((part, cells), F32),
        ),
        in_specs=[pl.BlockSpec(memory_space=pltpu.MemorySpace.HBM)] * 4,
        out_specs=[pl.BlockSpec(memory_space=pltpu.VMEM)] * 2,
        scratch_shapes=[
            pltpu.VMEM((rows, width), BF16),
            pltpu.VMEM((cells, width), BF16),
            pltpu.VMEM((1, rows), F32),
            pltpu.VMEM((slots, rows), jnp.int32),
            pltpu.VMEM((rows, width), BF16),
            pltpu.VMEM((width, rows), BF16),
            pltpu.VMEM((width, cells), BF16),
            pltpu.VMEM((cells, rows), F32),
            pltpu.VMEM((cells, rows), F32),
            pltpu.VMEM((cells, rows), F32),
            pltpu.VMEM((rows, width), F32),
            pltpu.VMEM((rows, width), F32),
            pltpu.VMEM((2, 1, rows), F32),
            pltpu.VMEM((10, 1, rows), F32),
            pltpu.VMEM((4, rows // 4, half), BF16),
            pltpu.VMEM((3, rows // 4, half), BF16),
            pltpu.VMEM((4, 8, 16, half), BF16),
            pltpu.VMEM((3, 8, 16, half), BF16),
            pltpu.VMEM((8, 16, half), BF16),
            pltpu.VMEM((7, 16, half), BF16),
            pltpu.VMEM((8, 16, half), BF16),
            pltpu.VMEM((7, 16, half), BF16),
            pltpu.VMEM((4, part, cells // 2), BF16),
            pltpu.VMEM((4, part, cells // 2), BF16),
            pltpu.VMEM((2, part, cells // 2), BF16),
            pltpu.VMEM((2, part, cells // 2), BF16),
            pltpu.VMEM((2, part, cells // 2), F32),
            pltpu.VMEM((1, cells), F32),
            pltpu.VMEM((3, 1, cells), F32),
            dma((4,)),
            dma((4,)),
            dma((2, 3)),
            dma((2, 3)),
            dma((4,)),
            dma((4,)),
            dma((4,)),
            dma((2,)),
            dma((2,)),
            dma((2, 3)),
            pltpu.SemaphoreType.REGULAR,
        ],
        compiler_params=pltpu.CompilerParams(
            collective_id=0, has_side_effects=True, vmem_limit_bytes=24 * 1024 * 1024
        ),
    )(*[pltpu.with_memory_space_constraint(a, pltpu.MemorySpace.HBM) for a in (queries, centroids, beta.reshape(1, rows), teacher_ids.T)])
    query_grad, centroid_grad = pl.pallas_call(
        store_results,
        out_shape=[jax.ShapeDtypeStruct(a.shape, a.dtype) for a in results],
        in_specs=[pl.BlockSpec(memory_space=pltpu.VMEM)] * 2,
        out_specs=[pl.BlockSpec(memory_space=pltpu.MemorySpace.HBM)] * 2,
        scratch_shapes=[dma((2,))],
        compiler_params=pltpu.CompilerParams(vmem_limit_bytes=1024 * 1024),
    )(*results)
    return query_grad, centroid_grad.T


def solution(mesh):
    in_specs = (P("dp", None), P("cent", None), P("dp"), P("dp", None))
    out_specs = (P(("dp", "cent"), None), P("cent", "dp"))
    return jax.shard_map(local, mesh=mesh, in_specs=in_specs, out_specs=out_specs, check_vma=False)
```

```python
import functools

import jax
import jax.numpy as jnp
from jax import lax
from jax.experimental import pallas as pl
from jax.experimental.pallas import tpu as pltpu
from jax.sharding import PartitionSpec as P

EPS = 1e-06
SCALE = 1024.0
MESH = pl.DeviceIdType.MESH
F32 = jnp.float32
BF16 = jnp.bfloat16
NT = (((1,), (1,)), ((), ()))
TN = (((0,), (0,)), ((), ()))


def dot(a, b, dims):
    return lax.dot_general(a, b, dims, preferred_element_type=F32)


def join(own, others):
    top = jnp.maximum(jnp.max(others, axis=0), own)
    return top + jnp.log(jnp.sum(jnp.exp(others - top[None]), axis=0) + jnp.exp(own - top))


def kernel(
    q_hbm, c_hbm, beta_hbm, ids_hbm,
    qg_ref, cg_ref,
    q_v, c_v, beta_v, ids_v,
    qh_v, qht_v, ct_v, cos_v, e_v, d_v,
    w_v, lse_s, lse_r,
    ex_s, ex_r, ez_s, ez_r,
    tx_s, tx_r, tz_s, tz_r,
    bx_s, bx_r, bz_s, bz_r,
    core_s, core_r, y_s, y_r,
    near_v, row_s, row_r,
    in_sem, lse_sem, a_send, a_recv, b_sem, core_send, core_recv, y_send, y_recv, row_sem, ready_sem,
):
    rows, width = q_hbm.shape
    cells = c_hbm.shape[0]
    slots = ids_hbm.shape[0]
    half = width // 2
    part = width // 4
    dp = lax.axis_index("dp")
    cent = lax.axis_index("cent")
    x = cent // 8
    yhi = (cent // 4) % 2
    z = cent % 4
    core = dp % 2
    ylo = dp // 2

    loads = [
        pltpu.make_async_copy(src, dst, in_sem.at[i])
        for i, (src, dst) in enumerate(((q_hbm, q_v), (c_hbm, c_v), (beta_hbm, beta_v), (ids_hbm, ids_v)))
    ]
    for load in loads:
        load.start()

    barrier = pltpu.get_barrier_semaphore()

    for r in range(1, 4):
        pl.semaphore_signal(barrier, inc=1, device_id=(dp, (((x + r) % 4) * 2 + yhi) * 4 + z), device_id_type=MESH)
        pl.semaphore_signal(barrier, inc=1, device_id=(dp, (x * 2 + yhi) * 4 + (z + r) % 4), device_id_type=MESH)
        pl.semaphore_signal(barrier, inc=1, device_id=((dp + r) % 4, cent), device_id_type=MESH)
    pl.semaphore_signal(barrier, inc=1, device_id=(dp, (x * 2 + 1 - yhi) * 4 + z), device_id_type=MESH)

    loads[0].wait()
    for i in range(4):
        block = pl.ds(i * (rows // 4), rows // 4)
        qf = q_v[block, :].astype(F32)
        inv = 1.0 / jnp.sqrt(jnp.sum(qf * qf, axis=1, keepdims=True) + EPS)
        qh_v[block, :] = (qf * inv).astype(BF16)

    loads[1].wait()
    loads[2].wait()
    loads[3].wait()
    for i in range(2):
        lanes = pl.ds(i * (rows // 2), rows // 2)
        cosine = dot(c_v[...], qh_v[lanes, :], NT)
        cos_v[:, lanes] = cosine
        score = cosine * beta_v[:, lanes]
        top = jnp.max(score, axis=0, keepdims=True)
        expo = jnp.exp(score - top)
        total = jnp.sum(expo, axis=0, keepdims=True)
        lse_s[0, :, lanes] = top + jnp.log(total)
        e_v[:, lanes] = expo * (1.0 / total)

    pl.semaphore_wait(barrier, 10)
    pl.semaphore_signal(ready_sem, inc=1, device_id=(dp, (x * 2 + 1 - yhi) * 4 + z), device_id_type=MESH)

    def line_copy(r):
        return pltpu.make_async_remote_copy(
            src_ref=lse_s.at[0], dst_ref=lse_r.at[r - 1], send_sem=lse_sem.at[0], recv_sem=lse_sem.at[1],
            device_id=(dp, (((x + r) % 4) * 2 + yhi) * 4 + z), device_id_type=MESH,
        )

    def plane_copy(r):
        return pltpu.make_async_remote_copy(
            src_ref=lse_s.at[1], dst_ref=lse_r.at[r + 2], send_sem=lse_sem.at[2], recv_sem=lse_sem.at[3],
            device_id=(dp, (x * 2 + (yhi + r // 4) % 2) * 4 + (z + r) % 4), device_id_type=MESH,
        )

    def column_copy(r):
        return pltpu.make_async_remote_copy(
            src_ref=lse_s.at[0], dst_ref=lse_r.at[r + 9], send_sem=lse_sem.at[4], recv_sem=lse_sem.at[5],
            device_id=(dp, (x * 2 + yhi) * 4 + (z + r) % 4), device_id_type=MESH,
        )

    for r in (2, 1, 3):
        line_copy(r).start()
    for r in (2, 1, 3):
        column_copy(r).start()

    def x_copy(src, dst, kind, to, r):
        return pltpu.make_async_remote_copy(
            src_ref=src.at[to], dst_ref=dst.at[r - 1], send_sem=a_send.at[kind, r - 1], recv_sem=a_recv.at[kind, r - 1],
            device_id=(dp, (to * 2 + yhi) * 4 + z), device_id_type=MESH,
        )

    def z_copy(src, dst, kind, to, r):
        return pltpu.make_async_remote_copy(
            src_ref=src.at[to], dst_ref=dst.at[r - 1], send_sem=a_send.at[kind, r - 1], recv_sem=a_recv.at[kind, r - 1],
            device_id=(dp, (x * 2 + yhi) * 4 + to), device_id_type=MESH,
        )

    def send_blocks(targets, x_src, x_dst, z_src, z_dst, kind):
        for to in targets:

            @pl.when(to != x)
            def _():
                x_copy(x_src, x_dst, kind, to, (to + 4 - x) % 4).start()

            @pl.when(to != z)
            def _():
                z_copy(z_src, z_dst, kind + 1, to, (to + 4 - z) % 4).start()

    def put_blocks(i, g, x_src, z_src):
        x_src[2 * i : 2 * i + 2] = g[:, :half].reshape(2, 128, half)
        for k in range(16):
            z_src[k % 4, 4 * i + k // 4] = g[k * 16 : (k + 1) * 16, half:]

    for i in range(2):
        lanes = pl.ds(i * (rows // 2), rows // 2)
        put_blocks(i, dot(e_v[:, lanes].astype(BF16), c_v[...], TN).astype(BF16), ex_s, ez_s)
    send_blocks((0, 1), ex_s, ex_r, ez_s, ez_r, 0)

    ids = ids_v[...] - cent * cells
    position = lax.broadcasted_iota(jnp.int32, (256, rows), 0).astype(F32).astype(BF16)
    for h in range(cells // 256):
        here = ids - h * 256
        here = jnp.where((here >= 0) & (here < 256), here, -1).astype(F32)
        count = jnp.zeros((256, rows), BF16)
        for slot in range(slots):
            hit = jnp.broadcast_to(here[slot : slot + 1], (256, rows)).astype(BF16) == position
            count = count + jnp.where(hit, jnp.bfloat16(SCALE / slots), jnp.bfloat16(0.0))
        d_v[pl.ds(h * 256, 256), :] = count
    for i in range(2):
        lanes = pl.ds(i * (rows // 2), rows // 2)
        put_blocks(i, dot(d_v[:, lanes], c_v[...], TN).astype(BF16), tx_s, tz_s)
    send_blocks((0, 1), tx_s, tx_r, tz_s, tz_r, 2)
    send_blocks((2, 3), ex_s, ex_r, ez_s, ez_r, 0)
    send_blocks((2, 3), tx_s, tx_r, tz_s, tz_r, 2)

    line = pl.ds(0, 3)
    pltpu.make_async_copy(lse_r.at[line], lse_r.at[line], lse_sem.at[1]).wait()
    lse_s[1] = join(lse_s[0], lse_r[0:3])
    for r in (1, 2, 3, 4):
        plane_copy(r).start()
    pl.semaphore_wait(ready_sem, 1)
    for r in (5, 6, 7):
        plane_copy(r).start()

    qht_v[...] = qh_v[...].T
    ct_v[...] = c_v[...].T

    plane = pl.ds(3, 7)
    pltpu.make_async_copy(lse_r.at[plane], lse_r.at[plane], lse_sem.at[3]).wait()
    lse = join(lse_s[1], lse_r[3:10])
    column = pl.ds(10, 3)
    pltpu.make_async_copy(lse_r.at[column], lse_r.at[column], lse_sem.at[5]).wait()
    weight = jnp.exp(lse_s[0] - lse) * SCALE

    def grad_part(to, d):
        return dot(qht_v[pl.ds(pl.multiple_of(to * part, 64), part), :], d, NT)

    def core_copy(i):
        return pltpu.make_async_remote_copy(
            src_ref=core_s.at[i], dst_ref=core_r.at[i], send_sem=core_send.at[i], recv_sem=core_recv.at[i],
            device_id=(ylo * 2 + 1 - core, cent), device_id_type=MESH,
        )

    def y_copy(i):
        return pltpu.make_async_remote_copy(
            src_ref=y_s.at[i], dst_ref=y_r.at[i], send_sem=y_send.at[i], recv_sem=y_recv.at[i],
            device_id=((1 - ylo) * 2 + core, cent), device_id_type=MESH,
        )

    ds = []
    for i in range(2):
        block = pl.ds(i * (cells // 2), cells // 2)
        d = (e_v[block, :] * weight - d_v[block, :].astype(F32)).astype(BF16)
        ds.append(d)
        core_s[i] = grad_part((1 - ylo) * 2 + 1 - core, d).astype(BF16)
        core_copy(i).start()
    def bx_copy(to, r):
        return pltpu.make_async_remote_copy(
            src_ref=bx_s.at[to], dst_ref=bx_r.at[r - 1], send_sem=b_sem.at[0], recv_sem=b_sem.at[1],
            device_id=(dp, x * 8 + to), device_id_type=MESH,
        )

    def bz_copy(to, r):
        return pltpu.make_async_remote_copy(
            src_ref=bz_s.at[to], dst_ref=bz_r.at[r - 1], send_sem=b_sem.at[2], recv_sem=b_sem.at[3],
            device_id=(dp, to * 4 + z), device_id_type=MESH,
        )

    weights = [weight] + [jnp.exp(lse_r[r] - lse) * SCALE for r in (0, 1, 2, 10, 11, 12)] + [weight]
    w_v[...] = jnp.concatenate(weights, axis=0).T
    for r in range(1, 4):
        x_copy(ex_s, ex_r, 0, 0, r).wait()
        x_copy(tx_s, tx_r, 2, 0, r).wait()
    w = w_v[pl.ds(pl.multiple_of(x * 128, 128), 128), :]
    total = ex_s[x].astype(F32) * w[:, 0:1] - tx_s[x].astype(F32)
    for r in range(3):
        total = total + (ex_r[r].astype(F32) * w[:, r + 1 : r + 2] - tx_r[r].astype(F32))
    bx_s[...] = total.astype(BF16).reshape(8, 16, half)

    @pl.loop(0, 8)
    def _(to):
        @pl.when(to != yhi * 4 + z)
        def _():
            bx_copy(to, ((to // 4 + 2 - yhi) % 2) * 4 + (to + 4 - z) % 4).start()

    for r in range(1, 4):
        z_copy(ez_s, ez_r, 1, 0, r).wait()
        z_copy(tz_s, tz_r, 3, 0, r).wait()
    for g in range(8):
        w = w_v[pl.ds(pl.multiple_of(g * 64 + z * 16, 16), 16), :]
        total = ez_s[z, g].astype(F32) * w[:, 0:1] - tz_s[z, g].astype(F32)
        for r in range(3):
            total = total + (ez_r[r, g].astype(F32) * w[:, r + 4 : r + 5] - tz_r[r, g].astype(F32))
        bz_s[g] = total.astype(BF16)

    @pl.loop(0, 8)
    def _(to):
        @pl.when(to != x * 2 + yhi)
        def _():
            bz_copy(to, ((to + 2 - yhi) % 2) * 4 + (to // 2 + 4 - x) % 4).start()

    far = [grad_part((1 - ylo) * 2 + core, d) for d in ds]
    for i in range(2):
        core_copy(i).wait()
        y_s[i] = (far[i] + core_r[i].astype(F32)).astype(BF16)
        y_copy(i).start()
    for i in range(2):
        core_s[2 + i] = grad_part(ylo * 2 + 1 - core, ds[i]).astype(BF16)
        core_copy(2 + i).start()
    for i in range(2):
        near_v[i] = grad_part(dp, ds[i])

    for i in range(2):
        block = pl.ds(i * (cells // 2), cells // 2)
        prod = ds[i].astype(F32) * cos_v[block, :]
        prod = prod[:, 0:128] + prod[:, 128:256] + prod[:, 256:384] + prod[:, 384:512]
        row_s[:, block] = jnp.sum(prod.T, axis=0, keepdims=True)

    def row_copy(r):
        return pltpu.make_async_remote_copy(
            src_ref=row_s, dst_ref=row_r.at[r - 1], send_sem=row_sem.at[0, r - 1], recv_sem=row_sem.at[1, r - 1],
            device_id=((dp + r) % 4, cent), device_id_type=MESH,
        )

    for r in range(1, 4):
        row_copy(r).start()

    for r in range(1, 4):
        row_copy(r).wait()
    rowdot = row_s[...] + row_r[0] + row_r[1] + row_r[2]
    own_rows = pl.ds(pl.multiple_of(dp * part, 64), part)
    for i in range(2):
        block = pl.ds(i * (cells // 2), cells // 2)
        core_copy(2 + i).wait()
        y_copy(i).wait()
        grad = near_v[i] + core_r[2 + i].astype(F32) + y_r[i].astype(F32)
        here = slice(i * (cells // 2), (i + 1) * (cells // 2))
        cg_ref[:, block] = grad - rowdot[:, here] * ct_v[own_rows, block].astype(F32)

    mine = pl.ds(pl.multiple_of(cent * 16, 16), 16)
    qf = q_v[mine, :].astype(F32)
    norm = jnp.sqrt(jnp.sum(qf * qf, axis=1, keepdims=True) + EPS)
    hat = qh_v[mine, :].astype(F32)
    pltpu.make_async_copy(bx_r, bx_r, b_sem.at[1]).wait()
    left = bx_s[yhi * 4 + z].astype(F32) + jnp.sum(bx_r[...].astype(F32), axis=0)
    pltpu.make_async_copy(bz_r, bz_r, b_sem.at[3]).wait()
    right = bz_s[x * 2 + yhi].astype(F32) + jnp.sum(bz_r[...].astype(F32), axis=0)
    grad = jnp.concatenate([left, right], axis=1)
    along = jnp.sum(grad * hat, axis=1, keepdims=True)
    qg_ref[...] = (grad - along * hat) / norm

    pltpu.make_async_copy(lse_r.at[column], lse_r.at[column], lse_sem.at[4]).wait()
    pltpu.make_async_copy(lse_r.at[line], lse_r.at[line], lse_sem.at[0]).wait()
    pltpu.make_async_copy(lse_r.at[plane], lse_r.at[plane], lse_sem.at[2]).wait()
    pltpu.make_async_copy(bx_r, bx_r, b_sem.at[0]).wait()
    pltpu.make_async_copy(bz_r, bz_r, b_sem.at[2]).wait()


def store_results(qg_v, cg_v, qg_hbm, cg_hbm, sem):
    copies = [pltpu.make_async_copy(cg_v, cg_hbm, sem.at[0]), pltpu.make_async_copy(qg_v, qg_hbm, sem.at[1])]
    for copy in copies:
        copy.start()
    for copy in copies:
        copy.wait()


def local(queries, centroids, beta, teacher_ids):
    rows, width = queries.shape
    cells = centroids.shape[0]
    slots = teacher_ids.shape[1]
    half, part = width // 2, width // 4
    dma = pltpu.SemaphoreType.DMA
    results = pl.pallas_call(
        kernel,
        out_shape=(
            jax.ShapeDtypeStruct((rows // 32, width), F32),
            jax.ShapeDtypeStruct((part, cells), F32),
        ),
        in_specs=[pl.BlockSpec(memory_space=pltpu.MemorySpace.HBM)] * 4,
        out_specs=[pl.BlockSpec(memory_space=pltpu.VMEM)] * 2,
        scratch_shapes=[
            pltpu.VMEM((rows, width), BF16),
            pltpu.VMEM((cells, width), BF16),
            pltpu.VMEM((1, rows), F32),
            pltpu.VMEM((slots, rows), jnp.int32),
            pltpu.VMEM((rows, width), BF16),
            pltpu.VMEM((width, rows), BF16),
            pltpu.VMEM((width, cells), BF16),
            pltpu.VMEM((cells, rows), F32),
            pltpu.VMEM((cells, rows), F32),
            pltpu.VMEM((cells, rows), BF16),
            pltpu.VMEM((rows, 8), F32),
            pltpu.VMEM((2, 1, rows), F32),
            pltpu.VMEM((13, 1, rows), F32),
            pltpu.VMEM((4, rows // 4, half), BF16),
            pltpu.VMEM((3, rows // 4, half), BF16),
            pltpu.VMEM((4, 8, 16, half), BF16),
            pltpu.VMEM((3, 8, 16, half), BF16),
            pltpu.VMEM((4, rows // 4, half), BF16),
            pltpu.VMEM((3, rows // 4, half), BF16),
            pltpu.VMEM((4, 8, 16, half), BF16),
            pltpu.VMEM((3, 8, 16, half), BF16),
            pltpu.VMEM((8, 16, half), BF16),
            pltpu.VMEM((7, 16, half), BF16),
            pltpu.VMEM((8, 16, half), BF16),
            pltpu.VMEM((7, 16, half), BF16),
            pltpu.VMEM((4, part, cells // 2), BF16),
            pltpu.VMEM((4, part, cells // 2), BF16),
            pltpu.VMEM((2, part, cells // 2), BF16),
            pltpu.VMEM((2, part, cells // 2), BF16),
            pltpu.VMEM((2, part, cells // 2), F32),
            pltpu.VMEM((1, cells), F32),
            pltpu.VMEM((3, 1, cells), F32),
            dma((4,)),
            dma((6,)),
            dma((4, 3)),
            dma((4, 3)),
            dma((4,)),
            dma((4,)),
            dma((4,)),
            dma((2,)),
            dma((2,)),
            dma((2, 3)),
            pltpu.SemaphoreType.REGULAR,
        ],
        compiler_params=pltpu.CompilerParams(
            collective_id=0, has_side_effects=True, vmem_limit_bytes=24 * 1024 * 1024
        ),
    )(*[pltpu.with_memory_space_constraint(a, pltpu.MemorySpace.HBM) for a in (queries, centroids, beta.reshape(1, rows), teacher_ids.T)])
    query_grad, centroid_grad = pl.pallas_call(
        store_results,
        out_shape=[jax.ShapeDtypeStruct(a.shape, a.dtype) for a in results],
        in_specs=[pl.BlockSpec(memory_space=pltpu.VMEM)] * 2,
        out_specs=[pl.BlockSpec(memory_space=pltpu.MemorySpace.HBM)] * 2,
        scratch_shapes=[dma((2,))],
        compiler_params=pltpu.CompilerParams(vmem_limit_bytes=1024 * 1024),
    )(*results)
    return query_grad, centroid_grad.T


def solution(mesh):
    in_specs = (P("dp", None), P("cent", None), P("dp"), P("dp", None))
    out_specs = (P(("dp", "cent"), None), P("cent", "dp"))
    return jax.shard_map(local, mesh=mesh, in_specs=in_specs, out_specs=out_specs, check_vma=False)
```

```python
import functools

import jax
import jax.numpy as jnp
from jax import lax
from jax.experimental import pallas as pl
from jax.experimental.pallas import tpu as pltpu
from jax.sharding import PartitionSpec as P

EPS = 1e-06
SCALE = 1024.0
MESH = pl.DeviceIdType.MESH
F32 = jnp.float32
BF16 = jnp.bfloat16
NT = (((1,), (1,)), ((), ()))
TN = (((0,), (0,)), ((), ()))


def dot(a, b, dims):
    return lax.dot_general(a, b, dims, preferred_element_type=F32)


def join(own, others):
    top = jnp.maximum(jnp.max(others, axis=0), own)
    return top + jnp.log(jnp.sum(jnp.exp(others - top[None]), axis=0) + jnp.exp(own - top))


def kernel(
    q_hbm, c_hbm, beta_hbm, ids_hbm,
    qg_ref, cg_ref,
    q_v, c_v, beta_v, ids_v,
    qh_v, qht_v, ct_v, cos_v, e_v, d_v,
    es_v, ts_v,
    lse_v, lse_s, lse_r, early_r,
    gx_s, gx_r, gz_s, gz_r,
    bx_s, bx_r, bz_s, bz_r,
    core_s, core_r, y_s, y_r,
    near_v, row_s, row_r,
    in_sem, lse_sem, a_send, a_recv, b_sem, core_send, core_recv, y_send, y_recv, row_sem, ready_sem,
):
    rows, width = q_hbm.shape
    cells = c_hbm.shape[0]
    slots = ids_hbm.shape[0]
    half = width // 2
    part = width // 4
    dp = lax.axis_index("dp")
    cent = lax.axis_index("cent")
    x = cent // 8
    yhi = (cent // 4) % 2
    z = cent % 4
    core = dp % 2
    ylo = dp // 2

    loads = [
        pltpu.make_async_copy(src, dst, in_sem.at[i])
        for i, (src, dst) in enumerate(((q_hbm, q_v), (c_hbm, c_v), (beta_hbm, beta_v), (ids_hbm, ids_v)))
    ]
    for load in loads:
        load.start()

    barrier = pltpu.get_barrier_semaphore()

    for r in range(1, 4):
        pl.semaphore_signal(barrier, inc=1, device_id=(dp, (((x + r) % 4) * 2 + yhi) * 4 + z), device_id_type=MESH)
        pl.semaphore_signal(barrier, inc=1, device_id=(dp, (x * 2 + yhi) * 4 + (z + r) % 4), device_id_type=MESH)
        pl.semaphore_signal(barrier, inc=1, device_id=((dp + r) % 4, cent), device_id_type=MESH)
    pl.semaphore_signal(barrier, inc=1, device_id=(dp, (x * 2 + 1 - yhi) * 4 + z), device_id_type=MESH)

    early = ((yhi == 0) & (x < 2)) & (z < 2)

    @pl.when(early)
    def _():
        @pl.loop(1, 32)
        def _(r):
            pl.semaphore_signal(barrier, inc=1, device_id=(dp, (cent + r) % 32), device_id_type=MESH)

    loads[0].wait()
    for i in range(4):
        block = pl.ds(i * (rows // 4), rows // 4)
        qf = q_v[block, :].astype(F32)
        inv = 1.0 / jnp.sqrt(jnp.sum(qf * qf, axis=1, keepdims=True) + EPS)
        qh_v[block, :] = (qf * inv).astype(BF16)

    loads[1].wait()
    loads[2].wait()
    loads[3].wait()
    for i in range(2):
        lanes = pl.ds(i * (rows // 2), rows // 2)
        cosine = dot(c_v[...], qh_v[lanes, :], NT)
        cos_v[:, lanes] = cosine
        score = cosine * beta_v[:, lanes]
        top = jnp.max(score, axis=0, keepdims=True)
        expo = jnp.exp(score - top)
        total = jnp.sum(expo, axis=0, keepdims=True)
        lse_s[0, :, lanes] = top + jnp.log(total)
        e_v[:, lanes] = expo * (1.0 / total)

    @pl.when(early)
    def _():
        pl.semaphore_wait(barrier, 13)

    @pl.when(jnp.logical_not(early))
    def _():
        pl.semaphore_wait(barrier, 14)

    pl.semaphore_signal(ready_sem, inc=1, device_id=(dp, (x * 2 + 1 - yhi) * 4 + z), device_id_type=MESH)

    def line_copy(r):
        return pltpu.make_async_remote_copy(
            src_ref=lse_s.at[0], dst_ref=lse_r.at[r - 1], send_sem=lse_sem.at[0], recv_sem=lse_sem.at[1],
            device_id=(dp, (((x + r) % 4) * 2 + yhi) * 4 + z), device_id_type=MESH,
        )

    def plane_copy(r):
        return pltpu.make_async_remote_copy(
            src_ref=lse_s.at[1], dst_ref=lse_r.at[r + 2], send_sem=lse_sem.at[2], recv_sem=lse_sem.at[3],
            device_id=(dp, (x * 2 + (yhi + r // 4) % 2) * 4 + (z + r) % 4), device_id_type=MESH,
        )

    def early_copy(to):
        return pltpu.make_async_remote_copy(
            src_ref=lse_s.at[0], dst_ref=early_r.at[(cent + 31 - to) % 32], send_sem=lse_sem.at[4], recv_sem=lse_sem.at[5],
            device_id=(dp, to), device_id_type=MESH,
        )

    for to in (0, 1, 8, 9):

        @pl.when(to != cent)
        def _():
            early_copy(to).start()

    for r in (2, 1, 3):
        line_copy(r).start()

    for i in range(2):
        lanes = pl.ds(i * (rows // 2), rows // 2)
        es_v[lanes, :] = dot(e_v[:, lanes].astype(BF16), c_v[...], TN)
    ids = ids_v[...] - cent * cells
    position = lax.broadcasted_iota(jnp.int32, (256, rows), 0).astype(F32).astype(BF16)
    for h in range(cells // 256):
        here = ids - h * 256
        here = jnp.where((here >= 0) & (here < 256), here, -1).astype(F32)
        count = jnp.zeros((256, rows), BF16)
        for slot in range(slots):
            hit = jnp.broadcast_to(here[slot : slot + 1], (256, rows)).astype(BF16) == position
            count = count + jnp.where(hit, jnp.bfloat16(SCALE / slots), jnp.bfloat16(0.0))
        d_v[pl.ds(h * 256, 256), :] = count
    for i in range(2):
        lanes = pl.ds(i * (rows // 2), rows // 2)
        ts_v[lanes, :] = dot(d_v[:, lanes], c_v[...], TN)
    qht_v[...] = qh_v[...].T
    ct_v[...] = c_v[...].T

    line = pl.ds(0, 3)
    pltpu.make_async_copy(lse_r.at[line], lse_r.at[line], lse_sem.at[1]).wait()
    lse_s[1] = join(lse_s[0], lse_r[0:3])
    for r in (1, 2, 3, 4):
        plane_copy(r).start()
    pl.semaphore_wait(ready_sem, 1)
    for r in (5, 6, 7):
        plane_copy(r).start()

    plane = pl.ds(3, 7)

    @pl.when(early)
    def _():
        pltpu.make_async_copy(early_r, early_r, lse_sem.at[5]).wait()
        lse_v[...] = join(lse_s[0], early_r[...])

    @pl.when(jnp.logical_not(early))
    def _():
        pltpu.make_async_copy(lse_r.at[plane], lse_r.at[plane], lse_sem.at[3]).wait()
        lse_v[...] = join(lse_s[1], lse_r[3:10])

    weight = jnp.exp(lse_s[0] - lse_v[...]) * SCALE
    weight_col = jnp.broadcast_to(weight, (128, rows)).T

    for i in range(rows // 128):
        block = pl.ds(i * 128, 128)
        for j in range(3):
            cols = pl.ds(j * 128, 128)
            gx_s[i, :, cols] = (es_v[block, cols] * weight_col[i * 128 : (i + 1) * 128] - ts_v[block, cols]).astype(BF16)
        for j in range(3):
            cols = pl.ds(half + j * 128, 128)
            g = (es_v[block, cols] * weight_col[i * 128 : (i + 1) * 128] - ts_v[block, cols]).astype(BF16)
            for k in range(8):
                gz_s[k % 4, 2 * i + k // 4, :, pl.ds(j * 128, 128)] = g[k * 16 : (k + 1) * 16]

    def x_copy(to, r):
        return pltpu.make_async_remote_copy(
            src_ref=gx_s.at[to], dst_ref=gx_r.at[r - 1], send_sem=a_send.at[0, r - 1], recv_sem=a_recv.at[0, r - 1],
            device_id=(dp, (to * 2 + yhi) * 4 + z), device_id_type=MESH,
        )

    def z_copy(to, r):
        return pltpu.make_async_remote_copy(
            src_ref=gz_s.at[to], dst_ref=gz_r.at[r - 1], send_sem=a_send.at[1, r - 1], recv_sem=a_recv.at[1, r - 1],
            device_id=(dp, (x * 2 + yhi) * 4 + to), device_id_type=MESH,
        )

    for to in range(4):

        @pl.when(to != x)
        def _():
            x_copy(to, (to + 4 - x) % 4).start()

        @pl.when(to != z)
        def _():
            z_copy(to, (to + 4 - z) % 4).start()

    def grad_part(to, d):
        return dot(qht_v[pl.ds(pl.multiple_of(to * part, 64), part), :], d, NT)

    def core_copy(i):
        return pltpu.make_async_remote_copy(
            src_ref=core_s.at[i], dst_ref=core_r.at[i], send_sem=core_send.at[i], recv_sem=core_recv.at[i],
            device_id=(ylo * 2 + 1 - core, cent), device_id_type=MESH,
        )

    def y_copy(i):
        return pltpu.make_async_remote_copy(
            src_ref=y_s.at[i], dst_ref=y_r.at[i], send_sem=y_send.at[i], recv_sem=y_recv.at[i],
            device_id=((1 - ylo) * 2 + core, cent), device_id_type=MESH,
        )

    ds = []
    for i in range(2):
        block = pl.ds(i * (cells // 2), cells // 2)
        d = (e_v[block, :] * weight - d_v[block, :].astype(F32)).astype(BF16)
        ds.append(d)
        core_s[i] = grad_part((1 - ylo) * 2 + 1 - core, d).astype(BF16)
        core_copy(i).start()
    for i in range(2):
        near_v[i] = grad_part((1 - ylo) * 2 + core, ds[i])
    for i in range(2):
        core_copy(i).wait()
        y_s[i] = (near_v[i] + core_r[i].astype(F32)).astype(BF16)
        y_copy(i).start()
    for i in range(2):
        core_s[2 + i] = grad_part(ylo * 2 + 1 - core, ds[i]).astype(BF16)
        core_copy(2 + i).start()
    for i in range(2):
        near_v[i] = grad_part(dp, ds[i])

    for i in range(2):
        block = pl.ds(i * (cells // 2), cells // 2)
        prod = ds[i].astype(F32) * cos_v[block, :]
        prod = prod[:, 0:128] + prod[:, 128:256] + prod[:, 256:384] + prod[:, 384:512]
        row_s[:, block] = jnp.sum(prod.T, axis=0, keepdims=True)

    def row_copy(r):
        return pltpu.make_async_remote_copy(
            src_ref=row_s, dst_ref=row_r.at[r - 1], send_sem=row_sem.at[0, r - 1], recv_sem=row_sem.at[1, r - 1],
            device_id=((dp + r) % 4, cent), device_id_type=MESH,
        )

    for r in range(1, 4):
        row_copy(r).start()

    def bx_copy(to, r):
        return pltpu.make_async_remote_copy(
            src_ref=bx_s.at[to], dst_ref=bx_r.at[r - 1], send_sem=b_sem.at[0], recv_sem=b_sem.at[1],
            device_id=(dp, x * 8 + to), device_id_type=MESH,
        )

    def bz_copy(to, r):
        return pltpu.make_async_remote_copy(
            src_ref=bz_s.at[to], dst_ref=bz_r.at[r - 1], send_sem=b_sem.at[2], recv_sem=b_sem.at[3],
            device_id=(dp, to * 4 + z), device_id_type=MESH,
        )

    for r in range(1, 4):
        x_copy(0, r).wait()
    total = gx_s[x].astype(F32)
    for r in range(3):
        total = total + gx_r[r].astype(F32)
    bx_s[...] = total.astype(BF16).reshape(8, 16, half)

    @pl.loop(0, 8)
    def _(to):
        @pl.when(to != yhi * 4 + z)
        def _():
            bx_copy(to, ((to // 4 + 2 - yhi) % 2) * 4 + (to + 4 - z) % 4).start()

    for r in range(1, 4):
        z_copy(0, r).wait()
    total = gz_s[z].astype(F32)
    for r in range(3):
        total = total + gz_r[r].astype(F32)
    bz_s[...] = total.astype(BF16)

    @pl.loop(0, 8)
    def _(to):
        @pl.when(to != x * 2 + yhi)
        def _():
            bz_copy(to, ((to + 2 - yhi) % 2) * 4 + (to // 2 + 4 - x) % 4).start()

    for r in range(1, 4):
        row_copy(r).wait()
    rowdot = row_s[...] + row_r[0] + row_r[1] + row_r[2]
    own_rows = pl.ds(pl.multiple_of(dp * part, 64), part)
    for i in range(2):
        block = pl.ds(i * (cells // 2), cells // 2)
        core_copy(2 + i).wait()
        y_copy(i).wait()
        grad = near_v[i] + core_r[2 + i].astype(F32) + y_r[i].astype(F32)
        here = slice(i * (cells // 2), (i + 1) * (cells // 2))
        cg_ref[:, block] = grad - rowdot[:, here] * ct_v[own_rows, block].astype(F32)

    mine = pl.ds(pl.multiple_of(cent * 16, 16), 16)
    qf = q_v[mine, :].astype(F32)
    norm = jnp.sqrt(jnp.sum(qf * qf, axis=1, keepdims=True) + EPS)
    hat = qh_v[mine, :].astype(F32)
    pltpu.make_async_copy(bx_r, bx_r, b_sem.at[1]).wait()
    left = bx_s[yhi * 4 + z].astype(F32) + jnp.sum(bx_r[...].astype(F32), axis=0)
    pltpu.make_async_copy(bz_r, bz_r, b_sem.at[3]).wait()
    right = bz_s[x * 2 + yhi].astype(F32) + jnp.sum(bz_r[...].astype(F32), axis=0)
    grad = jnp.concatenate([left, right], axis=1)
    along = jnp.sum(grad * hat, axis=1, keepdims=True)
    qg_ref[...] = (grad - along * hat) / norm

    pltpu.make_async_copy(lse_r.at[line], lse_r.at[line], lse_sem.at[0]).wait()
    pltpu.make_async_copy(lse_r.at[plane], lse_r.at[plane], lse_sem.at[2]).wait()

    @pl.when(early)
    def _():
        three = pl.ds(0, 3)
        pltpu.make_async_copy(early_r.at[three], early_r.at[three], lse_sem.at[4]).wait()
        pltpu.make_async_copy(lse_r.at[plane], lse_r.at[plane], lse_sem.at[3]).wait()

    @pl.when(jnp.logical_not(early))
    def _():
        four = pl.ds(0, 4)
        pltpu.make_async_copy(early_r.at[four], early_r.at[four], lse_sem.at[4]).wait()

    pltpu.make_async_copy(bx_r, bx_r, b_sem.at[0]).wait()
    pltpu.make_async_copy(bz_r, bz_r, b_sem.at[2]).wait()


def store_results(qg_v, cg_v, qg_hbm, cg_hbm, sem):
    copies = [pltpu.make_async_copy(cg_v, cg_hbm, sem.at[0]), pltpu.make_async_copy(qg_v, qg_hbm, sem.at[1])]
    for copy in copies:
        copy.start()
    for copy in copies:
        copy.wait()


def local(queries, centroids, beta, teacher_ids):
    rows, width = queries.shape
    cells = centroids.shape[0]
    slots = teacher_ids.shape[1]
    half, part = width // 2, width // 4
    dma = pltpu.SemaphoreType.DMA
    results = pl.pallas_call(
        kernel,
        out_shape=(
            jax.ShapeDtypeStruct((rows // 32, width), F32),
            jax.ShapeDtypeStruct((part, cells), F32),
        ),
        in_specs=[pl.BlockSpec(memory_space=pltpu.MemorySpace.HBM)] * 4,
        out_specs=[pl.BlockSpec(memory_space=pltpu.VMEM)] * 2,
        scratch_shapes=[
            pltpu.VMEM((rows, width), BF16),
            pltpu.VMEM((cells, width), BF16),
            pltpu.VMEM((1, rows), F32),
            pltpu.VMEM((slots, rows), jnp.int32),
            pltpu.VMEM((rows, width), BF16),
            pltpu.VMEM((width, rows), BF16),
            pltpu.VMEM((width, cells), BF16),
            pltpu.VMEM((cells, rows), F32),
            pltpu.VMEM((cells, rows), F32),
            pltpu.VMEM((cells, rows), BF16),
            pltpu.VMEM((rows, width), F32),
            pltpu.VMEM((rows, width), F32),
            pltpu.VMEM((1, rows), F32),
            pltpu.VMEM((2, 1, rows), F32),
            pltpu.VMEM((10, 1, rows), F32),
            pltpu.VMEM((31, 1, rows), F32),
            pltpu.VMEM((4, rows // 4, half), BF16),
            pltpu.VMEM((3, rows // 4, half), BF16),
            pltpu.VMEM((4, 8, 16, half), BF16),
            pltpu.VMEM((3, 8, 16, half), BF16),
            pltpu.VMEM((8, 16, half), BF16),
            pltpu.VMEM((7, 16, half), BF16),
            pltpu.VMEM((8, 16, half), BF16),
            pltpu.VMEM((7, 16, half), BF16),
            pltpu.VMEM((4, part, cells // 2), BF16),
            pltpu.VMEM((4, part, cells // 2), BF16),
            pltpu.VMEM((2, part, cells // 2), BF16),
            pltpu.VMEM((2, part, cells // 2), BF16),
            pltpu.VMEM((2, part, cells // 2), F32),
            pltpu.VMEM((1, cells), F32),
            pltpu.VMEM((3, 1, cells), F32),
            dma((4,)),
            dma((6,)),
            dma((2, 3)),
            dma((2, 3)),
            dma((4,)),
            dma((4,)),
            dma((4,)),
            dma((2,)),
            dma((2,)),
            dma((2, 3)),
            pltpu.SemaphoreType.REGULAR,
        ],
        compiler_params=pltpu.CompilerParams(
            collective_id=0, has_side_effects=True, vmem_limit_bytes=24 * 1024 * 1024
        ),
    )(*[pltpu.with_memory_space_constraint(a, pltpu.MemorySpace.HBM) for a in (queries, centroids, beta.reshape(1, rows), teacher_ids.T)])
    query_grad, centroid_grad = pl.pallas_call(
        store_results,
        out_shape=[jax.ShapeDtypeStruct(a.shape, a.dtype) for a in results],
        in_specs=[pl.BlockSpec(memory_space=pltpu.VMEM)] * 2,
        out_specs=[pl.BlockSpec(memory_space=pltpu.MemorySpace.HBM)] * 2,
        scratch_shapes=[dma((2,))],
        compiler_params=pltpu.CompilerParams(vmem_limit_bytes=1024 * 1024),
    )(*results)
    return query_grad, centroid_grad.T


def solution(mesh):
    in_specs = (P("dp", None), P("cent", None), P("dp"), P("dp", None))
    out_specs = (P(("dp", "cent"), None), P("cent", "dp"))
    return jax.shard_map(local, mesh=mesh, in_specs=in_specs, out_specs=out_specs, check_vma=False)
```

```python
import functools

import jax
import jax.numpy as jnp
from jax import lax
from jax.experimental import pallas as pl
from jax.experimental.pallas import tpu as pltpu
from jax.sharding import PartitionSpec as P

EPS = 1e-06
SCALE = 1024.0
LOWEST = -1e30
MESH = pl.DeviceIdType.MESH
F32 = jnp.float32
BF16 = jnp.bfloat16
NT = (((1,), (1,)), ((), ()))
TN = (((0,), (0,)), ((), ()))


def dot(a, b, dims):
    return lax.dot_general(a, b, dims, preferred_element_type=F32)


def join(parts):
    top = jnp.max(parts, axis=0)
    return top + jnp.log(jnp.sum(jnp.exp(parts - top[None]), axis=0))


def kernel(
    q_hbm, c_hbm, beta_hbm, ids_hbm,
    qg_ref, cg_ref,
    q_v, c_v, beta_v, ids_v,
    qh_v, qht_v, ct_v, cos_v, e_v, d_v,
    es_v, ts_v,
    lse_v, lse_s, stat_v, spare_v,
    gx_s, gx_r, gz_s, gz_r,
    bx_s, bx_r, bz_s, bz_r,
    core_s, core_r, y_s, y_r,
    near_v, row_s, row_r,
    in_sem, lse_send, lse_recv, a_send, a_recv, b_sem, core_send, core_recv, y_send, y_recv, row_sem, ready_sem,
):
    rows, width = q_hbm.shape
    cells = c_hbm.shape[0]
    slots = ids_hbm.shape[0]
    half = width // 2
    part = width // 4
    dp = lax.axis_index("dp")
    cent = lax.axis_index("cent")
    x = cent // 8
    yhi = (cent // 4) % 2
    z = cent % 4
    core = dp % 2
    ylo = dp // 2

    loads = [
        pltpu.make_async_copy(src, dst, in_sem.at[i])
        for i, (src, dst) in enumerate(((q_hbm, q_v), (c_hbm, c_v), (beta_hbm, beta_v), (ids_hbm, ids_v)))
    ]
    for load in loads:
        load.start()

    barrier = pltpu.get_barrier_semaphore()

    for r in range(1, 4):
        pl.semaphore_signal(barrier, inc=1, device_id=(dp, (((x + r) % 4) * 2 + yhi) * 4 + z), device_id_type=MESH)
        pl.semaphore_signal(barrier, inc=1, device_id=(dp, (x * 2 + yhi) * 4 + (z + r) % 4), device_id_type=MESH)
        pl.semaphore_signal(barrier, inc=1, device_id=((dp + r) % 4, cent), device_id_type=MESH)
    pl.semaphore_signal(barrier, inc=1, device_id=(dp, (x * 2 + 1 - yhi) * 4 + z), device_id_type=MESH)

    def start_time(line_yhi, line_z):
        return 27 * line_yhi + 11 * line_z + 2 * (line_z // 2)

    now = start_time(yhi, z)
    lines = [(i, start_time(i // 4, i % 4)) for i in range(8)]
    own_line = yhi * 4 + z
    earlier_lines = sum([jnp.where(time < now, 1, 0) for _, time in lines])
    for i, time in lines:

        @pl.when(time > now)
        def _():
            for to in range(4):
                pl.semaphore_signal(barrier, inc=1, device_id=(dp, to * 8 + i), device_id_type=MESH)

        @pl.when(time < now)
        def _():
            stat_v[i, 1:4] = jnp.full((3, 1, rows), LOWEST, F32)

    loads[0].wait()
    for i in range(4):
        block = pl.ds(i * (rows // 4), rows // 4)
        qf = q_v[block, :].astype(F32)
        inv = 1.0 / jnp.sqrt(jnp.sum(qf * qf, axis=1, keepdims=True) + EPS)
        qh_v[block, :] = (qf * inv).astype(BF16)

    loads[1].wait()
    loads[2].wait()
    loads[3].wait()
    for i in range(2):
        lanes = pl.ds(i * (rows // 2), rows // 2)
        cosine = dot(c_v[...], qh_v[lanes, :], NT)
        cos_v[:, lanes] = cosine
        score = cosine * beta_v[:, lanes]
        top = jnp.max(score, axis=0, keepdims=True)
        expo = jnp.exp(score - top)
        total = jnp.sum(expo, axis=0, keepdims=True)
        lse_s[0, :, lanes] = top + jnp.log(total)
        stat_v[own_line, x, :, lanes] = top + jnp.log(total)
        e_v[:, lanes] = expo * (1.0 / total)

    pl.semaphore_wait(barrier, 10 + 4 * earlier_lines)
    pl.semaphore_signal(ready_sem, inc=1, device_id=(dp, (x * 2 + 1 - yhi) * 4 + z), device_id_type=MESH)

    def line_copy(r):
        return pltpu.make_async_remote_copy(
            src_ref=lse_s.at[0], dst_ref=stat_v.at[own_line, x], send_sem=lse_send.at[8], recv_sem=lse_recv.at[8],
            device_id=(dp, ((x + r) % 4) * 8 + own_line), device_id_type=MESH,
        )

    def early_copy(i, to):
        return pltpu.make_async_remote_copy(
            src_ref=lse_s.at[0], dst_ref=stat_v.at[own_line, x], send_sem=lse_send.at[i], recv_sem=lse_recv.at[own_line],
            device_id=(dp, to * 8 + i), device_id_type=MESH,
        )

    def late_copy(i):
        return pltpu.make_async_remote_copy(
            src_ref=lse_s.at[1], dst_ref=stat_v.at[own_line, 0], send_sem=lse_send.at[i], recv_sem=lse_recv.at[own_line],
            device_id=(dp, x * 8 + i), device_id_type=MESH,
        )

    for r in (2, 1, 3):
        line_copy(r).start()
    for i, time in lines:

        @pl.when(time < now)
        def _():
            for to in range(4):
                early_copy(i, to).start()

    for i in range(2):
        lanes = pl.ds(i * (rows // 2), rows // 2)
        es_v[lanes, :] = dot(e_v[:, lanes].astype(BF16), c_v[...], TN)
    ids = ids_v[...] - cent * cells
    position = lax.broadcasted_iota(jnp.int32, (256, rows), 0).astype(F32).astype(BF16)
    for h in range(cells // 256):
        here = ids - h * 256
        here = jnp.where((here >= 0) & (here < 256), here, -1).astype(F32)
        count = jnp.zeros((256, rows), BF16)
        for slot in range(slots):
            hit = jnp.broadcast_to(here[slot : slot + 1], (256, rows)).astype(BF16) == position
            count = count + jnp.where(hit, jnp.bfloat16(SCALE / slots), jnp.bfloat16(0.0))
        d_v[pl.ds(h * 256, 256), :] = count
    for i in range(2):
        lanes = pl.ds(i * (rows // 2), rows // 2)
        ts_v[lanes, :] = dot(d_v[:, lanes], c_v[...], TN)
    qht_v[...] = qh_v[...].T
    ct_v[...] = c_v[...].T

    three = spare_v.at[pl.ds(0, 3)]
    pltpu.make_async_copy(three, three, lse_recv.at[8]).wait()
    lse_s[1] = join(stat_v[own_line])
    pl.semaphore_wait(ready_sem, 1)
    for i, time in lines:

        @pl.when(time > now)
        def _():
            late_copy(i).start()

    for i, time in lines:

        @pl.when(time > now)
        def _():
            pltpu.make_async_copy(spare_v, spare_v, lse_recv.at[i]).wait()

        @pl.when(time < now)
        def _():
            pltpu.make_async_copy(spare_v.at[0], spare_v.at[0], lse_recv.at[i]).wait()

    lse_v[...] = join(stat_v[...].reshape(32, 1, rows))
    weight = jnp.exp(lse_s[0] - lse_v[...]) * SCALE
    weight_col = jnp.broadcast_to(weight, (128, rows)).T

    for i in range(rows // 128):
        block = pl.ds(i * 128, 128)
        for j in range(3):
            cols = pl.ds(j * 128, 128)
            gx_s[i, :, cols] = (es_v[block, cols] * weight_col[i * 128 : (i + 1) * 128] - ts_v[block, cols]).astype(BF16)
        for j in range(3):
            cols = pl.ds(half + j * 128, 128)
            g = (es_v[block, cols] * weight_col[i * 128 : (i + 1) * 128] - ts_v[block, cols]).astype(BF16)
            for k in range(8):
                gz_s[k % 4, 2 * i + k // 4, :, pl.ds(j * 128, 128)] = g[k * 16 : (k + 1) * 16]

    def x_copy(to, r):
        return pltpu.make_async_remote_copy(
            src_ref=gx_s.at[to], dst_ref=gx_r.at[r - 1], send_sem=a_send.at[0, r - 1], recv_sem=a_recv.at[0, r - 1],
            device_id=(dp, (to * 2 + yhi) * 4 + z), device_id_type=MESH,
        )

    def z_copy(to, r):
        return pltpu.make_async_remote_copy(
            src_ref=gz_s.at[to], dst_ref=gz_r.at[r - 1], send_sem=a_send.at[1, r - 1], recv_sem=a_recv.at[1, r - 1],
            device_id=(dp, (x * 2 + yhi) * 4 + to), device_id_type=MESH,
        )

    for to in range(4):

        @pl.when(to != x)
        def _():
            x_copy(to, (to + 4 - x) % 4).start()

        @pl.when(to != z)
        def _():
            z_copy(to, (to + 4 - z) % 4).start()

    def grad_part(to, d):
        return dot(qht_v[pl.ds(pl.multiple_of(to * part, 64), part), :], d, NT)

    def core_copy(i):
        return pltpu.make_async_remote_copy(
            src_ref=core_s.at[i], dst_ref=core_r.at[i], send_sem=core_send.at[i], recv_sem=core_recv.at[i],
            device_id=(ylo * 2 + 1 - core, cent), device_id_type=MESH,
        )

    def y_copy(i):
        return pltpu.make_async_remote_copy(
            src_ref=y_s.at[i], dst_ref=y_r.at[i], send_sem=y_send.at[i], recv_sem=y_recv.at[i],
            device_id=((1 - ylo) * 2 + core, cent), device_id_type=MESH,
        )

    ds = []
    for i in range(2):
        block = pl.ds(i * (cells // 2), cells // 2)
        d = (e_v[block, :] * weight - d_v[block, :].astype(F32)).astype(BF16)
        ds.append(d)
        core_s[i] = grad_part((1 - ylo) * 2 + 1 - core, d).astype(BF16)
        core_copy(i).start()
    for i in range(2):
        near_v[i] = grad_part((1 - ylo) * 2 + core, ds[i])
    for i in range(2):
        core_copy(i).wait()
        y_s[i] = (near_v[i] + core_r[i].astype(F32)).astype(BF16)
        y_copy(i).start()
    for i in range(2):
        core_s[2 + i] = grad_part(ylo * 2 + 1 - core, ds[i]).astype(BF16)
        core_copy(2 + i).start()
    for i in range(2):
        near_v[i] = grad_part(dp, ds[i])

    for i in range(2):
        block = pl.ds(i * (cells // 2), cells // 2)
        prod = ds[i].astype(F32) * cos_v[block, :]
        prod = prod[:, 0:128] + prod[:, 128:256] + prod[:, 256:384] + prod[:, 384:512]
        row_s[:, block] = jnp.sum(prod.T, axis=0, keepdims=True)

    def row_copy(r):
        return pltpu.make_async_remote_copy(
            src_ref=row_s, dst_ref=row_r.at[r - 1], send_sem=row_sem.at[0, r - 1], recv_sem=row_sem.at[1, r - 1],
            device_id=((dp + r) % 4, cent), device_id_type=MESH,
        )

    for r in range(1, 4):
        row_copy(r).start()

    def bx_copy(to, r):
        return pltpu.make_async_remote_copy(
            src_ref=bx_s.at[to], dst_ref=bx_r.at[r - 1], send_sem=b_sem.at[0], recv_sem=b_sem.at[1],
            device_id=(dp, x * 8 + to), device_id_type=MESH,
        )

    def bz_copy(to, r):
        return pltpu.make_async_remote_copy(
            src_ref=bz_s.at[to], dst_ref=bz_r.at[r - 1], send_sem=b_sem.at[2], recv_sem=b_sem.at[3],
            device_id=(dp, to * 4 + z), device_id_type=MESH,
        )

    for r in range(1, 4):
        x_copy(0, r).wait()
    total = gx_s[x].astype(F32)
    for r in range(3):
        total = total + gx_r[r].astype(F32)
    bx_s[...] = total.astype(BF16).reshape(8, 16, half)

    @pl.loop(0, 8)
    def _(to):
        @pl.when(to != yhi * 4 + z)
        def _():
            bx_copy(to, ((to // 4 + 2 - yhi) % 2) * 4 + (to + 4 - z) % 4).start()

    for r in range(1, 4):
        z_copy(0, r).wait()
    total = gz_s[z].astype(F32)
    for r in range(3):
        total = total + gz_r[r].astype(F32)
    bz_s[...] = total.astype(BF16)

    @pl.loop(0, 8)
    def _(to):
        @pl.when(to != x * 2 + yhi)
        def _():
            bz_copy(to, ((to + 2 - yhi) % 2) * 4 + (to // 2 + 4 - x) % 4).start()

    for r in range(1, 4):
        row_copy(r).wait()
    rowdot = row_s[...] + row_r[0] + row_r[1] + row_r[2]
    own_rows = pl.ds(pl.multiple_of(dp * part, 64), part)
    for i in range(2):
        block = pl.ds(i * (cells // 2), cells // 2)
        core_copy(2 + i).wait()
        y_copy(i).wait()
        grad = near_v[i] + core_r[2 + i].astype(F32) + y_r[i].astype(F32)
        here = slice(i * (cells // 2), (i + 1) * (cells // 2))
        cg_ref[:, block] = grad - rowdot[:, here] * ct_v[own_rows, block].astype(F32)

    mine = pl.ds(pl.multiple_of(cent * 16, 16), 16)
    qf = q_v[mine, :].astype(F32)
    norm = jnp.sqrt(jnp.sum(qf * qf, axis=1, keepdims=True) + EPS)
    hat = qh_v[mine, :].astype(F32)
    pltpu.make_async_copy(bx_r, bx_r, b_sem.at[1]).wait()
    left = bx_s[yhi * 4 + z].astype(F32) + jnp.sum(bx_r[...].astype(F32), axis=0)
    pltpu.make_async_copy(bz_r, bz_r, b_sem.at[3]).wait()
    right = bz_s[x * 2 + yhi].astype(F32) + jnp.sum(bz_r[...].astype(F32), axis=0)
    grad = jnp.concatenate([left, right], axis=1)
    along = jnp.sum(grad * hat, axis=1, keepdims=True)
    qg_ref[...] = (grad - along * hat) / norm

    pltpu.make_async_copy(three, three, lse_send.at[8]).wait()
    for i, time in lines:

        @pl.when(time < now)
        def _():
            pltpu.make_async_copy(spare_v, spare_v, lse_send.at[i]).wait()

        @pl.when(time > now)
        def _():
            pltpu.make_async_copy(spare_v.at[0], spare_v.at[0], lse_send.at[i]).wait()

    pltpu.make_async_copy(bx_r, bx_r, b_sem.at[0]).wait()
    pltpu.make_async_copy(bz_r, bz_r, b_sem.at[2]).wait()


def store_results(qg_v, cg_v, qg_hbm, cg_hbm, sem):
    copies = [pltpu.make_async_copy(cg_v, cg_hbm, sem.at[0]), pltpu.make_async_copy(qg_v, qg_hbm, sem.at[1])]
    for copy in copies:
        copy.start()
    for copy in copies:
        copy.wait()


def local(queries, centroids, beta, teacher_ids):
    rows, width = queries.shape
    cells = centroids.shape[0]
    slots = teacher_ids.shape[1]
    half, part = width // 2, width // 4
    dma = pltpu.SemaphoreType.DMA
    results = pl.pallas_call(
        kernel,
        out_shape=(
            jax.ShapeDtypeStruct((rows // 32, width), F32),
            jax.ShapeDtypeStruct((part, cells), F32),
        ),
        in_specs=[pl.BlockSpec(memory_space=pltpu.MemorySpace.HBM)] * 4,
        out_specs=[pl.BlockSpec(memory_space=pltpu.VMEM)] * 2,
        scratch_shapes=[
            pltpu.VMEM((rows, width), BF16),
            pltpu.VMEM((cells, width), BF16),
            pltpu.VMEM((1, rows), F32),
            pltpu.VMEM((slots, rows), jnp.int32),
            pltpu.VMEM((rows, width), BF16),
            pltpu.VMEM((width, rows), BF16),
            pltpu.VMEM((width, cells), BF16),
            pltpu.VMEM((cells, rows), F32),
            pltpu.VMEM((cells, rows), F32),
            pltpu.VMEM((cells, rows), BF16),
            pltpu.VMEM((rows, width), F32),
            pltpu.VMEM((rows, width), F32),
            pltpu.VMEM((1, rows), F32),
            pltpu.VMEM((2, 1, rows), F32),
            pltpu.VMEM((8, 4, 1, rows), F32),
            pltpu.VMEM((4, 1, rows), F32),
            pltpu.VMEM((4, rows // 4, half), BF16),
            pltpu.VMEM((3, rows // 4, half), BF16),
            pltpu.VMEM((4, 8, 16, half), BF16),
            pltpu.VMEM((3, 8, 16, half), BF16),
            pltpu.VMEM((8, 16, half), BF16),
            pltpu.VMEM((7, 16, half), BF16),
            pltpu.VMEM((8, 16, half), BF16),
            pltpu.VMEM((7, 16, half), BF16),
            pltpu.VMEM((4, part, cells // 2), BF16),
            pltpu.VMEM((4, part, cells // 2), BF16),
            pltpu.VMEM((2, part, cells // 2), BF16),
            pltpu.VMEM((2, part, cells // 2), BF16),
            pltpu.VMEM((2, part, cells // 2), F32),
            pltpu.VMEM((1, cells), F32),
            pltpu.VMEM((3, 1, cells), F32),
            dma((4,)),
            dma((9,)),
            dma((9,)),
            dma((2, 3)),
            dma((2, 3)),
            dma((4,)),
            dma((4,)),
            dma((4,)),
            dma((2,)),
            dma((2,)),
            dma((2, 3)),
            pltpu.SemaphoreType.REGULAR,
        ],
        compiler_params=pltpu.CompilerParams(
            collective_id=0, has_side_effects=True, vmem_limit_bytes=24 * 1024 * 1024
        ),
    )(*[pltpu.with_memory_space_constraint(a, pltpu.MemorySpace.HBM) for a in (queries, centroids, beta.reshape(1, rows), teacher_ids.T)])
    query_grad, centroid_grad = pl.pallas_call(
        store_results,
        out_shape=[jax.ShapeDtypeStruct(a.shape, a.dtype) for a in results],
        in_specs=[pl.BlockSpec(memory_space=pltpu.VMEM)] * 2,
        out_specs=[pl.BlockSpec(memory_space=pltpu.MemorySpace.HBM)] * 2,
        scratch_shapes=[dma((2,))],
        compiler_params=pltpu.CompilerParams(vmem_limit_bytes=1024 * 1024),
    )(*results)
    return query_grad, centroid_grad.T


def solution(mesh):
    in_specs = (P("dp", None), P("cent", None), P("dp"), P("dp", None))
    out_specs = (P(("dp", "cent"), None), P("cent", "dp"))
    return jax.shard_map(local, mesh=mesh, in_specs=in_specs, out_specs=out_specs, check_vma=False)
```

```python
import functools

import jax
import jax.numpy as jnp
from jax import lax
from jax.experimental import pallas as pl
from jax.experimental.pallas import tpu as pltpu
from jax.sharding import PartitionSpec as P

EPS = 1e-06
SCALE = 1024.0
LOWEST = -1e30
MESH = pl.DeviceIdType.MESH
F32 = jnp.float32
BF16 = jnp.bfloat16
NT = (((1,), (1,)), ((), ()))
TN = (((0,), (0,)), ((), ()))


def dot(a, b, dims):
    return lax.dot_general(a, b, dims, preferred_element_type=F32)


def join(parts):
    top = jnp.max(parts, axis=0)
    return top + jnp.log(jnp.sum(jnp.exp(parts - top[None]), axis=0))


def kernel(
    q_hbm, c_hbm, beta_hbm, ids_hbm,
    qg_ref, cg_ref,
    q_v, c_v, beta_v, ids_v,
    qh_v, qht_v, ct_v, cos_v, e_v, d_v,
    es_v, ts_v,
    lse_v, lse_s, stat_v, spare_v,
    gx_s, gx_r, gz_s, gz_r,
    bx_s, bx_r, bz_s, bz_r,
    core_s, core_r, y_s, y_r,
    near_v, far_v, diff_v, row_s, row_r,
    in_sem, lse_send, lse_recv, a_send, a_recv, b_sem, core_send, core_recv, y_send, y_recv, row_sem, ready_sem,
):
    rows, width = q_hbm.shape
    cells = c_hbm.shape[0]
    slots = ids_hbm.shape[0]
    half = width // 2
    part = width // 4
    dp = lax.axis_index("dp")
    cent = lax.axis_index("cent")
    x = cent // 8
    yhi = (cent // 4) % 2
    z = cent % 4
    core = dp % 2
    ylo = dp // 2

    loads = [
        pltpu.make_async_copy(src, dst, in_sem.at[i])
        for i, (src, dst) in enumerate(((q_hbm, q_v), (c_hbm, c_v), (beta_hbm, beta_v), (ids_hbm, ids_v)))
    ]
    for load in loads:
        load.start()

    barrier = pltpu.get_barrier_semaphore()

    for r in range(1, 4):
        pl.semaphore_signal(barrier, inc=1, device_id=(dp, (((x + r) % 4) * 2 + yhi) * 4 + z), device_id_type=MESH)
        pl.semaphore_signal(barrier, inc=1, device_id=(dp, (x * 2 + yhi) * 4 + (z + r) % 4), device_id_type=MESH)
        pl.semaphore_signal(barrier, inc=1, device_id=((dp + r) % 4, cent), device_id_type=MESH)
    pl.semaphore_signal(barrier, inc=1, device_id=(dp, (x * 2 + 1 - yhi) * 4 + z), device_id_type=MESH)

    def start_time(line_yhi, line_z):
        return 27 * line_yhi + 11 * line_z + 2 * (line_z // 2)

    now = start_time(yhi, z)
    lines = [(i, start_time(i // 4, i % 4)) for i in range(8)]
    own_line = yhi * 4 + z
    earlier_lines = sum([jnp.where(time < now, 1, 0) for _, time in lines])
    for i, time in lines:

        @pl.when(time > now)
        def _():
            for to in range(4):
                pl.semaphore_signal(barrier, inc=1, device_id=(dp, to * 8 + i), device_id_type=MESH)

        @pl.when(time < now)
        def _():
            stat_v[i, 1:4] = jnp.full((3, 1, rows), LOWEST, F32)

    loads[0].wait()
    for i in range(4):
        block = pl.ds(i * (rows // 4), rows // 4)
        qf = q_v[block, :].astype(F32)
        inv = 1.0 / jnp.sqrt(jnp.sum(qf * qf, axis=1, keepdims=True) + EPS)
        qh_v[block, :] = (qf * inv).astype(BF16)

    loads[1].wait()
    loads[2].wait()
    loads[3].wait()
    for i in range(2):
        lanes = pl.ds(i * (rows // 2), rows // 2)
        cosine = dot(c_v[...], qh_v[lanes, :], NT)
        cos_v[:, lanes] = cosine
        score = cosine * beta_v[:, lanes]
        top = jnp.max(score, axis=0, keepdims=True)
        expo = jnp.exp(score - top)
        total = jnp.sum(expo, axis=0, keepdims=True)
        lse_s[0, :, lanes] = top + jnp.log(total)
        stat_v[own_line, x, :, lanes] = top + jnp.log(total)
        e_v[:, lanes] = expo * (1.0 / total)

    pl.semaphore_wait(barrier, 10 + 4 * earlier_lines)
    pl.semaphore_signal(ready_sem, inc=1, device_id=(dp, (x * 2 + 1 - yhi) * 4 + z), device_id_type=MESH)

    def line_copy(r):
        return pltpu.make_async_remote_copy(
            src_ref=lse_s.at[0], dst_ref=stat_v.at[own_line, x], send_sem=lse_send.at[8], recv_sem=lse_recv.at[8],
            device_id=(dp, ((x + r) % 4) * 8 + own_line), device_id_type=MESH,
        )

    def early_copy(i, to):
        return pltpu.make_async_remote_copy(
            src_ref=lse_s.at[0], dst_ref=stat_v.at[own_line, x], send_sem=lse_send.at[i], recv_sem=lse_recv.at[own_line],
            device_id=(dp, to * 8 + i), device_id_type=MESH,
        )

    def late_copy(i):
        return pltpu.make_async_remote_copy(
            src_ref=lse_s.at[1], dst_ref=stat_v.at[own_line, 0], send_sem=lse_send.at[i], recv_sem=lse_recv.at[own_line],
            device_id=(dp, x * 8 + i), device_id_type=MESH,
        )

    for r in (2, 1, 3):
        line_copy(r).start()
    for i, time in lines:

        @pl.when(time < now)
        def _():
            for to in range(4):
                early_copy(i, to).start()

    for i in range(2):
        lanes = pl.ds(i * (rows // 2), rows // 2)
        es_v[lanes, :] = dot(e_v[:, lanes].astype(BF16), c_v[...], TN)
    ids = ids_v[...] - cent * cells
    position = lax.broadcasted_iota(jnp.int32, (256, rows), 0).astype(F32).astype(BF16)
    for h in range(cells // 256):
        here = ids - h * 256
        here = jnp.where((here >= 0) & (here < 256), here, -1).astype(F32)
        count = jnp.zeros((256, rows), BF16)
        for slot in range(slots):
            hit = jnp.broadcast_to(here[slot : slot + 1], (256, rows)).astype(BF16) == position
            count = count + jnp.where(hit, jnp.bfloat16(SCALE / slots), jnp.bfloat16(0.0))
        d_v[pl.ds(h * 256, 256), :] = count
    for i in range(2):
        lanes = pl.ds(i * (rows // 2), rows // 2)
        ts_v[lanes, :] = dot(d_v[:, lanes], c_v[...], TN)
    qht_v[...] = qh_v[...].T
    ct_v[...] = c_v[...].T

    three = spare_v.at[pl.ds(0, 3)]
    pltpu.make_async_copy(three, three, lse_recv.at[8]).wait()
    lse_s[1] = join(stat_v[own_line])
    for i, time in lines:

        @pl.when((time > now) & ((i // 4 == yhi) | (i % 4 == z)))
        def _():
            late_copy(i).start()

    pl.semaphore_wait(ready_sem, 1)
    for i, time in lines:

        @pl.when((time > now) & (i // 4 != yhi) & (i % 4 != z))
        def _():
            late_copy(i).start()

    for i, time in lines:

        @pl.when(time > now)
        def _():
            pltpu.make_async_copy(spare_v, spare_v, lse_recv.at[i]).wait()

        @pl.when(time < now)
        def _():
            pltpu.make_async_copy(spare_v.at[0], spare_v.at[0], lse_recv.at[i]).wait()

    lse_v[...] = join(stat_v[...].reshape(32, 1, rows))
    weight = jnp.exp(lse_s[0] - lse_v[...]) * SCALE
    weight_col = jnp.broadcast_to(weight, (128, rows)).T

    for i in range(rows // 128):
        block = pl.ds(i * 128, 128)
        for j in range(3):
            cols = pl.ds(j * 128, 128)
            g = es_v[block, cols] * weight_col[i * 128 : (i + 1) * 128] - ts_v[block, cols]
            gx_s[i, :, :, cols] = g.astype(BF16).reshape(8, 16, 128)
        for j in range(3):
            cols = pl.ds(half + j * 128, 128)
            g = (es_v[block, cols] * weight_col[i * 128 : (i + 1) * 128] - ts_v[block, cols]).astype(BF16)
            for k in range(8):
                gz_s[k % 4, 4 * (k // 4) + i, :, pl.ds(j * 128, 128)] = g[k * 16 : (k + 1) * 16]

    def x_copy(p, to, r):
        pair = pl.ds(2 * p, 2)
        return pltpu.make_async_remote_copy(
            src_ref=gx_s.at[to, pair], dst_ref=gx_r.at[r - 1, pair], send_sem=a_send.at[0, p, r - 1], recv_sem=a_recv.at[0, p, r - 1],
            device_id=(dp, (to * 2 + yhi) * 4 + z), device_id_type=MESH,
        )

    def z_copy(p, to, r):
        pair = pl.ds(2 * p, 2)
        return pltpu.make_async_remote_copy(
            src_ref=gz_s.at[to, pair], dst_ref=gz_r.at[r - 1, pair], send_sem=a_send.at[1, p, r - 1], recv_sem=a_recv.at[1, p, r - 1],
            device_id=(dp, (x * 2 + yhi) * 4 + to), device_id_type=MESH,
        )

    for p in range(4):
        for to in range(4):

            @pl.when(to != x)
            def _():
                x_copy(p, to, (to + 4 - x) % 4).start()

            @pl.when(to != z)
            def _():
                z_copy(p, to, (to + 4 - z) % 4).start()

    def grad_part(to, d):
        return dot(qht_v[pl.ds(pl.multiple_of(to * part, 64), part), :], d, NT)

    def core_copy(i):
        return pltpu.make_async_remote_copy(
            src_ref=core_s.at[i], dst_ref=core_r.at[i], send_sem=core_send.at[i], recv_sem=core_recv.at[i],
            device_id=(ylo * 2 + 1 - core, cent), device_id_type=MESH,
        )

    def y_copy(i):
        return pltpu.make_async_remote_copy(
            src_ref=y_s.at[i], dst_ref=y_r.at[i], send_sem=y_send.at[i], recv_sem=y_recv.at[i],
            device_id=((1 - ylo) * 2 + core, cent), device_id_type=MESH,
        )

    def centroid_start():
        for i in range(2):
            block = pl.ds(i * (cells // 2), cells // 2)
            diff_v[block, :] = (e_v[block, :] * weight - d_v[block, :].astype(F32)).astype(BF16)
            core_s[i] = grad_part((1 - ylo) * 2 + 1 - core, diff_v[block, :]).astype(BF16)
            core_copy(i).start()
        for i in range(2):
            block = pl.ds(i * (cells // 2), cells // 2)
            far_v[i] = grad_part((1 - ylo) * 2 + core, diff_v[block, :])

    def centroid_cross():
        for i in range(2):
            core_copy(i).wait()
            y_s[i] = (far_v[i] + core_r[i].astype(F32)).astype(BF16)
            y_copy(i).start()

    centroid_start()

    @pl.when(yhi == 0)
    def _():
        centroid_cross()

    for i in range(2):
        block = pl.ds(i * (cells // 2), cells // 2)
        core_s[2 + i] = grad_part(ylo * 2 + 1 - core, diff_v[block, :]).astype(BF16)
        core_copy(2 + i).start()
    for i in range(2):
        block = pl.ds(i * (cells // 2), cells // 2)
        near_v[i] = grad_part(dp, diff_v[block, :])

    for i in range(2):
        block = pl.ds(i * (cells // 2), cells // 2)
        prod = diff_v[block, :].astype(F32) * cos_v[block, :]
        prod = prod[:, 0:128] + prod[:, 128:256] + prod[:, 256:384] + prod[:, 384:512]
        row_s[:, block] = jnp.sum(prod.T, axis=0, keepdims=True)

    def row_copy(r):
        return pltpu.make_async_remote_copy(
            src_ref=row_s, dst_ref=row_r.at[r - 1], send_sem=row_sem.at[0, r - 1], recv_sem=row_sem.at[1, r - 1],
            device_id=((dp + r) % 4, cent), device_id_type=MESH,
        )

    for r in range(1, 4):
        row_copy(r).start()

    def bx_copy(to, r):
        return pltpu.make_async_remote_copy(
            src_ref=bx_s.at[to], dst_ref=bx_r.at[r - 1], send_sem=b_sem.at[0], recv_sem=b_sem.at[1],
            device_id=(dp, x * 8 + to), device_id_type=MESH,
        )

    def bz_copy(to, r):
        return pltpu.make_async_remote_copy(
            src_ref=bz_s.at[to], dst_ref=bz_r.at[r - 1], send_sem=b_sem.at[2], recv_sem=b_sem.at[3],
            device_id=(dp, (to % 4) * 8 + (to // 4) * 4 + z), device_id_type=MESH,
        )

    def pass_on(p):
        pair = pl.ds(2 * p, 2)
        for copy, own, mine, got, out, send in (
            (x_copy, x, gx_s, gx_r, bx_s, bx_copy),
            (z_copy, z, gz_s, gz_r, bz_s, bz_copy),
        ):
            for r in range(1, 4):
                copy(p, 0, r).wait()
            total = mine[own, pair].astype(F32)
            for r in range(3):
                total = total + got[r, pair].astype(F32)
            out[pair] = total.astype(BF16)
            place = z if send is bx_copy else x
            for to in (2 * p, 2 * p + 1):

                @pl.when(to != yhi * 4 + place)
                def _():
                    send(to, ((to // 4 + 2 - yhi) % 2) * 4 + (to % 4 + 4 - place) % 4).start()

    pass_on(0)
    pass_on(1)

    @pl.when(yhi == 1)
    def _():
        centroid_cross()

    pass_on(2)
    pass_on(3)

    for r in range(1, 4):
        row_copy(r).wait()
    rowdot = row_s[...] + row_r[0] + row_r[1] + row_r[2]
    own_rows = pl.ds(pl.multiple_of(dp * part, 64), part)
    for i in range(2):
        block = pl.ds(i * (cells // 2), cells // 2)
        core_copy(2 + i).wait()
        y_copy(i).wait()
        grad = near_v[i] + core_r[2 + i].astype(F32) + y_r[i].astype(F32)
        here = slice(i * (cells // 2), (i + 1) * (cells // 2))
        cg_ref[:, block] = grad - rowdot[:, here] * ct_v[own_rows, block].astype(F32)

    mine = pl.ds(pl.multiple_of(cent * 16, 16), 16)
    qf = q_v[mine, :].astype(F32)
    norm = jnp.sqrt(jnp.sum(qf * qf, axis=1, keepdims=True) + EPS)
    hat = qh_v[mine, :].astype(F32)
    pltpu.make_async_copy(bx_r, bx_r, b_sem.at[1]).wait()
    left = bx_s[yhi * 4 + z].astype(F32) + jnp.sum(bx_r[...].astype(F32), axis=0)
    pltpu.make_async_copy(bz_r, bz_r, b_sem.at[3]).wait()
    right = bz_s[yhi * 4 + x].astype(F32) + jnp.sum(bz_r[...].astype(F32), axis=0)
    grad = jnp.concatenate([left, right], axis=1)
    along = jnp.sum(grad * hat, axis=1, keepdims=True)
    qg_ref[...] = (grad - along * hat) / norm

    pltpu.make_async_copy(three, three, lse_send.at[8]).wait()
    for i, time in lines:

        @pl.when(time < now)
        def _():
            pltpu.make_async_copy(spare_v, spare_v, lse_send.at[i]).wait()

        @pl.when(time > now)
        def _():
            pltpu.make_async_copy(spare_v.at[0], spare_v.at[0], lse_send.at[i]).wait()

    pltpu.make_async_copy(bx_r, bx_r, b_sem.at[0]).wait()
    pltpu.make_async_copy(bz_r, bz_r, b_sem.at[2]).wait()


def store_results(qg_v, cg_v, qg_hbm, cg_hbm, sem):
    copies = [pltpu.make_async_copy(cg_v, cg_hbm, sem.at[0]), pltpu.make_async_copy(qg_v, qg_hbm, sem.at[1])]
    for copy in copies:
        copy.start()
    for copy in copies:
        copy.wait()


def local(queries, centroids, beta, teacher_ids):
    rows, width = queries.shape
    cells = centroids.shape[0]
    slots = teacher_ids.shape[1]
    half, part = width // 2, width // 4
    dma = pltpu.SemaphoreType.DMA
    results = pl.pallas_call(
        kernel,
        out_shape=(
            jax.ShapeDtypeStruct((rows // 32, width), F32),
            jax.ShapeDtypeStruct((part, cells), F32),
        ),
        in_specs=[pl.BlockSpec(memory_space=pltpu.MemorySpace.HBM)] * 4,
        out_specs=[pl.BlockSpec(memory_space=pltpu.VMEM)] * 2,
        scratch_shapes=[
            pltpu.VMEM((rows, width), BF16),
            pltpu.VMEM((cells, width), BF16),
            pltpu.VMEM((1, rows), F32),
            pltpu.VMEM((slots, rows), jnp.int32),
            pltpu.VMEM((rows, width), BF16),
            pltpu.VMEM((width, rows), BF16),
            pltpu.VMEM((width, cells), BF16),
            pltpu.VMEM((cells, rows), F32),
            pltpu.VMEM((cells, rows), F32),
            pltpu.VMEM((cells, rows), BF16),
            pltpu.VMEM((rows, width), F32),
            pltpu.VMEM((rows, width), F32),
            pltpu.VMEM((1, rows), F32),
            pltpu.VMEM((2, 1, rows), F32),
            pltpu.VMEM((8, 4, 1, rows), F32),
            pltpu.VMEM((4, 1, rows), F32),
            pltpu.VMEM((4, 8, 16, half), BF16),
            pltpu.VMEM((3, 8, 16, half), BF16),
            pltpu.VMEM((4, 8, 16, half), BF16),
            pltpu.VMEM((3, 8, 16, half), BF16),
            pltpu.VMEM((8, 16, half), BF16),
            pltpu.VMEM((7, 16, half), BF16),
            pltpu.VMEM((8, 16, half), BF16),
            pltpu.VMEM((7, 16, half), BF16),
            pltpu.VMEM((4, part, cells // 2), BF16),
            pltpu.VMEM((4, part, cells // 2), BF16),
            pltpu.VMEM((2, part, cells // 2), BF16),
            pltpu.VMEM((2, part, cells // 2), BF16),
            pltpu.VMEM((2, part, cells // 2), F32),
            pltpu.VMEM((2, part, cells // 2), F32),
            pltpu.VMEM((cells, rows), BF16),
            pltpu.VMEM((1, cells), F32),
            pltpu.VMEM((3, 1, cells), F32),
            dma((4,)),
            dma((9,)),
            dma((9,)),
            dma((2, 4, 3)),
            dma((2, 4, 3)),
            dma((4,)),
            dma((4,)),
            dma((4,)),
            dma((2,)),
            dma((2,)),
            dma((2, 3)),
            pltpu.SemaphoreType.REGULAR,
        ],
        compiler_params=pltpu.CompilerParams(
            collective_id=0, has_side_effects=True, vmem_limit_bytes=24 * 1024 * 1024
        ),
    )(*[pltpu.with_memory_space_constraint(a, pltpu.MemorySpace.HBM) for a in (queries, centroids, beta.reshape(1, rows), teacher_ids.T)])
    query_grad, centroid_grad = pl.pallas_call(
        store_results,
        out_shape=[jax.ShapeDtypeStruct(a.shape, a.dtype) for a in results],
        in_specs=[pl.BlockSpec(memory_space=pltpu.VMEM)] * 2,
        out_specs=[pl.BlockSpec(memory_space=pltpu.MemorySpace.HBM)] * 2,
        scratch_shapes=[dma((2,))],
        compiler_params=pltpu.CompilerParams(vmem_limit_bytes=1024 * 1024),
    )(*results)
    return query_grad, centroid_grad.T


def solution(mesh):
    in_specs = (P("dp", None), P("cent", None), P("dp"), P("dp", None))
    out_specs = (P(("dp", "cent"), None), P("cent", "dp"))
    return jax.shard_map(local, mesh=mesh, in_specs=in_specs, out_specs=out_specs, check_vma=False)
```

```python
import functools

import jax
import jax.numpy as jnp
from jax import lax
from jax.experimental import pallas as pl
from jax.experimental.pallas import tpu as pltpu
from jax.sharding import PartitionSpec as P

EPS = 1e-06
SCALE = 1024.0
LOWEST = -1e30
MESH = pl.DeviceIdType.MESH
F32 = jnp.float32
BF16 = jnp.bfloat16
NT = (((1,), (1,)), ((), ()))
TN = (((0,), (0,)), ((), ()))


def dot(a, b, dims):
    return lax.dot_general(a, b, dims, preferred_element_type=F32)


def join(parts):
    top = jnp.max(parts, axis=0)
    return top + jnp.log(jnp.sum(jnp.exp(parts - top[None]), axis=0))


def kernel(
    q_hbm, c_hbm, beta_hbm, ids_hbm,
    qg_ref, cg_ref,
    q_v, c_v, beta_v, ids_v,
    qh_v, qht_v, ct_v, cos_v, e_v, d_v,
    es_v, ts_v,
    lse_v, lse_s, stat_v, spare_v,
    gx_s, gx_r, gz_s, gz_r,
    bx_s, bx_r, bz_s, bz_r,
    core_s, core_r, y_s, y_r,
    near_v, far_v, diff_v, row_s, row_r,
    in_sem, lse_send, lse_recv, a_send, a_recv, b_sem, core_send, core_recv, y_send, y_recv, row_sem, ready_sem,
):
    rows, width = q_hbm.shape
    cells = c_hbm.shape[0]
    slots = ids_hbm.shape[0]
    half = width // 2
    part = width // 4
    dp = lax.axis_index("dp")
    cent = lax.axis_index("cent")
    x = cent // 8
    yhi = (cent // 4) % 2
    z = cent % 4
    core = dp % 2
    ylo = dp // 2

    loads = [
        pltpu.make_async_copy(src, dst, in_sem.at[i])
        for i, (src, dst) in enumerate(((q_hbm, q_v), (c_hbm, c_v), (beta_hbm, beta_v), (ids_hbm, ids_v)))
    ]
    for load in loads:
        load.start()

    barrier = pltpu.get_barrier_semaphore()

    for r in range(1, 4):
        pl.semaphore_signal(barrier, inc=1, device_id=(dp, (((x + r) % 4) * 2 + yhi) * 4 + z), device_id_type=MESH)
        pl.semaphore_signal(barrier, inc=1, device_id=(dp, (x * 2 + yhi) * 4 + (z + r) % 4), device_id_type=MESH)
        pl.semaphore_signal(barrier, inc=1, device_id=((dp + r) % 4, cent), device_id_type=MESH)
    pl.semaphore_signal(barrier, inc=1, device_id=(dp, (x * 2 + 1 - yhi) * 4 + z), device_id_type=MESH)

    def start_time(line_yhi, line_z):
        return (27 - 17 * ylo) * line_yhi + 11 * line_z + 2 * (line_z // 2)

    now = start_time(yhi, z)
    lines = [(i, start_time(i // 4, i % 4)) for i in range(8)]
    own_line = yhi * 4 + z
    earlier_lines = sum([jnp.where(time < now, 1, 0) for _, time in lines])
    for i, time in lines:

        @pl.when(time > now)
        def _():
            for to in range(4):
                pl.semaphore_signal(barrier, inc=1, device_id=(dp, to * 8 + i), device_id_type=MESH)

        @pl.when(time < now)
        def _():
            stat_v[i, 1:4] = jnp.full((3, 1, rows), LOWEST, F32)

    loads[0].wait()
    for i in range(4):
        block = pl.ds(i * (rows // 4), rows // 4)
        qf = q_v[block, :].astype(F32)
        inv = 1.0 / jnp.sqrt(jnp.sum(qf * qf, axis=1, keepdims=True) + EPS)
        qh_v[block, :] = (qf * inv).astype(BF16)

    loads[1].wait()
    loads[2].wait()
    loads[3].wait()
    for i in range(2):
        lanes = pl.ds(i * (rows // 2), rows // 2)
        cosine = dot(c_v[...], qh_v[lanes, :], NT)
        cos_v[:, lanes] = cosine
        score = cosine * beta_v[:, lanes]
        top = jnp.max(score, axis=0, keepdims=True)
        expo = jnp.exp(score - top)
        total = jnp.sum(expo, axis=0, keepdims=True)
        lse_s[0, :, lanes] = top + jnp.log(total)
        stat_v[own_line, x, :, lanes] = top + jnp.log(total)
        e_v[:, lanes] = expo * (1.0 / total)

    pl.semaphore_wait(barrier, 10 + 4 * earlier_lines)
    pl.semaphore_signal(ready_sem, inc=1, device_id=(dp, (x * 2 + 1 - yhi) * 4 + z), device_id_type=MESH)

    def line_copy(r):
        return pltpu.make_async_remote_copy(
            src_ref=lse_s.at[0], dst_ref=stat_v.at[own_line, x], send_sem=lse_send.at[8], recv_sem=lse_recv.at[8],
            device_id=(dp, ((x + r) % 4) * 8 + own_line), device_id_type=MESH,
        )

    def early_copy(i, to):
        return pltpu.make_async_remote_copy(
            src_ref=lse_s.at[0], dst_ref=stat_v.at[own_line, x], send_sem=lse_send.at[i], recv_sem=lse_recv.at[own_line],
            device_id=(dp, to * 8 + i), device_id_type=MESH,
        )

    def late_copy(i):
        return pltpu.make_async_remote_copy(
            src_ref=lse_s.at[1], dst_ref=stat_v.at[own_line, 0], send_sem=lse_send.at[i], recv_sem=lse_recv.at[own_line],
            device_id=(dp, x * 8 + i), device_id_type=MESH,
        )

    for r in (2, 1, 3):
        line_copy(r).start()
    for i, time in lines:

        @pl.when(time < now)
        def _():
            for to in range(4):
                early_copy(i, to).start()

    for i in range(2):
        lanes = pl.ds(i * (rows // 2), rows // 2)
        es_v[lanes, :] = dot(e_v[:, lanes].astype(BF16), c_v[...], TN)
    ids = ids_v[...] - cent * cells
    position = lax.broadcasted_iota(jnp.int32, (256, rows), 0).astype(F32).astype(BF16)
    for h in range(cells // 256):
        here = ids - h * 256
        here = jnp.where((here >= 0) & (here < 256), here, -1).astype(F32)
        count = jnp.zeros((256, rows), BF16)
        for slot in range(slots):
            hit = jnp.broadcast_to(here[slot : slot + 1], (256, rows)).astype(BF16) == position
            count = count + jnp.where(hit, jnp.bfloat16(SCALE / slots), jnp.bfloat16(0.0))
        d_v[pl.ds(h * 256, 256), :] = count
    for i in range(2):
        lanes = pl.ds(i * (rows // 2), rows // 2)
        ts_v[lanes, :] = dot(d_v[:, lanes], c_v[...], TN)
    qht_v[...] = qh_v[...].T
    ct_v[...] = c_v[...].T

    three = spare_v.at[pl.ds(0, 3)]
    pltpu.make_async_copy(three, three, lse_recv.at[8]).wait()
    lse_s[1] = join(stat_v[own_line])
    for i, time in lines:

        @pl.when((time > now) & ((i // 4 == yhi) | (i % 4 == z)))
        def _():
            late_copy(i).start()

    pl.semaphore_wait(ready_sem, 1)
    for i, time in lines:

        @pl.when((time > now) & (i // 4 != yhi) & (i % 4 != z))
        def _():
            late_copy(i).start()

    for i, time in lines:

        @pl.when(time > now)
        def _():
            pltpu.make_async_copy(spare_v, spare_v, lse_recv.at[i]).wait()

        @pl.when(time < now)
        def _():
            pltpu.make_async_copy(spare_v.at[0], spare_v.at[0], lse_recv.at[i]).wait()

    lse_v[...] = join(stat_v[...].reshape(32, 1, rows))
    weight = jnp.exp(lse_s[0] - lse_v[...]) * SCALE
    weight_col = jnp.broadcast_to(weight, (128, rows)).T

    for i in range(rows // 128):
        block = pl.ds(i * 128, 128)
        for j in range(3):
            cols = pl.ds(j * 128, 128)
            g = es_v[block, cols] * weight_col[i * 128 : (i + 1) * 128] - ts_v[block, cols]
            gx_s[i, :, :, cols] = g.astype(BF16).reshape(8, 16, 128)
        for j in range(3):
            cols = pl.ds(half + j * 128, 128)
            g = (es_v[block, cols] * weight_col[i * 128 : (i + 1) * 128] - ts_v[block, cols]).astype(BF16)
            for k in range(8):
                gz_s[k % 4, 4 * (k // 4) + i, :, pl.ds(j * 128, 128)] = g[k * 16 : (k + 1) * 16]

    def x_copy(p, to, r):
        pair = pl.ds(2 * p, 2)
        return pltpu.make_async_remote_copy(
            src_ref=gx_s.at[to, pair], dst_ref=gx_r.at[r - 1, pair], send_sem=a_send.at[0, p, r - 1], recv_sem=a_recv.at[0, p, r - 1],
            device_id=(dp, (to * 2 + yhi) * 4 + z), device_id_type=MESH,
        )

    def z_copy(p, to, r):
        pair = pl.ds(2 * p, 2)
        return pltpu.make_async_remote_copy(
            src_ref=gz_s.at[to, pair], dst_ref=gz_r.at[r - 1, pair], send_sem=a_send.at[1, p, r - 1], recv_sem=a_recv.at[1, p, r - 1],
            device_id=(dp, (x * 2 + yhi) * 4 + to), device_id_type=MESH,
        )

    for p in (0, 2, 1, 3):
        for to in range(4):

            @pl.when(to != x)
            def _():
                x_copy(p, to, (to + 4 - x) % 4).start()

            @pl.when(to != z)
            def _():
                z_copy(p, to, (to + 4 - z) % 4).start()

    def grad_part(to, d):
        return dot(qht_v[pl.ds(pl.multiple_of(to * part, 64), part), :], d, NT)

    def core_copy(i):
        return pltpu.make_async_remote_copy(
            src_ref=core_s.at[i], dst_ref=core_r.at[i], send_sem=core_send.at[i], recv_sem=core_recv.at[i],
            device_id=(ylo * 2 + 1 - core, cent), device_id_type=MESH,
        )

    def y_copy(i):
        return pltpu.make_async_remote_copy(
            src_ref=y_s.at[i], dst_ref=y_r.at[i], send_sem=y_send.at[i], recv_sem=y_recv.at[i],
            device_id=((1 - ylo) * 2 + core, cent), device_id_type=MESH,
        )

    def centroid_start():
        for i in range(2):
            block = pl.ds(i * (cells // 2), cells // 2)
            diff_v[block, :] = (e_v[block, :] * weight - d_v[block, :].astype(F32)).astype(BF16)
            core_s[i] = grad_part((1 - ylo) * 2 + 1 - core, diff_v[block, :]).astype(BF16)
            core_copy(i).start()
        for i in range(2):
            block = pl.ds(i * (cells // 2), cells // 2)
            far_v[i] = grad_part((1 - ylo) * 2 + core, diff_v[block, :])

    def centroid_cross():
        for i in range(2):
            core_copy(i).wait()
            y_s[i] = (far_v[i] + core_r[i].astype(F32)).astype(BF16)
            y_copy(i).start()

    centroid_start()

    @pl.when(yhi == 0)
    def _():
        centroid_cross()

    for i in range(2):
        block = pl.ds(i * (cells // 2), cells // 2)
        core_s[2 + i] = grad_part(ylo * 2 + 1 - core, diff_v[block, :]).astype(BF16)
        core_copy(2 + i).start()
    for i in range(2):
        block = pl.ds(i * (cells // 2), cells // 2)
        near_v[i] = grad_part(dp, diff_v[block, :])

    for i in range(2):
        block = pl.ds(i * (cells // 2), cells // 2)
        prod = diff_v[block, :].astype(F32) * cos_v[block, :]
        prod = prod[:, 0:128] + prod[:, 128:256] + prod[:, 256:384] + prod[:, 384:512]
        row_s[:, block] = jnp.sum(prod.T, axis=0, keepdims=True)

    def row_copy(r):
        return pltpu.make_async_remote_copy(
            src_ref=row_s, dst_ref=row_r.at[r - 1], send_sem=row_sem.at[0, r - 1], recv_sem=row_sem.at[1, r - 1],
            device_id=((dp + r) % 4, cent), device_id_type=MESH,
        )

    for r in range(1, 4):
        row_copy(r).start()

    def bx_copy(to, r):
        return pltpu.make_async_remote_copy(
            src_ref=bx_s.at[to], dst_ref=bx_r.at[r - 1], send_sem=b_sem.at[0], recv_sem=b_sem.at[1],
            device_id=(dp, x * 8 + to), device_id_type=MESH,
        )

    def bz_copy(to, r):
        return pltpu.make_async_remote_copy(
            src_ref=bz_s.at[to], dst_ref=bz_r.at[r - 1], send_sem=b_sem.at[2], recv_sem=b_sem.at[3],
            device_id=(dp, (to % 4) * 8 + (to // 4) * 4 + z), device_id_type=MESH,
        )

    def pass_on(p):
        pair = pl.ds(2 * p, 2)
        for copy, own, mine, got, out, send in (
            (x_copy, x, gx_s, gx_r, bx_s, bx_copy),
            (z_copy, z, gz_s, gz_r, bz_s, bz_copy),
        ):
            for r in range(1, 4):
                copy(p, 0, r).wait()
            total = mine[own, pair].astype(F32)
            for r in range(3):
                total = total + got[r, pair].astype(F32)
            out[pair] = total.astype(BF16)
            place = z if send is bx_copy else x
            for to in (2 * p, 2 * p + 1):

                @pl.when(to != yhi * 4 + place)
                def _():
                    send(to, ((to // 4 + 2 - yhi) % 2) * 4 + (to % 4 + 4 - place) % 4).start()

    pass_on(0)

    @pl.when(yhi == 1)
    def _():
        centroid_cross()

    pass_on(2)
    pass_on(1)
    pass_on(3)

    for r in range(1, 4):
        row_copy(r).wait()
    rowdot = row_s[...] + row_r[0] + row_r[1] + row_r[2]
    own_rows = pl.ds(pl.multiple_of(dp * part, 64), part)
    for i in range(2):
        block = pl.ds(i * (cells // 2), cells // 2)
        core_copy(2 + i).wait()
        y_copy(i).wait()
        grad = near_v[i] + core_r[2 + i].astype(F32) + y_r[i].astype(F32)
        here = slice(i * (cells // 2), (i + 1) * (cells // 2))
        cg_ref[:, block] = grad - rowdot[:, here] * ct_v[own_rows, block].astype(F32)

    mine = pl.ds(pl.multiple_of(cent * 16, 16), 16)
    qf = q_v[mine, :].astype(F32)
    norm = jnp.sqrt(jnp.sum(qf * qf, axis=1, keepdims=True) + EPS)
    hat = qh_v[mine, :].astype(F32)
    pltpu.make_async_copy(bx_r, bx_r, b_sem.at[1]).wait()
    left = bx_s[yhi * 4 + z].astype(F32) + jnp.sum(bx_r[...].astype(F32), axis=0)
    pltpu.make_async_copy(bz_r, bz_r, b_sem.at[3]).wait()
    right = bz_s[yhi * 4 + x].astype(F32) + jnp.sum(bz_r[...].astype(F32), axis=0)
    grad = jnp.concatenate([left, right], axis=1)
    along = jnp.sum(grad * hat, axis=1, keepdims=True)
    qg_ref[...] = (grad - along * hat) / norm

    pltpu.make_async_copy(three, three, lse_send.at[8]).wait()
    for i, time in lines:

        @pl.when(time < now)
        def _():
            pltpu.make_async_copy(spare_v, spare_v, lse_send.at[i]).wait()

        @pl.when(time > now)
        def _():
            pltpu.make_async_copy(spare_v.at[0], spare_v.at[0], lse_send.at[i]).wait()

    pltpu.make_async_copy(bx_r, bx_r, b_sem.at[0]).wait()
    pltpu.make_async_copy(bz_r, bz_r, b_sem.at[2]).wait()


def store_results(qg_v, cg_v, qg_hbm, cg_hbm, sem):
    copies = [pltpu.make_async_copy(cg_v, cg_hbm, sem.at[0]), pltpu.make_async_copy(qg_v, qg_hbm, sem.at[1])]
    for copy in copies:
        copy.start()
    for copy in copies:
        copy.wait()


def local(queries, centroids, beta, teacher_ids):
    rows, width = queries.shape
    cells = centroids.shape[0]
    slots = teacher_ids.shape[1]
    half, part = width // 2, width // 4
    dma = pltpu.SemaphoreType.DMA
    results = pl.pallas_call(
        kernel,
        out_shape=(
            jax.ShapeDtypeStruct((rows // 32, width), F32),
            jax.ShapeDtypeStruct((part, cells), F32),
        ),
        in_specs=[pl.BlockSpec(memory_space=pltpu.MemorySpace.HBM)] * 4,
        out_specs=[pl.BlockSpec(memory_space=pltpu.VMEM)] * 2,
        scratch_shapes=[
            pltpu.VMEM((rows, width), BF16),
            pltpu.VMEM((cells, width), BF16),
            pltpu.VMEM((1, rows), F32),
            pltpu.VMEM((slots, rows), jnp.int32),
            pltpu.VMEM((rows, width), BF16),
            pltpu.VMEM((width, rows), BF16),
            pltpu.VMEM((width, cells), BF16),
            pltpu.VMEM((cells, rows), F32),
            pltpu.VMEM((cells, rows), F32),
            pltpu.VMEM((cells, rows), BF16),
            pltpu.VMEM((rows, width), F32),
            pltpu.VMEM((rows, width), F32),
            pltpu.VMEM((1, rows), F32),
            pltpu.VMEM((2, 1, rows), F32),
            pltpu.VMEM((8, 4, 1, rows), F32),
            pltpu.VMEM((4, 1, rows), F32),
            pltpu.VMEM((4, 8, 16, half), BF16),
            pltpu.VMEM((3, 8, 16, half), BF16),
            pltpu.VMEM((4, 8, 16, half), BF16),
            pltpu.VMEM((3, 8, 16, half), BF16),
            pltpu.VMEM((8, 16, half), BF16),
            pltpu.VMEM((7, 16, half), BF16),
            pltpu.VMEM((8, 16, half), BF16),
            pltpu.VMEM((7, 16, half), BF16),
            pltpu.VMEM((4, part, cells // 2), BF16),
            pltpu.VMEM((4, part, cells // 2), BF16),
            pltpu.VMEM((2, part, cells // 2), BF16),
            pltpu.VMEM((2, part, cells // 2), BF16),
            pltpu.VMEM((2, part, cells // 2), F32),
            pltpu.VMEM((2, part, cells // 2), F32),
            pltpu.VMEM((cells, rows), BF16),
            pltpu.VMEM((1, cells), F32),
            pltpu.VMEM((3, 1, cells), F32),
            dma((4,)),
            dma((9,)),
            dma((9,)),
            dma((2, 4, 3)),
            dma((2, 4, 3)),
            dma((4,)),
            dma((4,)),
            dma((4,)),
            dma((2,)),
            dma((2,)),
            dma((2, 3)),
            pltpu.SemaphoreType.REGULAR,
        ],
        compiler_params=pltpu.CompilerParams(
            collective_id=0, has_side_effects=True, vmem_limit_bytes=24 * 1024 * 1024
        ),
    )(*[pltpu.with_memory_space_constraint(a, pltpu.MemorySpace.HBM) for a in (queries, centroids, beta.reshape(1, rows), teacher_ids.T)])
    query_grad, centroid_grad = pl.pallas_call(
        store_results,
        out_shape=[jax.ShapeDtypeStruct(a.shape, a.dtype) for a in results],
        in_specs=[pl.BlockSpec(memory_space=pltpu.VMEM)] * 2,
        out_specs=[pl.BlockSpec(memory_space=pltpu.MemorySpace.HBM)] * 2,
        scratch_shapes=[dma((2,))],
        compiler_params=pltpu.CompilerParams(vmem_limit_bytes=1024 * 1024),
    )(*results)
    return query_grad, centroid_grad.T


def solution(mesh):
    in_specs = (P("dp", None), P("cent", None), P("dp"), P("dp", None))
    out_specs = (P(("dp", "cent"), None), P("cent", "dp"))
    return jax.shard_map(local, mesh=mesh, in_specs=in_specs, out_specs=out_specs, check_vma=False)
```

```python
import functools

import jax
import jax.numpy as jnp
from jax import lax
from jax.experimental import pallas as pl
from jax.experimental.pallas import tpu as pltpu
from jax.sharding import PartitionSpec as P

EPS = 1e-06
SCALE = 1024.0
MESH = pl.DeviceIdType.MESH
F32 = jnp.float32
BF16 = jnp.bfloat16
NT = (((1,), (1,)), ((), ()))
TN = (((0,), (0,)), ((), ()))


def dot(a, b, dims):
    return lax.dot_general(a, b, dims, preferred_element_type=F32)


def join(own, others):
    top = jnp.maximum(jnp.max(others, axis=0), own)
    return top + jnp.log(jnp.sum(jnp.exp(others - top[None]), axis=0) + jnp.exp(own - top))


def kernel(
    q_hbm, c_hbm, beta_hbm, ids_hbm,
    qg_ref, cg_ref,
    q_v, c_v, beta_v, ids_v,
    qh_v, qht_v, ct_v, cos_v, e_v, d_v,
    es_v, ts_v,
    lse_v, lse_s, lse_r, early_r,
    gx_s, gx_r, gz_s, gz_r,
    bx_s, bx_r, bz_s, bz_r,
    core_s, core_r, y_s, y_r,
    near_v, far_v, diff_v, row_s, row_r,
    in_sem, lse_sem, a_send, a_recv, b_sem, core_send, core_recv, y_send, y_recv, row_sem, ready_sem,
):
    rows, width = q_hbm.shape
    cells = c_hbm.shape[0]
    slots = ids_hbm.shape[0]
    half = width // 2
    part = width // 4
    dp = lax.axis_index("dp")
    cent = lax.axis_index("cent")
    x = cent // 8
    yhi = (cent // 4) % 2
    z = cent % 4
    core = dp % 2
    ylo = dp // 2

    loads = [
        pltpu.make_async_copy(src, dst, in_sem.at[i])
        for i, (src, dst) in enumerate(((q_hbm, q_v), (c_hbm, c_v), (beta_hbm, beta_v), (ids_hbm, ids_v)))
    ]
    for load in loads:
        load.start()

    barrier = pltpu.get_barrier_semaphore()

    for r in range(1, 4):
        pl.semaphore_signal(barrier, inc=1, device_id=(dp, (((x + r) % 4) * 2 + yhi) * 4 + z), device_id_type=MESH)
        pl.semaphore_signal(barrier, inc=1, device_id=(dp, (x * 2 + yhi) * 4 + (z + r) % 4), device_id_type=MESH)
        pl.semaphore_signal(barrier, inc=1, device_id=((dp + r) % 4, cent), device_id_type=MESH)
    pl.semaphore_signal(barrier, inc=1, device_id=(dp, (x * 2 + 1 - yhi) * 4 + z), device_id_type=MESH)

    early = ((yhi == 0) & (x < 2)) & (z < 2)

    @pl.when(early)
    def _():
        @pl.loop(1, 32)
        def _(r):
            pl.semaphore_signal(barrier, inc=1, device_id=(dp, (cent + r) % 32), device_id_type=MESH)

    loads[0].wait()
    for i in range(4):
        block = pl.ds(i * (rows // 4), rows // 4)
        qf = q_v[block, :].astype(F32)
        inv = 1.0 / jnp.sqrt(jnp.sum(qf * qf, axis=1, keepdims=True) + EPS)
        qh_v[block, :] = (qf * inv).astype(BF16)

    loads[1].wait()
    loads[2].wait()
    loads[3].wait()
    for i in range(2):
        lanes = pl.ds(i * (rows // 2), rows // 2)
        cosine = dot(c_v[...], qh_v[lanes, :], NT)
        cos_v[:, lanes] = cosine
        score = cosine * beta_v[:, lanes]
        top = jnp.max(score, axis=0, keepdims=True)
        expo = jnp.exp(score - top)
        total = jnp.sum(expo, axis=0, keepdims=True)
        lse_s[0, :, lanes] = top + jnp.log(total)
        e_v[:, lanes] = expo * (1.0 / total)

    @pl.when(early)
    def _():
        pl.semaphore_wait(barrier, 13)

    @pl.when(jnp.logical_not(early))
    def _():
        pl.semaphore_wait(barrier, 14)

    pl.semaphore_signal(ready_sem, inc=1, device_id=(dp, (x * 2 + 1 - yhi) * 4 + z), device_id_type=MESH)

    def line_copy(r):
        return pltpu.make_async_remote_copy(
            src_ref=lse_s.at[0], dst_ref=lse_r.at[r - 1], send_sem=lse_sem.at[0], recv_sem=lse_sem.at[1],
            device_id=(dp, (((x + r) % 4) * 2 + yhi) * 4 + z), device_id_type=MESH,
        )

    def plane_copy(r):
        return pltpu.make_async_remote_copy(
            src_ref=lse_s.at[1], dst_ref=lse_r.at[r + 2], send_sem=lse_sem.at[2], recv_sem=lse_sem.at[3],
            device_id=(dp, (x * 2 + (yhi + r // 4) % 2) * 4 + (z + r) % 4), device_id_type=MESH,
        )

    def early_copy(to):
        return pltpu.make_async_remote_copy(
            src_ref=lse_s.at[0], dst_ref=early_r.at[(cent + 31 - to) % 32], send_sem=lse_sem.at[4], recv_sem=lse_sem.at[5],
            device_id=(dp, to), device_id_type=MESH,
        )

    for to in (0, 1, 8, 9):

        @pl.when(to != cent)
        def _():
            early_copy(to).start()

    for r in (2, 1, 3):
        line_copy(r).start()

    for i in range(2):
        lanes = pl.ds(i * (rows // 2), rows // 2)
        es_v[lanes, :] = dot(e_v[:, lanes].astype(BF16), c_v[...], TN)
    ids = ids_v[...] - cent * cells
    position = lax.broadcasted_iota(jnp.int32, (256, rows), 0).astype(F32).astype(BF16)
    for h in range(cells // 256):
        here = ids - h * 256
        here = jnp.where((here >= 0) & (here < 256), here, -1).astype(F32)
        count = jnp.zeros((256, rows), BF16)
        for slot in range(slots):
            hit = jnp.broadcast_to(here[slot : slot + 1], (256, rows)).astype(BF16) == position
            count = count + jnp.where(hit, jnp.bfloat16(SCALE / slots), jnp.bfloat16(0.0))
        d_v[pl.ds(h * 256, 256), :] = count
    for i in range(2):
        lanes = pl.ds(i * (rows // 2), rows // 2)
        ts_v[lanes, :] = dot(d_v[:, lanes], c_v[...], TN)
    qht_v[...] = qh_v[...].T
    ct_v[...] = c_v[...].T

    line = pl.ds(0, 3)
    pltpu.make_async_copy(lse_r.at[line], lse_r.at[line], lse_sem.at[1]).wait()
    lse_s[1] = join(lse_s[0], lse_r[0:3])
    for r in (1, 2, 3, 4):
        plane_copy(r).start()
    pl.semaphore_wait(ready_sem, 1)
    for r in (5, 6, 7):
        plane_copy(r).start()

    plane = pl.ds(3, 7)

    @pl.when(early)
    def _():
        pltpu.make_async_copy(early_r, early_r, lse_sem.at[5]).wait()
        lse_v[...] = join(lse_s[0], early_r[...])

    @pl.when(jnp.logical_not(early))
    def _():
        pltpu.make_async_copy(lse_r.at[plane], lse_r.at[plane], lse_sem.at[3]).wait()
        lse_v[...] = join(lse_s[1], lse_r[3:10])

    weight = jnp.exp(lse_s[0] - lse_v[...]) * SCALE
    weight_col = jnp.broadcast_to(weight, (128, rows)).T

    def x_copy(p, to, r):
        pair = pl.ds(2 * p, 2)
        return pltpu.make_async_remote_copy(
            src_ref=gx_s.at[to, pair], dst_ref=gx_r.at[r - 1, pair], send_sem=a_send.at[0], recv_sem=a_recv.at[0, p],
            device_id=(dp, (to * 2 + yhi) * 4 + z), device_id_type=MESH,
        )

    def z_copy(p, to, r):
        pair = pl.ds(2 * p, 2)
        return pltpu.make_async_remote_copy(
            src_ref=gz_s.at[to, pair], dst_ref=gz_r.at[r - 1, pair], send_sem=a_send.at[1], recv_sem=a_recv.at[1, p],
            device_id=(dp, (x * 2 + yhi) * 4 + to), device_id_type=MESH,
        )

    def weighted(first_row, count, first_col):
        block = slice(first_row, first_row + count)
        w = weight_col[block]
        cols = [slice(first_col + 128 * j, first_col + 128 * (j + 1)) for j in range(3)]
        return [(es_v[block, c] * w - ts_v[block, c]).astype(BF16) for c in cols]

    for p in (0, 2, 1, 3):
        for i in range(4):
            for j, g in enumerate(weighted(i * 128 + 32 * p, 32, 0)):
                gx_s[i, 2 * p : 2 * p + 2, :, 128 * j : 128 * (j + 1)] = g.reshape(2, 16, 128)
        for i in (2 * (p % 2), 2 * (p % 2) + 1):
            for j, g in enumerate(weighted(i * 128 + 64 * (p // 2), 64, half)):
                for k in range(4):
                    gz_s[k, 4 * (p // 2) + i, :, 128 * j : 128 * (j + 1)] = g[k * 16 : (k + 1) * 16]
        for to in range(4):

            @pl.when(to != x)
            def _():
                x_copy(p, to, (to + 4 - x) % 4).start()

            @pl.when(to != z)
            def _():
                z_copy(p, to, (to + 4 - z) % 4).start()

    def grad_part(to, d):
        return dot(qht_v[pl.ds(pl.multiple_of(to * part, 64), part), :], d, NT)

    def core_copy(i):
        return pltpu.make_async_remote_copy(
            src_ref=core_s.at[i], dst_ref=core_r.at[i], send_sem=core_send.at[i], recv_sem=core_recv.at[i],
            device_id=(ylo * 2 + 1 - core, cent), device_id_type=MESH,
        )

    def y_copy(i):
        return pltpu.make_async_remote_copy(
            src_ref=y_s.at[i], dst_ref=y_r.at[i], send_sem=y_send.at[i], recv_sem=y_recv.at[i],
            device_id=((1 - ylo) * 2 + core, cent), device_id_type=MESH,
        )

    def centroid_start():
        for i in range(2):
            block = pl.ds(i * (cells // 2), cells // 2)
            diff_v[block, :] = (e_v[block, :] * weight - d_v[block, :].astype(F32)).astype(BF16)
            core_s[i] = grad_part((1 - ylo) * 2 + 1 - core, diff_v[block, :]).astype(BF16)
            core_copy(i).start()
        for i in range(2):
            block = pl.ds(i * (cells // 2), cells // 2)
            far_v[i] = grad_part((1 - ylo) * 2 + core, diff_v[block, :])

    def centroid_cross():
        for i in range(2):
            core_copy(i).wait()
            y_s[i] = (far_v[i] + core_r[i].astype(F32)).astype(BF16)
            y_copy(i).start()

    centroid_start()

    @pl.when(yhi == 0)
    def _():
        centroid_cross()

    for i in range(2):
        block = pl.ds(i * (cells // 2), cells // 2)
        core_s[2 + i] = grad_part(ylo * 2 + 1 - core, diff_v[block, :]).astype(BF16)
        core_copy(2 + i).start()
    for i in range(2):
        block = pl.ds(i * (cells // 2), cells // 2)
        near_v[i] = grad_part(dp, diff_v[block, :])

    for i in range(2):
        block = pl.ds(i * (cells // 2), cells // 2)
        prod = diff_v[block, :].astype(F32) * cos_v[block, :]
        prod = prod[:, 0:128] + prod[:, 128:256] + prod[:, 256:384] + prod[:, 384:512]
        row_s[:, block] = jnp.sum(prod.T, axis=0, keepdims=True)

    def row_copy(r):
        return pltpu.make_async_remote_copy(
            src_ref=row_s, dst_ref=row_r.at[r - 1], send_sem=row_sem.at[0], recv_sem=row_sem.at[1],
            device_id=((dp + r) % 4, cent), device_id_type=MESH,
        )

    for r in range(1, 4):
        row_copy(r).start()

    def bx_copy(to, r):
        return pltpu.make_async_remote_copy(
            src_ref=bx_s.at[to], dst_ref=bx_r.at[r - 1], send_sem=b_sem.at[0], recv_sem=b_sem.at[1],
            device_id=(dp, x * 8 + to), device_id_type=MESH,
        )

    def bz_copy(to, r):
        return pltpu.make_async_remote_copy(
            src_ref=bz_s.at[to], dst_ref=bz_r.at[r - 1], send_sem=b_sem.at[2], recv_sem=b_sem.at[3],
            device_id=(dp, (to % 4) * 8 + (to // 4) * 4 + z), device_id_type=MESH,
        )

    def pass_on(p):
        pair = pl.ds(2 * p, 2)
        for axis, own, mine, got, out, send in (
            (0, x, gx_s, gx_r, bx_s, bx_copy),
            (1, z, gz_s, gz_r, bz_s, bz_copy),
        ):
            pltpu.make_async_copy(got.at[:, pair], got.at[:, pair], a_recv.at[axis, p]).wait()
            total = mine[own, pair].astype(F32)
            for r in range(3):
                total = total + got[r, pair].astype(F32)
            out[pair] = total.astype(BF16)
            place = z if send is bx_copy else x
            for to in (2 * p, 2 * p + 1):

                @pl.when(to != yhi * 4 + place)
                def _():
                    send(to, ((to // 4 + 2 - yhi) % 2) * 4 + (to % 4 + 4 - place) % 4).start()

    pass_on(0)

    @pl.when(yhi == 1)
    def _():
        centroid_cross()

    pass_on(2)
    pass_on(1)
    pass_on(3)

    pltpu.make_async_copy(row_r, row_r, row_sem.at[0]).wait()
    pltpu.make_async_copy(row_r, row_r, row_sem.at[1]).wait()
    rowdot = row_s[...] + row_r[0] + row_r[1] + row_r[2]
    own_rows = pl.ds(pl.multiple_of(dp * part, 64), part)
    for i in range(2):
        block = pl.ds(i * (cells // 2), cells // 2)
        core_copy(2 + i).wait()
        y_copy(i).wait()
        grad = near_v[i] + core_r[2 + i].astype(F32) + y_r[i].astype(F32)
        here = slice(i * (cells // 2), (i + 1) * (cells // 2))
        cg_ref[:, block] = grad - rowdot[:, here] * ct_v[own_rows, block].astype(F32)

    mine = pl.ds(pl.multiple_of(cent * 16, 16), 16)
    qf = q_v[mine, :].astype(F32)
    norm = jnp.sqrt(jnp.sum(qf * qf, axis=1, keepdims=True) + EPS)
    hat = qh_v[mine, :].astype(F32)
    pltpu.make_async_copy(bx_r, bx_r, b_sem.at[1]).wait()
    left = bx_s[yhi * 4 + z].astype(F32) + jnp.sum(bx_r[...].astype(F32), axis=0)
    pltpu.make_async_copy(bz_r, bz_r, b_sem.at[3]).wait()
    right = bz_s[yhi * 4 + x].astype(F32) + jnp.sum(bz_r[...].astype(F32), axis=0)
    grad = jnp.concatenate([left, right], axis=1)
    along = jnp.sum(grad * hat, axis=1, keepdims=True)
    qg_ref[...] = (grad - along * hat) / norm

    pltpu.make_async_copy(lse_r.at[line], lse_r.at[line], lse_sem.at[0]).wait()
    pltpu.make_async_copy(lse_r.at[plane], lse_r.at[plane], lse_sem.at[2]).wait()

    @pl.when(early)
    def _():
        three = pl.ds(0, 3)
        pltpu.make_async_copy(early_r.at[three], early_r.at[three], lse_sem.at[4]).wait()
        pltpu.make_async_copy(lse_r.at[plane], lse_r.at[plane], lse_sem.at[3]).wait()

    @pl.when(jnp.logical_not(early))
    def _():
        four = pl.ds(0, 4)
        pltpu.make_async_copy(early_r.at[four], early_r.at[four], lse_sem.at[4]).wait()

    pltpu.make_async_copy(gx_r, gx_r, a_send.at[0]).wait()
    pltpu.make_async_copy(gz_r, gz_r, a_send.at[1]).wait()
    pltpu.make_async_copy(bx_r, bx_r, b_sem.at[0]).wait()
    pltpu.make_async_copy(bz_r, bz_r, b_sem.at[2]).wait()


def store_results(qg_v, cg_v, qg_hbm, cg_hbm, sem):
    copies = [pltpu.make_async_copy(cg_v, cg_hbm, sem.at[0]), pltpu.make_async_copy(qg_v, qg_hbm, sem.at[1])]
    for copy in copies:
        copy.start()
    for copy in copies:
        copy.wait()


def local(queries, centroids, beta, teacher_ids):
    rows, width = queries.shape
    cells = centroids.shape[0]
    slots = teacher_ids.shape[1]
    half, part = width // 2, width // 4
    dma = pltpu.SemaphoreType.DMA
    results = pl.pallas_call(
        kernel,
        out_shape=(
            jax.ShapeDtypeStruct((rows // 32, width), F32),
            jax.ShapeDtypeStruct((part, cells), F32),
        ),
        in_specs=[pl.BlockSpec(memory_space=pltpu.MemorySpace.HBM)] * 4,
        out_specs=[pl.BlockSpec(memory_space=pltpu.VMEM)] * 2,
        scratch_shapes=[
            pltpu.VMEM((rows, width), BF16),
            pltpu.VMEM((cells, width), BF16),
            pltpu.VMEM((1, rows), F32),
            pltpu.VMEM((slots, rows), jnp.int32),
            pltpu.VMEM((rows, width), BF16),
            pltpu.VMEM((width, rows), BF16),
            pltpu.VMEM((width, cells), BF16),
            pltpu.VMEM((cells, rows), F32),
            pltpu.VMEM((cells, rows), F32),
            pltpu.VMEM((cells, rows), BF16),
            pltpu.VMEM((rows, width), F32),
            pltpu.VMEM((rows, width), F32),
            pltpu.VMEM((1, rows), F32),
            pltpu.VMEM((2, 1, rows), F32),
            pltpu.VMEM((10, 1, rows), F32),
            pltpu.VMEM((31, 1, rows), F32),
            pltpu.VMEM((4, 8, 16, half), BF16),
            pltpu.VMEM((3, 8, 16, half), BF16),
            pltpu.VMEM((4, 8, 16, half), BF16),
            pltpu.VMEM((3, 8, 16, half), BF16),
            pltpu.VMEM((8, 16, half), BF16),
            pltpu.VMEM((7, 16, half), BF16),
            pltpu.VMEM((8, 16, half), BF16),
            pltpu.VMEM((7, 16, half), BF16),
            pltpu.VMEM((4, part, cells // 2), BF16),
            pltpu.VMEM((4, part, cells // 2), BF16),
            pltpu.VMEM((2, part, cells // 2), BF16),
            pltpu.VMEM((2, part, cells // 2), BF16),
            pltpu.VMEM((2, part, cells // 2), F32),
            pltpu.VMEM((2, part, cells // 2), F32),
            pltpu.VMEM((cells, rows), BF16),
            pltpu.VMEM((1, cells), F32),
            pltpu.VMEM((3, 1, cells), F32),
            dma((4,)),
            dma((6,)),
            dma((2,)),
            dma((2, 4)),
            dma((4,)),
            dma((4,)),
            dma((4,)),
            dma((2,)),
            dma((2,)),
            dma((2,)),
            pltpu.SemaphoreType.REGULAR,
        ],
        compiler_params=pltpu.CompilerParams(
            collective_id=0, has_side_effects=True, vmem_limit_bytes=24 * 1024 * 1024
        ),
    )(*[pltpu.with_memory_space_constraint(a, pltpu.MemorySpace.HBM) for a in (queries, centroids, beta.reshape(1, rows), teacher_ids.T)])
    query_grad, centroid_grad = pl.pallas_call(
        store_results,
        out_shape=[jax.ShapeDtypeStruct(a.shape, a.dtype) for a in results],
        in_specs=[pl.BlockSpec(memory_space=pltpu.VMEM)] * 2,
        out_specs=[pl.BlockSpec(memory_space=pltpu.MemorySpace.HBM)] * 2,
        scratch_shapes=[dma((2,))],
        compiler_params=pltpu.CompilerParams(vmem_limit_bytes=1024 * 1024),
    )(*results)
    return query_grad, centroid_grad.T


def solution(mesh):
    in_specs = (P("dp", None), P("cent", None), P("dp"), P("dp", None))
    out_specs = (P(("dp", "cent"), None), P("cent", "dp"))
    return jax.shard_map(local, mesh=mesh, in_specs=in_specs, out_specs=out_specs, check_vma=False)
```

```python
import functools

import jax
import jax.numpy as jnp
from jax import lax
from jax.experimental import pallas as pl
from jax.experimental.pallas import tpu as pltpu
from jax.sharding import PartitionSpec as P

EPS = 1e-06
SCALE = 1024.0
MESH = pl.DeviceIdType.MESH
F32 = jnp.float32
BF16 = jnp.bfloat16
NT = (((1,), (1,)), ((), ()))
TN = (((0,), (0,)), ((), ()))


def dot(a, b, dims):
    return lax.dot_general(a, b, dims, preferred_element_type=F32)


def join(own, others):
    top = jnp.maximum(jnp.max(others, axis=0), own)
    return top + jnp.log(jnp.sum(jnp.exp(others - top[None]), axis=0) + jnp.exp(own - top))


def kernel(
    q_hbm, c_hbm, beta_hbm, ids_hbm,
    qg_ref, cg_ref,
    q_v, c_v, beta_v, ids_v,
    qh_v, qht_v, ct_v, cos_v, e_v, d_v,
    es_v, ts_v,
    lse_v, lse_s, lse_r, early_r,
    gx_s, gx_r, gz_s, gz_r,
    bx_s, bx_r, bz_s, bz_r,
    core_s, core_r, y_s, y_r,
    near_v, far_v, diff_v, row_s, row_r,
    in_sem, lse_sem, a_send, a_recv, b_sem, core_send, core_recv, y_send, y_recv, row_sem, ready_sem,
):
    rows, width = q_hbm.shape
    cells = c_hbm.shape[0]
    slots = ids_hbm.shape[0]
    half = width // 2
    part = width // 4
    dp = lax.axis_index("dp")
    cent = lax.axis_index("cent")
    x = cent // 8
    yhi = (cent // 4) % 2
    z = cent % 4
    core = dp % 2
    ylo = dp // 2

    loads = [
        pltpu.make_async_copy(src, dst, in_sem.at[i])
        for i, (src, dst) in enumerate(((q_hbm, q_v), (c_hbm, c_v), (beta_hbm, beta_v), (ids_hbm, ids_v)))
    ]
    for load in loads:
        load.start()

    barrier = pltpu.get_barrier_semaphore()

    for r in range(1, 4):
        pl.semaphore_signal(barrier, inc=1, device_id=(dp, (((x + r) % 4) * 2 + yhi) * 4 + z), device_id_type=MESH)
        pl.semaphore_signal(barrier, inc=1, device_id=(dp, (x * 2 + yhi) * 4 + (z + r) % 4), device_id_type=MESH)
        pl.semaphore_signal(barrier, inc=1, device_id=((dp + r) % 4, cent), device_id_type=MESH)
    pl.semaphore_signal(barrier, inc=1, device_id=(dp, (x * 2 + 1 - yhi) * 4 + z), device_id_type=MESH)

    early = ((yhi == 0) & (x < 2)) & (z < 2)

    @pl.when(early)
    def _():
        @pl.loop(1, 32)
        def _(r):
            pl.semaphore_signal(barrier, inc=1, device_id=(dp, (cent + r) % 32), device_id_type=MESH)

    loads[0].wait()
    for i in range(4):
        block = pl.ds(i * (rows // 4), rows // 4)
        qf = q_v[block, :].astype(F32)
        inv = 1.0 / jnp.sqrt(jnp.sum(qf * qf, axis=1, keepdims=True) + EPS)
        qh_v[block, :] = (qf * inv).astype(BF16)

    loads[1].wait()
    loads[2].wait()
    loads[3].wait()
    for i in range(2):
        lanes = pl.ds(i * (rows // 2), rows // 2)
        cosine = dot(c_v[...], qh_v[lanes, :], NT)
        cos_v[:, lanes] = cosine
        score = cosine * beta_v[:, lanes]
        top = jnp.max(score, axis=0, keepdims=True)
        expo = jnp.exp(score - top)
        total = jnp.sum(expo, axis=0, keepdims=True)
        lse_s[0, :, lanes] = top + jnp.log(total)
        e_v[:, lanes] = expo * (1.0 / total)

    @pl.when(early)
    def _():
        pl.semaphore_wait(barrier, 13)

    @pl.when(jnp.logical_not(early))
    def _():
        pl.semaphore_wait(barrier, 14)

    pl.semaphore_signal(ready_sem, inc=1, device_id=(dp, (x * 2 + 1 - yhi) * 4 + z), device_id_type=MESH)

    def line_copy(r):
        return pltpu.make_async_remote_copy(
            src_ref=lse_s.at[0], dst_ref=lse_r.at[r - 1], send_sem=lse_sem.at[0], recv_sem=lse_sem.at[1],
            device_id=(dp, (((x + r) % 4) * 2 + yhi) * 4 + z), device_id_type=MESH,
        )

    def plane_copy(r):
        return pltpu.make_async_remote_copy(
            src_ref=lse_s.at[1], dst_ref=lse_r.at[r + 2], send_sem=lse_sem.at[2], recv_sem=lse_sem.at[3],
            device_id=(dp, (x * 2 + (yhi + r // 4) % 2) * 4 + (z + r) % 4), device_id_type=MESH,
        )

    def early_copy(to):
        return pltpu.make_async_remote_copy(
            src_ref=lse_s.at[0], dst_ref=early_r.at[(cent + 31 - to) % 32], send_sem=lse_sem.at[4], recv_sem=lse_sem.at[5],
            device_id=(dp, to), device_id_type=MESH,
        )

    for to in (0, 1, 8, 9):

        @pl.when(to != cent)
        def _():
            early_copy(to).start()

    for r in (2, 1, 3):
        line_copy(r).start()

    for i in range(2):
        lanes = pl.ds(i * (rows // 2), rows // 2)
        es_v[lanes, :] = dot(e_v[:, lanes].astype(BF16), c_v[...], TN)
    ids = ids_v[...] - cent * cells
    position = lax.broadcasted_iota(jnp.int32, (256, rows), 0).astype(F32).astype(BF16)
    for h in range(cells // 256):
        here = ids - h * 256
        here = jnp.where((here >= 0) & (here < 256), here, -1).astype(F32)
        count = jnp.zeros((256, rows), BF16)
        for slot in range(slots):
            hit = jnp.broadcast_to(here[slot : slot + 1], (256, rows)).astype(BF16) == position
            count = count + jnp.where(hit, jnp.bfloat16(SCALE / slots), jnp.bfloat16(0.0))
        d_v[pl.ds(h * 256, 256), :] = count
    for i in range(2):
        lanes = pl.ds(i * (rows // 2), rows // 2)
        ts_v[lanes, :] = dot(d_v[:, lanes], c_v[...], TN)
    qht_v[...] = qh_v[...].T
    ct_v[...] = c_v[...].T

    line = pl.ds(0, 3)
    pltpu.make_async_copy(lse_r.at[line], lse_r.at[line], lse_sem.at[1]).wait()
    lse_s[1] = join(lse_s[0], lse_r[0:3])
    for r in (1, 2, 3, 4):
        plane_copy(r).start()
    pl.semaphore_wait(ready_sem, 1)
    for r in (5, 6, 7):
        plane_copy(r).start()

    plane = pl.ds(3, 7)

    @pl.when(early)
    def _():
        pltpu.make_async_copy(early_r, early_r, lse_sem.at[5]).wait()
        lse_v[...] = join(lse_s[0], early_r[...])

    @pl.when(jnp.logical_not(early))
    def _():
        pltpu.make_async_copy(lse_r.at[plane], lse_r.at[plane], lse_sem.at[3]).wait()
        lse_v[...] = join(lse_s[1], lse_r[3:10])

    weight = jnp.exp(lse_s[0] - lse_v[...]) * SCALE
    weight_col = jnp.broadcast_to(weight, (128, rows)).T

    def x_copy(p, to, r):
        pair = pl.ds(2 * p, 2)
        return pltpu.make_async_remote_copy(
            src_ref=gx_s.at[to, pair], dst_ref=gx_r.at[r - 1, pair], send_sem=a_send.at[0], recv_sem=a_recv.at[0, p],
            device_id=(dp, (to * 2 + yhi) * 4 + z), device_id_type=MESH,
        )

    def z_copy(p, to, r):
        pair = pl.ds(2 * p, 2)
        return pltpu.make_async_remote_copy(
            src_ref=gz_s.at[to, pair], dst_ref=gz_r.at[r - 1, pair], send_sem=a_send.at[1], recv_sem=a_recv.at[1, p],
            device_id=(dp, (x * 2 + yhi) * 4 + to), device_id_type=MESH,
        )

    def weighted(first_row, count, first_col):
        block = slice(first_row, first_row + count)
        w = weight_col[block]
        cols = [slice(first_col + 128 * j, first_col + 128 * (j + 1)) for j in range(3)]
        return [(es_v[block, c] * w - ts_v[block, c]).astype(BF16) for c in cols]

    def query_part(p):
        for i in range(4):
            for j, g in enumerate(weighted(i * 128 + 32 * p, 32, 0)):
                gx_s[i, 2 * p : 2 * p + 2, :, 128 * j : 128 * (j + 1)] = g.reshape(2, 16, 128)
        for i in (2 * (p % 2), 2 * (p % 2) + 1):
            for j, g in enumerate(weighted(i * 128 + 64 * (p // 2), 64, half)):
                for k in range(4):
                    gz_s[k, 4 * (p // 2) + i, :, 128 * j : 128 * (j + 1)] = g[k * 16 : (k + 1) * 16]
        for to in range(4):

            @pl.when(to != x)
            def _():
                x_copy(p, to, (to + 4 - x) % 4).start()

            @pl.when(to != z)
            def _():
                z_copy(p, to, (to + 4 - z) % 4).start()

    def grad_part(to, d):
        return dot(qht_v[pl.ds(pl.multiple_of(to * part, 64), part), :], d, NT)

    def core_copy(i):
        return pltpu.make_async_remote_copy(
            src_ref=core_s.at[i], dst_ref=core_r.at[i], send_sem=core_send.at[i], recv_sem=core_recv.at[i],
            device_id=(ylo * 2 + 1 - core, cent), device_id_type=MESH,
        )

    def y_copy(i):
        return pltpu.make_async_remote_copy(
            src_ref=y_s.at[i], dst_ref=y_r.at[i], send_sem=y_send.at[i], recv_sem=y_recv.at[i],
            device_id=((1 - ylo) * 2 + core, cent), device_id_type=MESH,
        )

    def centroid_start():
        for i in range(2):
            block = pl.ds(i * (cells // 2), cells // 2)
            diff_v[block, :] = (e_v[block, :] * weight - d_v[block, :].astype(F32)).astype(BF16)
            core_s[i] = grad_part((1 - ylo) * 2 + 1 - core, diff_v[block, :]).astype(BF16)
            core_copy(i).start()
        for i in range(2):
            block = pl.ds(i * (cells // 2), cells // 2)
            far_v[i] = grad_part((1 - ylo) * 2 + core, diff_v[block, :])

    def centroid_cross():
        for i in range(2):
            core_copy(i).wait()
            y_s[i] = (far_v[i] + core_r[i].astype(F32)).astype(BF16)
            y_copy(i).start()

    query_part(0)
    centroid_start()
    query_part(2)
    query_part(1)
    query_part(3)

    @pl.when(yhi == 0)
    def _():
        centroid_cross()

    for i in range(2):
        block = pl.ds(i * (cells // 2), cells // 2)
        core_s[2 + i] = grad_part(ylo * 2 + 1 - core, diff_v[block, :]).astype(BF16)
        core_copy(2 + i).start()
    for i in range(2):
        block = pl.ds(i * (cells // 2), cells // 2)
        near_v[i] = grad_part(dp, diff_v[block, :])

    for i in range(2):
        block = pl.ds(i * (cells // 2), cells // 2)
        prod = diff_v[block, :].astype(F32) * cos_v[block, :]
        prod = prod[:, 0:128] + prod[:, 128:256] + prod[:, 256:384] + prod[:, 384:512]
        row_s[:, block] = jnp.sum(prod.T, axis=0, keepdims=True)

    def row_copy(r):
        return pltpu.make_async_remote_copy(
            src_ref=row_s, dst_ref=row_r.at[r - 1], send_sem=row_sem.at[0], recv_sem=row_sem.at[1],
            device_id=((dp + r) % 4, cent), device_id_type=MESH,
        )

    for r in range(1, 4):
        row_copy(r).start()

    def bx_copy(to, r):
        return pltpu.make_async_remote_copy(
            src_ref=bx_s.at[to], dst_ref=bx_r.at[r - 1], send_sem=b_sem.at[0], recv_sem=b_sem.at[1],
            device_id=(dp, x * 8 + to), device_id_type=MESH,
        )

    def bz_copy(to, r):
        return pltpu.make_async_remote_copy(
            src_ref=bz_s.at[to], dst_ref=bz_r.at[r - 1], send_sem=b_sem.at[2], recv_sem=b_sem.at[3],
            device_id=(dp, (to % 4) * 8 + (to // 4) * 4 + z), device_id_type=MESH,
        )

    def pass_on(p):
        pair = pl.ds(2 * p, 2)
        for axis, own, mine, got, out, send in (
            (0, x, gx_s, gx_r, bx_s, bx_copy),
            (1, z, gz_s, gz_r, bz_s, bz_copy),
        ):
            pltpu.make_async_copy(got.at[:, pair], got.at[:, pair], a_recv.at[axis, p]).wait()
            total = mine[own, pair].astype(F32)
            for r in range(3):
                total = total + got[r, pair].astype(F32)
            out[pair] = total.astype(BF16)
            place = z if send is bx_copy else x
            for to in (2 * p, 2 * p + 1):

                @pl.when(to != yhi * 4 + place)
                def _():
                    send(to, ((to // 4 + 2 - yhi) % 2) * 4 + (to % 4 + 4 - place) % 4).start()

    pass_on(0)

    @pl.when(yhi == 1)
    def _():
        centroid_cross()

    pass_on(2)
    pass_on(1)
    pass_on(3)

    pltpu.make_async_copy(row_r, row_r, row_sem.at[0]).wait()
    pltpu.make_async_copy(row_r, row_r, row_sem.at[1]).wait()
    rowdot = row_s[...] + row_r[0] + row_r[1] + row_r[2]
    own_rows = pl.ds(pl.multiple_of(dp * part, 64), part)
    for i in range(2):
        block = pl.ds(i * (cells // 2), cells // 2)
        core_copy(2 + i).wait()
        y_copy(i).wait()
        grad = near_v[i] + core_r[2 + i].astype(F32) + y_r[i].astype(F32)
        here = slice(i * (cells // 2), (i + 1) * (cells // 2))
        cg_ref[:, block] = grad - rowdot[:, here] * ct_v[own_rows, block].astype(F32)

    mine = pl.ds(pl.multiple_of(cent * 16, 16), 16)
    qf = q_v[mine, :].astype(F32)
    norm = jnp.sqrt(jnp.sum(qf * qf, axis=1, keepdims=True) + EPS)
    hat = qh_v[mine, :].astype(F32)
    pltpu.make_async_copy(bx_r, bx_r, b_sem.at[1]).wait()
    left = bx_s[yhi * 4 + z].astype(F32) + jnp.sum(bx_r[...].astype(F32), axis=0)
    pltpu.make_async_copy(bz_r, bz_r, b_sem.at[3]).wait()
    right = bz_s[yhi * 4 + x].astype(F32) + jnp.sum(bz_r[...].astype(F32), axis=0)
    grad = jnp.concatenate([left, right], axis=1)
    along = jnp.sum(grad * hat, axis=1, keepdims=True)
    qg_ref[...] = (grad - along * hat) / norm

    pltpu.make_async_copy(lse_r.at[line], lse_r.at[line], lse_sem.at[0]).wait()
    pltpu.make_async_copy(lse_r.at[plane], lse_r.at[plane], lse_sem.at[2]).wait()

    @pl.when(early)
    def _():
        three = pl.ds(0, 3)
        pltpu.make_async_copy(early_r.at[three], early_r.at[three], lse_sem.at[4]).wait()
        pltpu.make_async_copy(lse_r.at[plane], lse_r.at[plane], lse_sem.at[3]).wait()

    @pl.when(jnp.logical_not(early))
    def _():
        four = pl.ds(0, 4)
        pltpu.make_async_copy(early_r.at[four], early_r.at[four], lse_sem.at[4]).wait()

    pltpu.make_async_copy(gx_r, gx_r, a_send.at[0]).wait()
    pltpu.make_async_copy(gz_r, gz_r, a_send.at[1]).wait()
    pltpu.make_async_copy(bx_r, bx_r, b_sem.at[0]).wait()
    pltpu.make_async_copy(bz_r, bz_r, b_sem.at[2]).wait()


def store_results(qg_v, cg_v, qg_hbm, cg_hbm, sem):
    copies = [pltpu.make_async_copy(cg_v, cg_hbm, sem.at[0]), pltpu.make_async_copy(qg_v, qg_hbm, sem.at[1])]
    for copy in copies:
        copy.start()
    for copy in copies:
        copy.wait()


def local(queries, centroids, beta, teacher_ids):
    rows, width = queries.shape
    cells = centroids.shape[0]
    slots = teacher_ids.shape[1]
    half, part = width // 2, width // 4
    dma = pltpu.SemaphoreType.DMA
    results = pl.pallas_call(
        kernel,
        out_shape=(
            jax.ShapeDtypeStruct((rows // 32, width), F32),
            jax.ShapeDtypeStruct((part, cells), F32),
        ),
        in_specs=[pl.BlockSpec(memory_space=pltpu.MemorySpace.HBM)] * 4,
        out_specs=[pl.BlockSpec(memory_space=pltpu.VMEM)] * 2,
        scratch_shapes=[
            pltpu.VMEM((rows, width), BF16),
            pltpu.VMEM((cells, width), BF16),
            pltpu.VMEM((1, rows), F32),
            pltpu.VMEM((slots, rows), jnp.int32),
            pltpu.VMEM((rows, width), BF16),
            pltpu.VMEM((width, rows), BF16),
            pltpu.VMEM((width, cells), BF16),
            pltpu.VMEM((cells, rows), F32),
            pltpu.VMEM((cells, rows), F32),
            pltpu.VMEM((cells, rows), BF16),
            pltpu.VMEM((rows, width), F32),
            pltpu.VMEM((rows, width), F32),
            pltpu.VMEM((1, rows), F32),
            pltpu.VMEM((2, 1, rows), F32),
            pltpu.VMEM((10, 1, rows), F32),
            pltpu.VMEM((31, 1, rows), F32),
            pltpu.VMEM((4, 8, 16, half), BF16),
            pltpu.VMEM((3, 8, 16, half), BF16),
            pltpu.VMEM((4, 8, 16, half), BF16),
            pltpu.VMEM((3, 8, 16, half), BF16),
            pltpu.VMEM((8, 16, half), BF16),
            pltpu.VMEM((7, 16, half), BF16),
            pltpu.VMEM((8, 16, half), BF16),
            pltpu.VMEM((7, 16, half), BF16),
            pltpu.VMEM((4, part, cells // 2), BF16),
            pltpu.VMEM((4, part, cells // 2), BF16),
            pltpu.VMEM((2, part, cells // 2), BF16),
            pltpu.VMEM((2, part, cells // 2), BF16),
            pltpu.VMEM((2, part, cells // 2), F32),
            pltpu.VMEM((2, part, cells // 2), F32),
            pltpu.VMEM((cells, rows), BF16),
            pltpu.VMEM((1, cells), F32),
            pltpu.VMEM((3, 1, cells), F32),
            dma((4,)),
            dma((6,)),
            dma((2,)),
            dma((2, 4)),
            dma((4,)),
            dma((4,)),
            dma((4,)),
            dma((2,)),
            dma((2,)),
            dma((2,)),
            pltpu.SemaphoreType.REGULAR,
        ],
        compiler_params=pltpu.CompilerParams(
            collective_id=0, has_side_effects=True, vmem_limit_bytes=24 * 1024 * 1024
        ),
    )(*[pltpu.with_memory_space_constraint(a, pltpu.MemorySpace.HBM) for a in (queries, centroids, beta.reshape(1, rows), teacher_ids.T)])
    query_grad, centroid_grad = pl.pallas_call(
        store_results,
        out_shape=[jax.ShapeDtypeStruct(a.shape, a.dtype) for a in results],
        in_specs=[pl.BlockSpec(memory_space=pltpu.VMEM)] * 2,
        out_specs=[pl.BlockSpec(memory_space=pltpu.MemorySpace.HBM)] * 2,
        scratch_shapes=[dma((2,))],
        compiler_params=pltpu.CompilerParams(vmem_limit_bytes=1024 * 1024),
    )(*results)
    return query_grad, centroid_grad.T


def solution(mesh):
    in_specs = (P("dp", None), P("cent", None), P("dp"), P("dp", None))
    out_specs = (P(("dp", "cent"), None), P("cent", "dp"))
    return jax.shard_map(local, mesh=mesh, in_specs=in_specs, out_specs=out_specs, check_vma=False)
```

```python
import functools

import jax
import jax.numpy as jnp
from jax import lax
from jax.experimental import pallas as pl
from jax.experimental.pallas import tpu as pltpu
from jax.sharding import PartitionSpec as P

EPS = 1e-06
SCALE = 1024.0
MESH = pl.DeviceIdType.MESH
F32 = jnp.float32
BF16 = jnp.bfloat16
NT = (((1,), (1,)), ((), ()))
TN = (((0,), (0,)), ((), ()))


def dot(a, b, dims):
    return lax.dot_general(a, b, dims, preferred_element_type=F32)


def join(own, others):
    top = jnp.maximum(jnp.max(others, axis=0), own)
    return top + jnp.log(jnp.sum(jnp.exp(others - top[None]), axis=0) + jnp.exp(own - top))


def kernel(
    q_hbm, c_hbm, beta_hbm, ids_hbm,
    qg_ref, cg_ref,
    q_v, c_v, beta_v, ids_v,
    qh_v, qht_v, ct_v, cos_v, e_v, d_v,
    es_v, ts_v,
    lse_v, lse_s, lse_r, early_r,
    gx_s, gx_r, gz_s, gz_r,
    bx_s, bx_r, bz_s, bz_r,
    core_s, core_r, y_s, y_r,
    near_v, far_v, diff_v, row_s, row_r,
    in_sem, lse_sem, a_send, a_recv, b_sem, core_send, core_recv, y_send, y_recv, row_sem, ready_sem,
):
    rows, width = q_hbm.shape
    cells = c_hbm.shape[0]
    slots = ids_hbm.shape[0]
    half = width // 2
    part = width // 4
    dp = lax.axis_index("dp")
    cent = lax.axis_index("cent")
    x = cent // 8
    yhi = (cent // 4) % 2
    z = cent % 4
    core = dp % 2
    ylo = dp // 2

    loads = [
        pltpu.make_async_copy(src, dst, in_sem.at[i])
        for i, (src, dst) in enumerate(((q_hbm, q_v), (c_hbm, c_v), (beta_hbm, beta_v), (ids_hbm, ids_v)))
    ]
    for load in loads:
        load.start()

    barrier = pltpu.get_barrier_semaphore()

    for r in range(1, 4):
        pl.semaphore_signal(barrier, inc=1, device_id=(dp, (((x + r) % 4) * 2 + yhi) * 4 + z), device_id_type=MESH)
        pl.semaphore_signal(barrier, inc=1, device_id=(dp, (x * 2 + yhi) * 4 + (z + r) % 4), device_id_type=MESH)
        pl.semaphore_signal(barrier, inc=1, device_id=((dp + r) % 4, cent), device_id_type=MESH)
    pl.semaphore_signal(barrier, inc=1, device_id=(dp, (x * 2 + 1 - yhi) * 4 + z), device_id_type=MESH)

    early = ((yhi == 0) & (x < 2)) & (z < 2)

    @pl.when(early)
    def _():
        @pl.loop(1, 32)
        def _(r):
            pl.semaphore_signal(barrier, inc=1, device_id=(dp, (cent + r) % 32), device_id_type=MESH)

    loads[0].wait()
    for i in range(4):
        block = pl.ds(i * (rows // 4), rows // 4)
        qf = q_v[block, :].astype(F32)
        inv = 1.0 / jnp.sqrt(jnp.sum(qf * qf, axis=1, keepdims=True) + EPS)
        qh_v[block, :] = (qf * inv).astype(BF16)

    loads[1].wait()
    loads[2].wait()
    loads[3].wait()
    for i in range(2):
        lanes = pl.ds(i * (rows // 2), rows // 2)
        cosine = dot(c_v[...], qh_v[lanes, :], NT)
        cos_v[:, lanes] = cosine
        score = cosine * beta_v[:, lanes]
        top = jnp.max(score, axis=0, keepdims=True)
        expo = jnp.exp(score - top)
        total = jnp.sum(expo, axis=0, keepdims=True)
        lse_s[0, :, lanes] = top + jnp.log(total)
        e_v[:, lanes] = expo * (1.0 / total)

    @pl.when(early)
    def _():
        pl.semaphore_wait(barrier, 13)

    @pl.when(jnp.logical_not(early))
    def _():
        pl.semaphore_wait(barrier, 14)

    pl.semaphore_signal(ready_sem, inc=1, device_id=(dp, (x * 2 + 1 - yhi) * 4 + z), device_id_type=MESH)

    def line_copy(r):
        return pltpu.make_async_remote_copy(
            src_ref=lse_s.at[0], dst_ref=lse_r.at[r - 1], send_sem=lse_sem.at[0], recv_sem=lse_sem.at[1],
            device_id=(dp, (((x + r) % 4) * 2 + yhi) * 4 + z), device_id_type=MESH,
        )

    def plane_copy(r):
        return pltpu.make_async_remote_copy(
            src_ref=lse_s.at[1], dst_ref=lse_r.at[r + 2], send_sem=lse_sem.at[2], recv_sem=lse_sem.at[3],
            device_id=(dp, (x * 2 + (yhi + r // 4) % 2) * 4 + (z + r) % 4), device_id_type=MESH,
        )

    def early_copy(to):
        return pltpu.make_async_remote_copy(
            src_ref=lse_s.at[0], dst_ref=early_r.at[(cent + 31 - to) % 32], send_sem=lse_sem.at[4], recv_sem=lse_sem.at[5],
            device_id=(dp, to), device_id_type=MESH,
        )

    for to in (0, 1, 8, 9):

        @pl.when(to != cent)
        def _():
            early_copy(to).start()

    for r in (2, 1, 3):
        line_copy(r).start()

    for i in range(2):
        lanes = pl.ds(i * (rows // 2), rows // 2)
        es_v[lanes, :] = dot(e_v[:, lanes].astype(BF16), c_v[...], TN)
    ids = ids_v[...] - cent * cells
    position = lax.broadcasted_iota(jnp.int32, (256, rows), 0).astype(F32).astype(BF16)
    for h in range(cells // 256):
        here = ids - h * 256
        here = jnp.where((here >= 0) & (here < 256), here, -1).astype(F32)
        count = jnp.zeros((256, rows), BF16)
        for slot in range(slots):
            hit = jnp.broadcast_to(here[slot : slot + 1], (256, rows)).astype(BF16) == position
            count = count + jnp.where(hit, jnp.bfloat16(SCALE / slots), jnp.bfloat16(0.0))
        d_v[pl.ds(h * 256, 256), :] = count
    for i in range(2):
        lanes = pl.ds(i * (rows // 2), rows // 2)
        ts_v[lanes, :] = dot(d_v[:, lanes], c_v[...], TN)
    line = pl.ds(0, 3)
    pltpu.make_async_copy(lse_r.at[line], lse_r.at[line], lse_sem.at[1]).wait()
    lse_s[1] = join(lse_s[0], lse_r[0:3])
    for r in (1, 2, 3, 4):
        plane_copy(r).start()
    pl.semaphore_wait(ready_sem, 1)
    for r in (5, 6, 7):
        plane_copy(r).start()

    qht_v[...] = qh_v[...].T
    ct_v[...] = c_v[...].T

    plane = pl.ds(3, 7)

    @pl.when(early)
    def _():
        pltpu.make_async_copy(early_r, early_r, lse_sem.at[5]).wait()
        lse_v[...] = join(lse_s[0], early_r[...])

    @pl.when(jnp.logical_not(early))
    def _():
        pltpu.make_async_copy(lse_r.at[plane], lse_r.at[plane], lse_sem.at[3]).wait()
        lse_v[...] = join(lse_s[1], lse_r[3:10])

    weight = jnp.exp(lse_s[0] - lse_v[...]) * SCALE
    weight_col = jnp.broadcast_to(weight, (128, rows)).T

    def x_copy(p, to, r):
        pair = pl.ds(2 * p, 2)
        return pltpu.make_async_remote_copy(
            src_ref=gx_s.at[to, pair], dst_ref=gx_r.at[r - 1, pair], send_sem=a_send.at[0], recv_sem=a_recv.at[0, p],
            device_id=(dp, (to * 2 + yhi) * 4 + z), device_id_type=MESH,
        )

    def z_copy(p, to, r):
        pair = pl.ds(2 * p, 2)
        return pltpu.make_async_remote_copy(
            src_ref=gz_s.at[to, pair], dst_ref=gz_r.at[r - 1, pair], send_sem=a_send.at[1], recv_sem=a_recv.at[1, p],
            device_id=(dp, (x * 2 + yhi) * 4 + to), device_id_type=MESH,
        )

    def weighted(first_row, count, first_col):
        block = slice(first_row, first_row + count)
        w = weight_col[block]
        cols = [slice(first_col + 128 * j, first_col + 128 * (j + 1)) for j in range(3)]
        return [(es_v[block, c] * w - ts_v[block, c]).astype(BF16) for c in cols]

    def query_part(p):
        for i in range(4):
            for j, g in enumerate(weighted(i * 128 + 32 * p, 32, 0)):
                gx_s[i, 2 * p : 2 * p + 2, :, 128 * j : 128 * (j + 1)] = g.reshape(2, 16, 128)
        for i in (2 * (p % 2), 2 * (p % 2) + 1):
            for j, g in enumerate(weighted(i * 128 + 64 * (p // 2), 64, half)):
                for k in range(4):
                    gz_s[k, 4 * (p // 2) + i, :, 128 * j : 128 * (j + 1)] = g[k * 16 : (k + 1) * 16]

    def x_send(p):
        for to in range(4):

            @pl.when(to != x)
            def _():
                x_copy(p, to, (to + 4 - x) % 4).start()

    def z_send(p, targets):
        for to in targets:

            @pl.when(to != z)
            def _():
                z_copy(p, to, (to + 4 - z) % 4).start()

    def grad_part(to, d):
        return dot(qht_v[pl.ds(pl.multiple_of(to * part, 64), part), :], d, NT)

    def core_copy(i):
        return pltpu.make_async_remote_copy(
            src_ref=core_s.at[i], dst_ref=core_r.at[i], send_sem=core_send.at[i], recv_sem=core_recv.at[i],
            device_id=(ylo * 2 + 1 - core, cent), device_id_type=MESH,
        )

    def y_copy(i):
        return pltpu.make_async_remote_copy(
            src_ref=y_s.at[i], dst_ref=y_r.at[i], send_sem=y_send.at[i], recv_sem=y_recv.at[i],
            device_id=((1 - ylo) * 2 + core, cent), device_id_type=MESH,
        )

    def centroid_start():
        for i in range(2):
            block = pl.ds(i * (cells // 2), cells // 2)
            diff_v[block, :] = (e_v[block, :] * weight - d_v[block, :].astype(F32)).astype(BF16)
            core_s[i] = grad_part((1 - ylo) * 2 + 1 - core, diff_v[block, :]).astype(BF16)
            core_copy(i).start()
        for i in range(2):
            block = pl.ds(i * (cells // 2), cells // 2)
            far_v[i] = grad_part((1 - ylo) * 2 + core, diff_v[block, :])

    def centroid_cross():
        for i in range(2):
            core_copy(i).wait()
            y_s[i] = (far_v[i] + core_r[i].astype(F32)).astype(BF16)
            y_copy(i).start()

    query_part(0)
    z_send(0, (0, 1))
    x_send(0)
    centroid_start()
    query_part(2)
    z_send(2, (0, 1))
    x_send(2)
    z_send(0, (2, 3))
    z_send(2, (2, 3))
    for p in (1, 3):
        query_part(p)
        x_send(p)
        z_send(p, range(4))

    @pl.when(yhi == 0)
    def _():
        centroid_cross()

    for i in range(2):
        block = pl.ds(i * (cells // 2), cells // 2)
        core_s[2 + i] = grad_part(ylo * 2 + 1 - core, diff_v[block, :]).astype(BF16)
        core_copy(2 + i).start()
    for i in range(2):
        block = pl.ds(i * (cells // 2), cells // 2)
        near_v[i] = grad_part(dp, diff_v[block, :])

    for i in range(2):
        block = pl.ds(i * (cells // 2), cells // 2)
        prod = diff_v[block, :].astype(F32) * cos_v[block, :]
        prod = prod[:, 0:128] + prod[:, 128:256] + prod[:, 256:384] + prod[:, 384:512]
        row_s[:, block] = jnp.sum(prod.T, axis=0, keepdims=True)

    def row_copy(r):
        return pltpu.make_async_remote_copy(
            src_ref=row_s, dst_ref=row_r.at[r - 1], send_sem=row_sem.at[0], recv_sem=row_sem.at[1],
            device_id=((dp + r) % 4, cent), device_id_type=MESH,
        )

    for r in range(1, 4):
        row_copy(r).start()

    def bx_copy(to, r):
        return pltpu.make_async_remote_copy(
            src_ref=bx_s.at[to], dst_ref=bx_r.at[r - 1], send_sem=b_sem.at[0], recv_sem=b_sem.at[1],
            device_id=(dp, x * 8 + to), device_id_type=MESH,
        )

    def bz_copy(to, r):
        return pltpu.make_async_remote_copy(
            src_ref=bz_s.at[to], dst_ref=bz_r.at[r - 1], send_sem=b_sem.at[2], recv_sem=b_sem.at[3],
            device_id=(dp, (to % 4) * 8 + (to // 4) * 4 + z), device_id_type=MESH,
        )

    def pass_on(p):
        pair = pl.ds(2 * p, 2)
        for axis, own, mine, got, out, send in (
            (0, x, gx_s, gx_r, bx_s, bx_copy),
            (1, z, gz_s, gz_r, bz_s, bz_copy),
        ):
            pltpu.make_async_copy(got.at[:, pair], got.at[:, pair], a_recv.at[axis, p]).wait()
            total = mine[own, pair].astype(F32)
            for r in range(3):
                total = total + got[r, pair].astype(F32)
            out[pair] = total.astype(BF16)
            place = z if send is bx_copy else x
            for to in (2 * p, 2 * p + 1):

                @pl.when(to != yhi * 4 + place)
                def _():
                    send(to, ((to // 4 + 2 - yhi) % 2) * 4 + (to % 4 + 4 - place) % 4).start()

    pass_on(0)

    @pl.when(yhi == 1)
    def _():
        centroid_cross()

    pass_on(2)
    pass_on(1)
    pass_on(3)

    pltpu.make_async_copy(row_r, row_r, row_sem.at[0]).wait()
    pltpu.make_async_copy(row_r, row_r, row_sem.at[1]).wait()
    rowdot = row_s[...] + row_r[0] + row_r[1] + row_r[2]
    own_rows = pl.ds(pl.multiple_of(dp * part, 64), part)
    for i in range(2):
        block = pl.ds(i * (cells // 2), cells // 2)
        core_copy(2 + i).wait()
        y_copy(i).wait()
        grad = near_v[i] + core_r[2 + i].astype(F32) + y_r[i].astype(F32)
        here = slice(i * (cells // 2), (i + 1) * (cells // 2))
        cg_ref[:, block] = grad - rowdot[:, here] * ct_v[own_rows, block].astype(F32)

    mine = pl.ds(pl.multiple_of(cent * 16, 16), 16)
    qf = q_v[mine, :].astype(F32)
    norm = jnp.sqrt(jnp.sum(qf * qf, axis=1, keepdims=True) + EPS)
    hat = qh_v[mine, :].astype(F32)
    pltpu.make_async_copy(bx_r, bx_r, b_sem.at[1]).wait()
    left = bx_s[yhi * 4 + z].astype(F32) + jnp.sum(bx_r[...].astype(F32), axis=0)
    pltpu.make_async_copy(bz_r, bz_r, b_sem.at[3]).wait()
    right = bz_s[yhi * 4 + x].astype(F32) + jnp.sum(bz_r[...].astype(F32), axis=0)
    grad = jnp.concatenate([left, right], axis=1)
    along = jnp.sum(grad * hat, axis=1, keepdims=True)
    qg_ref[...] = (grad - along * hat) / norm

    pltpu.make_async_copy(lse_r.at[line], lse_r.at[line], lse_sem.at[0]).wait()
    pltpu.make_async_copy(lse_r.at[plane], lse_r.at[plane], lse_sem.at[2]).wait()

    @pl.when(early)
    def _():
        three = pl.ds(0, 3)
        pltpu.make_async_copy(early_r.at[three], early_r.at[three], lse_sem.at[4]).wait()
        pltpu.make_async_copy(lse_r.at[plane], lse_r.at[plane], lse_sem.at[3]).wait()

    @pl.when(jnp.logical_not(early))
    def _():
        four = pl.ds(0, 4)
        pltpu.make_async_copy(early_r.at[four], early_r.at[four], lse_sem.at[4]).wait()

    pltpu.make_async_copy(gx_r, gx_r, a_send.at[0]).wait()
    pltpu.make_async_copy(gz_r, gz_r, a_send.at[1]).wait()
    pltpu.make_async_copy(bx_r, bx_r, b_sem.at[0]).wait()
    pltpu.make_async_copy(bz_r, bz_r, b_sem.at[2]).wait()


def store_results(qg_v, cg_v, qg_hbm, cg_hbm, sem):
    copies = [pltpu.make_async_copy(cg_v, cg_hbm, sem.at[0]), pltpu.make_async_copy(qg_v, qg_hbm, sem.at[1])]
    for copy in copies:
        copy.start()
    for copy in copies:
        copy.wait()


def local(queries, centroids, beta, teacher_ids):
    rows, width = queries.shape
    cells = centroids.shape[0]
    slots = teacher_ids.shape[1]
    half, part = width // 2, width // 4
    dma = pltpu.SemaphoreType.DMA
    results = pl.pallas_call(
        kernel,
        out_shape=(
            jax.ShapeDtypeStruct((rows // 32, width), F32),
            jax.ShapeDtypeStruct((part, cells), F32),
        ),
        in_specs=[pl.BlockSpec(memory_space=pltpu.MemorySpace.HBM)] * 4,
        out_specs=[pl.BlockSpec(memory_space=pltpu.VMEM)] * 2,
        scratch_shapes=[
            pltpu.VMEM((rows, width), BF16),
            pltpu.VMEM((cells, width), BF16),
            pltpu.VMEM((1, rows), F32),
            pltpu.VMEM((slots, rows), jnp.int32),
            pltpu.VMEM((rows, width), BF16),
            pltpu.VMEM((width, rows), BF16),
            pltpu.VMEM((width, cells), BF16),
            pltpu.VMEM((cells, rows), F32),
            pltpu.VMEM((cells, rows), F32),
            pltpu.VMEM((cells, rows), BF16),
            pltpu.VMEM((rows, width), F32),
            pltpu.VMEM((rows, width), F32),
            pltpu.VMEM((1, rows), F32),
            pltpu.VMEM((2, 1, rows), F32),
            pltpu.VMEM((10, 1, rows), F32),
            pltpu.VMEM((31, 1, rows), F32),
            pltpu.VMEM((4, 8, 16, half), BF16),
            pltpu.VMEM((3, 8, 16, half), BF16),
            pltpu.VMEM((4, 8, 16, half), BF16),
            pltpu.VMEM((3, 8, 16, half), BF16),
            pltpu.VMEM((8, 16, half), BF16),
            pltpu.VMEM((7, 16, half), BF16),
            pltpu.VMEM((8, 16, half), BF16),
            pltpu.VMEM((7, 16, half), BF16),
            pltpu.VMEM((4, part, cells // 2), BF16),
            pltpu.VMEM((4, part, cells // 2), BF16),
            pltpu.VMEM((2, part, cells // 2), BF16),
            pltpu.VMEM((2, part, cells // 2), BF16),
            pltpu.VMEM((2, part, cells // 2), F32),
            pltpu.VMEM((2, part, cells // 2), F32),
            pltpu.VMEM((cells, rows), BF16),
            pltpu.VMEM((1, cells), F32),
            pltpu.VMEM((3, 1, cells), F32),
            dma((4,)),
            dma((6,)),
            dma((2,)),
            dma((2, 4)),
            dma((4,)),
            dma((4,)),
            dma((4,)),
            dma((2,)),
            dma((2,)),
            dma((2,)),
            pltpu.SemaphoreType.REGULAR,
        ],
        compiler_params=pltpu.CompilerParams(
            collective_id=0, has_side_effects=True, vmem_limit_bytes=24 * 1024 * 1024
        ),
    )(*[pltpu.with_memory_space_constraint(a, pltpu.MemorySpace.HBM) for a in (queries, centroids, beta.reshape(1, rows), teacher_ids.T)])
    query_grad, centroid_grad = pl.pallas_call(
        store_results,
        out_shape=[jax.ShapeDtypeStruct(a.shape, a.dtype) for a in results],
        in_specs=[pl.BlockSpec(memory_space=pltpu.VMEM)] * 2,
        out_specs=[pl.BlockSpec(memory_space=pltpu.MemorySpace.HBM)] * 2,
        scratch_shapes=[dma((2,))],
        compiler_params=pltpu.CompilerParams(vmem_limit_bytes=1024 * 1024),
    )(*results)
    return query_grad, centroid_grad.T


def solution(mesh):
    in_specs = (P("dp", None), P("cent", None), P("dp"), P("dp", None))
    out_specs = (P(("dp", "cent"), None), P("cent", "dp"))
    return jax.shard_map(local, mesh=mesh, in_specs=in_specs, out_specs=out_specs, check_vma=False)
```

```python
import functools

import jax
import jax.numpy as jnp
from jax import lax
from jax.experimental import pallas as pl
from jax.experimental.pallas import tpu as pltpu
from jax.sharding import PartitionSpec as P

EPS = 1e-06
SCALE = 1024.0
MESH = pl.DeviceIdType.MESH
F32 = jnp.float32
BF16 = jnp.bfloat16
NT = (((1,), (1,)), ((), ()))
TN = (((0,), (0,)), ((), ()))


def dot(a, b, dims):
    return lax.dot_general(a, b, dims, preferred_element_type=F32)


def join(own, others):
    top = jnp.maximum(jnp.max(others, axis=0), own)
    return top + jnp.log(jnp.sum(jnp.exp(others - top[None]), axis=0) + jnp.exp(own - top))


def kernel(
    q_hbm, c_hbm, beta_hbm, ids_hbm,
    qg_ref, cg_ref,
    q_v, c_v, beta_v, ids_v,
    qh_v, qht_v, ct_v, cos_v, e_v, d_v,
    es_v, ts_v,
    lse_v, lse_s, lse_r, early_r,
    gx_s, gx_r, gz_s, gz_r,
    bx_s, bx_r, bz_s, bz_r,
    core_s, core_r, y_s, y_r,
    near_v, far_v, diff_v, row_s, row_r,
    in_sem, lse_sem, a_send, a_recv, b_sem, core_send, core_recv, y_send, y_recv, row_sem, ready_sem,
):
    rows, width = q_hbm.shape
    cells = c_hbm.shape[0]
    slots = ids_hbm.shape[0]
    half = width // 2
    part = width // 4
    dp = lax.axis_index("dp")
    cent = lax.axis_index("cent")
    x = cent // 8
    yhi = (cent // 4) % 2
    z = cent % 4
    core = dp % 2
    ylo = dp // 2

    loads = [
        pltpu.make_async_copy(src, dst, in_sem.at[i])
        for i, (src, dst) in enumerate(((q_hbm, q_v), (c_hbm, c_v), (beta_hbm, beta_v), (ids_hbm, ids_v)))
    ]
    for load in loads:
        load.start()

    barrier = pltpu.get_barrier_semaphore()

    for r in range(1, 4):
        pl.semaphore_signal(barrier, inc=1, device_id=(dp, (((x + r) % 4) * 2 + yhi) * 4 + z), device_id_type=MESH)
        pl.semaphore_signal(barrier, inc=1, device_id=(dp, (x * 2 + yhi) * 4 + (z + r) % 4), device_id_type=MESH)
        pl.semaphore_signal(barrier, inc=1, device_id=((dp + r) % 4, cent), device_id_type=MESH)
    pl.semaphore_signal(barrier, inc=1, device_id=(dp, (x * 2 + 1 - yhi) * 4 + z), device_id_type=MESH)

    early = ((yhi == 0) & (x < 2)) & (z < 2)

    @pl.when(early)
    def _():
        @pl.loop(1, 32)
        def _(r):
            pl.semaphore_signal(barrier, inc=1, device_id=(dp, (cent + r) % 32), device_id_type=MESH)

    loads[0].wait()
    for i in range(4):
        block = pl.ds(i * (rows // 4), rows // 4)
        qf = q_v[block, :].astype(F32)
        inv = 1.0 / jnp.sqrt(jnp.sum(qf * qf, axis=1, keepdims=True) + EPS)
        qh_v[block, :] = (qf * inv).astype(BF16)

    loads[1].wait()
    loads[2].wait()
    loads[3].wait()
    for i in range(2):
        lanes = pl.ds(i * (rows // 2), rows // 2)
        cosine = dot(c_v[...], qh_v[lanes, :], NT)
        cos_v[:, lanes] = cosine
        score = cosine * beta_v[:, lanes]
        top = jnp.max(score, axis=0, keepdims=True)
        expo = jnp.exp(score - top)
        total = jnp.sum(expo, axis=0, keepdims=True)
        lse_s[0, :, lanes] = top + jnp.log(total)
        e_v[:, lanes] = expo * (1.0 / total)

    @pl.when(early)
    def _():
        pl.semaphore_wait(barrier, 13)

    @pl.when(jnp.logical_not(early))
    def _():
        pl.semaphore_wait(barrier, 14)

    pl.semaphore_signal(ready_sem, inc=1, device_id=(dp, (x * 2 + 1 - yhi) * 4 + z), device_id_type=MESH)

    def line_copy(r):
        return pltpu.make_async_remote_copy(
            src_ref=lse_s.at[0], dst_ref=lse_r.at[r - 1], send_sem=lse_sem.at[0], recv_sem=lse_sem.at[1],
            device_id=(dp, (((x + r) % 4) * 2 + yhi) * 4 + z), device_id_type=MESH,
        )

    def plane_copy(r):
        return pltpu.make_async_remote_copy(
            src_ref=lse_s.at[1], dst_ref=lse_r.at[r + 2], send_sem=lse_sem.at[2], recv_sem=lse_sem.at[3],
            device_id=(dp, (x * 2 + (yhi + r // 4) % 2) * 4 + (z + r) % 4), device_id_type=MESH,
        )

    def early_copy(to):
        return pltpu.make_async_remote_copy(
            src_ref=lse_s.at[0], dst_ref=early_r.at[(cent + 31 - to) % 32], send_sem=lse_sem.at[4], recv_sem=lse_sem.at[5],
            device_id=(dp, to), device_id_type=MESH,
        )

    for to in (0, 1, 8, 9):

        @pl.when(to != cent)
        def _():
            early_copy(to).start()

    for r in (2, 1, 3):
        line_copy(r).start()

    for i in range(2):
        lanes = pl.ds(i * (rows // 2), rows // 2)
        es_v[lanes, :] = dot(e_v[:, lanes].astype(BF16), c_v[...], TN)
    ids = ids_v[...] - cent * cells
    position = lax.broadcasted_iota(jnp.int32, (256, rows), 0).astype(F32).astype(BF16)
    for h in range(cells // 256):
        here = ids - h * 256
        here = jnp.where((here >= 0) & (here < 256), here, -1).astype(F32)
        count = jnp.zeros((256, rows), BF16)
        for slot in range(slots):
            hit = jnp.broadcast_to(here[slot : slot + 1], (256, rows)).astype(BF16) == position
            count = count + jnp.where(hit, jnp.bfloat16(SCALE / slots), jnp.bfloat16(0.0))
        d_v[pl.ds(h * 256, 256), :] = count
    for i in range(2):
        lanes = pl.ds(i * (rows // 2), rows // 2)
        ts_v[lanes, :] = dot(d_v[:, lanes], c_v[...], TN)
    line = pl.ds(0, 3)
    pltpu.make_async_copy(lse_r.at[line], lse_r.at[line], lse_sem.at[1]).wait()
    lse_s[1] = join(lse_s[0], lse_r[0:3])
    for r in (4, 2, 3, 1):
        plane_copy(r).start()
    pl.semaphore_wait(ready_sem, 1)
    for r in (6, 5, 7):
        plane_copy(r).start()

    qht_v[...] = qh_v[...].T
    ct_v[...] = c_v[...].T

    plane = pl.ds(3, 7)

    @pl.when(early)
    def _():
        pltpu.make_async_copy(early_r, early_r, lse_sem.at[5]).wait()
        lse_v[...] = join(lse_s[0], early_r[...])

    @pl.when(jnp.logical_not(early))
    def _():
        pltpu.make_async_copy(lse_r.at[plane], lse_r.at[plane], lse_sem.at[3]).wait()
        lse_v[...] = join(lse_s[1], lse_r[3:10])

    weight = jnp.exp(lse_s[0] - lse_v[...]) * SCALE
    weight_col = jnp.broadcast_to(weight, (128, rows)).T

    def x_copy(p, to, r):
        pair = pl.ds(2 * p, 2)
        return pltpu.make_async_remote_copy(
            src_ref=gx_s.at[to, pair], dst_ref=gx_r.at[r - 1, pair], send_sem=a_send.at[0], recv_sem=a_recv.at[0, p],
            device_id=(dp, (to * 2 + yhi) * 4 + z), device_id_type=MESH,
        )

    def z_copy(p, to, r):
        pair = pl.ds(2 * p, 2)
        return pltpu.make_async_remote_copy(
            src_ref=gz_s.at[to, pair], dst_ref=gz_r.at[r - 1, pair], send_sem=a_send.at[1], recv_sem=a_recv.at[1, p],
            device_id=(dp, (x * 2 + yhi) * 4 + to), device_id_type=MESH,
        )

    def weighted(first_row, count, first_col):
        block = slice(first_row, first_row + count)
        w = weight_col[block]
        cols = [slice(first_col + 128 * j, first_col + 128 * (j + 1)) for j in range(3)]
        return [(es_v[block, c] * w - ts_v[block, c]).astype(BF16) for c in cols]

    def query_part(p):
        for i in range(4):
            for j, g in enumerate(weighted(i * 128 + 32 * p, 32, 0)):
                gx_s[i, 2 * p : 2 * p + 2, :, 128 * j : 128 * (j + 1)] = g.reshape(2, 16, 128)
        for i in (2 * (p % 2), 2 * (p % 2) + 1):
            for j, g in enumerate(weighted(i * 128 + 64 * (p // 2), 64, half)):
                for k in range(4):
                    gz_s[k, 4 * (p // 2) + i, :, 128 * j : 128 * (j + 1)] = g[k * 16 : (k + 1) * 16]

    def x_send(p):
        for to in range(4):

            @pl.when(to != x)
            def _():
                x_copy(p, to, (to + 4 - x) % 4).start()

    def z_send(p, targets):
        for to in targets:

            @pl.when(to != z)
            def _():
                z_copy(p, to, (to + 4 - z) % 4).start()

    def grad_part(to, d):
        return dot(qht_v[pl.ds(pl.multiple_of(to * part, 64), part), :], d, NT)

    def core_copy(i):
        return pltpu.make_async_remote_copy(
            src_ref=core_s.at[i], dst_ref=core_r.at[i], send_sem=core_send.at[i], recv_sem=core_recv.at[i],
            device_id=(ylo * 2 + 1 - core, cent), device_id_type=MESH,
        )

    def y_copy(i):
        return pltpu.make_async_remote_copy(
            src_ref=y_s.at[i], dst_ref=y_r.at[i], send_sem=y_send.at[i], recv_sem=y_recv.at[i],
            device_id=((1 - ylo) * 2 + core, cent), device_id_type=MESH,
        )

    def centroid_start():
        for i in range(2):
            block = pl.ds(i * (cells // 2), cells // 2)
            diff_v[block, :] = (e_v[block, :] * weight - d_v[block, :].astype(F32)).astype(BF16)
            core_s[i] = grad_part((1 - ylo) * 2 + 1 - core, diff_v[block, :]).astype(BF16)
            core_copy(i).start()
        for i in range(2):
            block = pl.ds(i * (cells // 2), cells // 2)
            far_v[i] = grad_part((1 - ylo) * 2 + core, diff_v[block, :])

    def centroid_cross():
        for i in range(2):
            core_copy(i).wait()
            y_s[i] = (far_v[i] + core_r[i].astype(F32)).astype(BF16)
            y_copy(i).start()

    query_part(0)
    z_send(0, (0, 1))
    x_send(0)
    centroid_start()
    query_part(2)
    z_send(2, (0, 1))
    x_send(2)
    z_send(0, (2, 3))
    z_send(2, (2, 3))
    for p in (1, 3):
        query_part(p)
        x_send(p)
        z_send(p, range(4))

    @pl.when(yhi == 0)
    def _():
        centroid_cross()

    for i in range(2):
        block = pl.ds(i * (cells // 2), cells // 2)
        core_s[2 + i] = grad_part(ylo * 2 + 1 - core, diff_v[block, :]).astype(BF16)
        core_copy(2 + i).start()
    for i in range(2):
        block = pl.ds(i * (cells // 2), cells // 2)
        near_v[i] = grad_part(dp, diff_v[block, :])

    for i in range(2):
        block = pl.ds(i * (cells // 2), cells // 2)
        prod = diff_v[block, :].astype(F32) * cos_v[block, :]
        prod = prod[:, 0:128] + prod[:, 128:256] + prod[:, 256:384] + prod[:, 384:512]
        row_s[:, block] = jnp.sum(prod.T, axis=0, keepdims=True)

    def row_copy(r):
        return pltpu.make_async_remote_copy(
            src_ref=row_s, dst_ref=row_r.at[r - 1], send_sem=row_sem.at[0], recv_sem=row_sem.at[1],
            device_id=((dp + r) % 4, cent), device_id_type=MESH,
        )

    for r in range(1, 4):
        row_copy(r).start()

    def bx_copy(to, r):
        return pltpu.make_async_remote_copy(
            src_ref=bx_s.at[to], dst_ref=bx_r.at[r - 1], send_sem=b_sem.at[0], recv_sem=b_sem.at[1],
            device_id=(dp, x * 8 + to), device_id_type=MESH,
        )

    def bz_copy(to, r):
        return pltpu.make_async_remote_copy(
            src_ref=bz_s.at[to], dst_ref=bz_r.at[r - 1], send_sem=b_sem.at[2], recv_sem=b_sem.at[3],
            device_id=(dp, (to % 4) * 8 + (to // 4) * 4 + z), device_id_type=MESH,
        )

    def pass_on(p):
        pair = pl.ds(2 * p, 2)
        for axis, own, mine, got, out, send in (
            (0, x, gx_s, gx_r, bx_s, bx_copy),
            (1, z, gz_s, gz_r, bz_s, bz_copy),
        ):
            pltpu.make_async_copy(got.at[:, pair], got.at[:, pair], a_recv.at[axis, p]).wait()
            total = mine[own, pair].astype(F32)
            for r in range(3):
                total = total + got[r, pair].astype(F32)
            out[pair] = total.astype(BF16)
            place = z if send is bx_copy else x
            for to in (2 * p, 2 * p + 1):

                @pl.when(to != yhi * 4 + place)
                def _():
                    send(to, ((to // 4 + 2 - yhi) % 2) * 4 + (to % 4 + 4 - place) % 4).start()

    pass_on(0)

    @pl.when(yhi == 1)
    def _():
        centroid_cross()

    pass_on(2)
    pass_on(1)
    pass_on(3)

    pltpu.make_async_copy(row_r, row_r, row_sem.at[0]).wait()
    pltpu.make_async_copy(row_r, row_r, row_sem.at[1]).wait()
    rowdot = row_s[...] + row_r[0] + row_r[1] + row_r[2]
    own_rows = pl.ds(pl.multiple_of(dp * part, 64), part)
    for i in range(2):
        block = pl.ds(i * (cells // 2), cells // 2)
        core_copy(2 + i).wait()
        y_copy(i).wait()
        grad = near_v[i] + core_r[2 + i].astype(F32) + y_r[i].astype(F32)
        here = slice(i * (cells // 2), (i + 1) * (cells // 2))
        cg_ref[:, block] = grad - rowdot[:, here] * ct_v[own_rows, block].astype(F32)

    mine = pl.ds(pl.multiple_of(cent * 16, 16), 16)
    qf = q_v[mine, :].astype(F32)
    norm = jnp.sqrt(jnp.sum(qf * qf, axis=1, keepdims=True) + EPS)
    hat = qh_v[mine, :].astype(F32)
    pltpu.make_async_copy(bx_r, bx_r, b_sem.at[1]).wait()
    left = bx_s[yhi * 4 + z].astype(F32) + jnp.sum(bx_r[...].astype(F32), axis=0)
    pltpu.make_async_copy(bz_r, bz_r, b_sem.at[3]).wait()
    right = bz_s[yhi * 4 + x].astype(F32) + jnp.sum(bz_r[...].astype(F32), axis=0)
    grad = jnp.concatenate([left, right], axis=1)
    along = jnp.sum(grad * hat, axis=1, keepdims=True)
    qg_ref[...] = (grad - along * hat) / norm

    pltpu.make_async_copy(lse_r.at[line], lse_r.at[line], lse_sem.at[0]).wait()
    pltpu.make_async_copy(lse_r.at[plane], lse_r.at[plane], lse_sem.at[2]).wait()

    @pl.when(early)
    def _():
        three = pl.ds(0, 3)
        pltpu.make_async_copy(early_r.at[three], early_r.at[three], lse_sem.at[4]).wait()
        pltpu.make_async_copy(lse_r.at[plane], lse_r.at[plane], lse_sem.at[3]).wait()

    @pl.when(jnp.logical_not(early))
    def _():
        four = pl.ds(0, 4)
        pltpu.make_async_copy(early_r.at[four], early_r.at[four], lse_sem.at[4]).wait()

    pltpu.make_async_copy(gx_r, gx_r, a_send.at[0]).wait()
    pltpu.make_async_copy(gz_r, gz_r, a_send.at[1]).wait()
    pltpu.make_async_copy(bx_r, bx_r, b_sem.at[0]).wait()
    pltpu.make_async_copy(bz_r, bz_r, b_sem.at[2]).wait()


def store_results(qg_v, cg_v, qg_hbm, cg_hbm, sem):
    copies = [pltpu.make_async_copy(cg_v, cg_hbm, sem.at[0]), pltpu.make_async_copy(qg_v, qg_hbm, sem.at[1])]
    for copy in copies:
        copy.start()
    for copy in copies:
        copy.wait()


def local(queries, centroids, beta, teacher_ids):
    rows, width = queries.shape
    cells = centroids.shape[0]
    slots = teacher_ids.shape[1]
    half, part = width // 2, width // 4
    dma = pltpu.SemaphoreType.DMA
    results = pl.pallas_call(
        kernel,
        out_shape=(
            jax.ShapeDtypeStruct((rows // 32, width), F32),
            jax.ShapeDtypeStruct((part, cells), F32),
        ),
        in_specs=[pl.BlockSpec(memory_space=pltpu.MemorySpace.HBM)] * 4,
        out_specs=[pl.BlockSpec(memory_space=pltpu.VMEM)] * 2,
        scratch_shapes=[
            pltpu.VMEM((rows, width), BF16),
            pltpu.VMEM((cells, width), BF16),
            pltpu.VMEM((1, rows), F32),
            pltpu.VMEM((slots, rows), jnp.int32),
            pltpu.VMEM((rows, width), BF16),
            pltpu.VMEM((width, rows), BF16),
            pltpu.VMEM((width, cells), BF16),
            pltpu.VMEM((cells, rows), F32),
            pltpu.VMEM((cells, rows), F32),
            pltpu.VMEM((cells, rows), BF16),
            pltpu.VMEM((rows, width), F32),
            pltpu.VMEM((rows, width), F32),
            pltpu.VMEM((1, rows), F32),
            pltpu.VMEM((2, 1, rows), F32),
            pltpu.VMEM((10, 1, rows), F32),
            pltpu.VMEM((31, 1, rows), F32),
            pltpu.VMEM((4, 8, 16, half), BF16),
            pltpu.VMEM((3, 8, 16, half), BF16),
            pltpu.VMEM((4, 8, 16, half), BF16),
            pltpu.VMEM((3, 8, 16, half), BF16),
            pltpu.VMEM((8, 16, half), BF16),
            pltpu.VMEM((7, 16, half), BF16),
            pltpu.VMEM((8, 16, half), BF16),
            pltpu.VMEM((7, 16, half), BF16),
            pltpu.VMEM((4, part, cells // 2), BF16),
            pltpu.VMEM((4, part, cells // 2), BF16),
            pltpu.VMEM((2, part, cells // 2), BF16),
            pltpu.VMEM((2, part, cells // 2), BF16),
            pltpu.VMEM((2, part, cells // 2), F32),
            pltpu.VMEM((2, part, cells // 2), F32),
            pltpu.VMEM((cells, rows), BF16),
            pltpu.VMEM((1, cells), F32),
            pltpu.VMEM((3, 1, cells), F32),
            dma((4,)),
            dma((6,)),
            dma((2,)),
            dma((2, 4)),
            dma((4,)),
            dma((4,)),
            dma((4,)),
            dma((2,)),
            dma((2,)),
            dma((2,)),
            pltpu.SemaphoreType.REGULAR,
        ],
        compiler_params=pltpu.CompilerParams(
            collective_id=0, has_side_effects=True, vmem_limit_bytes=24 * 1024 * 1024
        ),
    )(*[pltpu.with_memory_space_constraint(a, pltpu.MemorySpace.HBM) for a in (queries, centroids, beta.reshape(1, rows), teacher_ids.T)])
    query_grad, centroid_grad = pl.pallas_call(
        store_results,
        out_shape=[jax.ShapeDtypeStruct(a.shape, a.dtype) for a in results],
        in_specs=[pl.BlockSpec(memory_space=pltpu.VMEM)] * 2,
        out_specs=[pl.BlockSpec(memory_space=pltpu.MemorySpace.HBM)] * 2,
        scratch_shapes=[dma((2,))],
        compiler_params=pltpu.CompilerParams(vmem_limit_bytes=1024 * 1024),
    )(*results)
    return query_grad, centroid_grad.T


def solution(mesh):
    in_specs = (P("dp", None), P("cent", None), P("dp"), P("dp", None))
    out_specs = (P(("dp", "cent"), None), P("cent", "dp"))
    return jax.shard_map(local, mesh=mesh, in_specs=in_specs, out_specs=out_specs, check_vma=False)
```
